32 devices in a mesh: dp: 8 (over z, x), mp: 4 (over y, core).
Axes of the slice: x: 2, y: 2, z: 4, core: 2. Of those that a mesh axis runs over, the one named last changes fastest.
Arguments:
- tokens: bfloat16 [24, 512, 768], P('dp'), may hold values from -6 to 6
- lengths: int32 [24], P('dp'), may hold values from 216 to 512, as said below
- gain_attn: bfloat16 [768], replicated, may hold values from 0.5 to 1.5
- bias_attn: bfloat16 [768], replicated, may hold values from -4 to 4
- query_w: bfloat16 [768, 768], P(None, 'mp'), may hold values from -0.21875 to 0.21875
- query_b: bfloat16 [768], P('mp'), may hold values from -4 to 4
- key_w: bfloat16 [768, 768], P(None, 'mp'), may hold values from -0.21875 to 0.21875
- value_w: bfloat16 [768, 768], P(None, 'mp'), may hold values from -0.21875 to 0.21875
- value_b: bfloat16 [768], P('mp'), may hold values from -0.75 to 0.75
- out_w: bfloat16 [768, 768], P('mp'), may hold values from -1.75 to 1.75
- out_b: bfloat16 [768], replicated, may hold values from -4 to 4
- gain_mlp: bfloat16 [768], replicated, may hold values from 0.5 to 1.5
- bias_mlp: bfloat16 [768], replicated, may hold values from -4 to 4
- up_w: bfloat16 [768, 3072], P(None, 'mp'), may hold values from -0.21875 to 0.21875
- up_b: bfloat16 [3072], P('mp'), may hold values from -4 to 4
- down_w: bfloat16 [3072, 768], P('mp'), may hold values from -0.15625 to 0.15625
- down_b: bfloat16 [768], replicated, may hold values from -4 to 4
- deconv_w: bfloat16 [768, 1024], P(None, 'mp'), may hold values from -0.21875 to 0.21875
- scale_norm: bfloat16 [128], replicated, may hold values from 0.5 to 1.5
- shift_norm: bfloat16 [128], replicated, may hold values from -6 to 6
- cotangent: bfloat16 [24, 512, 1024], P('dp', None, 'mp'), may hold values from -6 to 6
Outputs:
- volume: float32 [24, 512, 1024], P('dp', None, 'mp')
- grad_tokens: float32 [12288, 768], P(('dp', 'mp'))
- grad_gain_attn: float32 [768], replicated
- grad_bias_attn: float32 [768], replicated
- grad_query_w: float32 [768, 768], P(None, 'mp')
- grad_query_b: float32 [768], P('mp')
- grad_key_w: float32 [768, 768], P(None, 'mp')
- grad_value_w: float32 [768, 768], P(None, 'mp')
- grad_value_b: float32 [768], P('mp')
- grad_out_w: float32 [768, 768], P('mp')
- grad_out_b: float32 [768], replicated
- grad_gain_mlp: float32 [768], replicated
- grad_bias_mlp: float32 [768], replicated
- grad_up_w: float32 [768, 3072], P(None, 'mp')
- grad_up_b: float32 [3072], P('mp')
- grad_down_w: float32 [3072, 768], P('mp')
- grad_down_b: float32 [768], replicated
- grad_deconv_w: float32 [768, 1024], P(None, 'mp')
- grad_scale_norm: float32 [128], replicated
- grad_shift_norm: float32 [128], replicated
The draws below stay inside these ranges and needn't reach their ends.
Inputs may be any that keep to these rules, and one draw needn't show every extreme that they name: `lengths`: each item holds 216, 256 or 512 patches, drawn independently for each item except that the first item of the whole batch holds 512.
All inputs are finite; a program needn't handle non-finite values.
Results may differ from the reference program's by a relative error of at most 0.025.
Values may be sent and summed in bfloat16 or wider, within the bound.
No kernel may reach another device: no remote copies, remote signals or barrier semaphores. Data moves between devices by JAX's collectives and lax.ppermute only.
A program may use at most 128 MiB of HBM per device.

```python
import math
import jax
import jax.numpy as jnp
from jax import lax

D = 768
HEADS = 12
HEAD_DIM = 64
FF = 3072
CH = 128
L = 512
ITEMS = 24


def draw_lengths(key, part):
    picked = jax.random.randint(key, (ITEMS,), 0, 3)
    table = jnp.array([27 * L // 64, L // 2, L], jnp.int32)
    chosen = jnp.sum(jnp.where(picked[:, None] == jnp.arange(3)[None, :], table[None, :], 0), axis=1)
    return chosen.astype(jnp.int32).at[0].set(L)


def block_levels(own_key, dims, pieces, least, high):
    def one(position, blocks):
        steps = jax.random.uniform(jax.random.fold_in(jax.random.fold_in(own_key, 6), position), (blocks,), jnp.float32, least / len(pieces), high / len(pieces))
        return jnp.repeat(jnp.exp(steps), dims[position] // blocks).reshape((-1,) + (1,) * (len(dims) - position - 1))

    loudness = one(*pieces[0])
    for cut in pieces[1:]:
        loudness = loudness * one(*cut)
    return loudness


def centred(key, shape, scale, reach, split=(), held_as=jnp.bfloat16):
    entries = jax.random.normal(key, shape, jnp.float32) * scale
    if len(split) > 0:
        entries = block_levels(key, shape, split, -0.22, 0.18) * entries
    return jnp.clip(entries, min=-reach, max=reach).astype(held_as)


def setup_inputs(seed: int = 0) -> dict:
    keys = jax.random.split(jax.random.key(seed), 22)
    tokens = centred(keys[0], (ITEMS, L, D), 1.0, 6.0, ((0, 8),))
    lengths = draw_lengths(jax.random.fold_in(keys[21], 71), 0)
    gain_attn = jnp.clip(1.0 + 0.1 * jax.random.normal(keys[2], (D,), jnp.float32), 0.5, 1.5).astype(jnp.bfloat16)
    bias_attn = centred(keys[3], (D,), 0.3, 4.0)
    query_w = centred(keys[4], (D, D), D ** -0.5, 0.21875, ((1, 4),))
    query_b = centred(keys[5], (D,), 0.3, 4.0, ((0, 4),))
    key_w = centred(keys[6], (D, D), D ** -0.5, 0.21875, ((1, 4),))
    value_w = centred(keys[7], (D, D), D ** -0.5, 0.21875, ((1, 4),))
    value_b = centred(keys[8], (D,), 0.05, 0.75, ((0, 4),))
    out_w = centred(keys[9], (D, D), (D // 64) ** -0.5, 1.75, ((0, 4),))
    out_b = centred(keys[10], (D,), 0.3, 4.0)
    gain_mlp = jnp.clip(1.0 + 0.1 * jax.random.normal(keys[11], (D,), jnp.float32), 0.5, 1.5).astype(jnp.bfloat16)
    bias_mlp = centred(keys[12], (D,), 0.3, 4.0)
    up_w = centred(keys[13], (D, FF), D ** -0.5, 0.21875, ((1, 4),))
    up_b = centred(keys[14], (FF,), 0.3, 4.0, ((0, 4),))
    down_w = centred(keys[15], (FF, D), (FF // 2) ** -0.5, 0.15625, ((0, 4),))
    down_b = centred(keys[16], (D,), 0.3, 4.0)
    deconv_w = centred(keys[17], (D, 8 * CH), D ** -0.5, 0.21875, ((1, 4),))
    scale_norm = jnp.clip(1.0 + 0.1 * jax.random.normal(keys[18], (CH,), jnp.float32), 0.5, 1.5).astype(jnp.bfloat16)
    shift_norm = centred(keys[19], (CH,), 0.5, 6.0)
    cotangent = centred(keys[20], (ITEMS, L, 8 * CH), 1.0, 6.0, ((0, 8), (2, 4)))
    return dict(tokens=tokens, lengths=lengths, gain_attn=gain_attn, bias_attn=bias_attn, query_w=query_w, query_b=query_b, key_w=key_w, value_w=value_w, value_b=value_b, out_w=out_w, out_b=out_b, gain_mlp=gain_mlp, bias_mlp=bias_mlp, up_w=up_w, up_b=up_b, down_w=down_w, down_b=down_b, deconv_w=deconv_w, scale_norm=scale_norm, shift_norm=shift_norm, cotangent=cotangent)


EPSILON = 1e-05
PRECISE = lax.Precision.HIGHEST

@jax.custom_vjp
def low(v):
    return lax.optimization_barrier(v.astype(jnp.bfloat16)).astype(jnp.float32)

@jax.custom_vjp
def low_back(v):
    return v

def low_keep(v):
    return (low(v), None)

def low_pass(kept, grad):
    return (grad,)

def back_keep(v):
    return (v, None)

def back_low(kept, grad):
    return (low(grad),)
low.defvjp(low_keep, low_pass)
low_back.defvjp(back_keep, back_low)

def layer_norm(values, gain_vec, bias_vec):
    center = values - lax.optimization_barrier(jnp.mean(values, axis=-1, keepdims=True))
    inverse = lax.rsqrt(lax.optimization_barrier(jnp.mean(center * center, axis=-1, keepdims=True)) + EPSILON)
    return center * inverse * gain_vec + bias_vec

def matmul(left_side, right_side):
    return jnp.einsum('gnd,de->gne', left_side, right_side, precision=PRECISE)

def attend(queries, key_rows, value_rows, key_valid):
    scores = low_back(jnp.einsum('gqhe,gkhe->ghqk', queries, key_rows, precision=PRECISE) * HEAD_DIM ** (-0.5))
    scores = jnp.where(key_valid[:, None, None, :], scores, -1000000000.0)
    maximum = lax.optimization_barrier(jnp.max(scores, axis=-1, keepdims=True))
    raised = jnp.exp(scores - maximum)
    probability = low(raised / lax.optimization_barrier(jnp.sum(raised, axis=-1, keepdims=True)))
    return jnp.einsum('ghqk,gkhe->gqhe', probability, value_rows, precision=PRECISE)

def forward(inputs, item_lengths, gain_attn, bias_attn, query_w, query_b, key_w, value_w, value_b, out_w, out_b, gain_mlp, bias_mlp, up_w, up_b, down_w, down_b, deconv_w, scale_norm, shift_norm):
    group = inputs.shape[0]
    key_valid = jnp.arange(L)[None, :] < item_lengths[:, None]
    normed = low(layer_norm(inputs, gain_attn, bias_attn))
    queries = low(low_back(matmul(normed, query_w) + query_b))
    key_rows = low(low_back(matmul(normed, key_w)))
    value_rows = low(low_back(matmul(normed, value_w) + value_b))
    head_shape = (group, L, HEADS, HEAD_DIM)
    mixture = jax.checkpoint(attend)(queries.reshape(head_shape), key_rows.reshape(head_shape), value_rows.reshape(head_shape), key_valid)
    mixture = low(low_back(mixture.reshape(group, L, D)))
    middle = inputs + low_back(matmul(mixture, out_w)) + out_b
    normed_two = low(layer_norm(middle, gain_mlp, bias_mlp))
    preact = low_back(matmul(normed_two, up_w) + up_b)
    active = low(jax.nn.gelu(preact, approximate=False))
    output_rows = middle + low_back(matmul(active, down_w)) + down_b
    deconv = low_back(matmul(low(output_rows), deconv_w)).reshape(group, L, 8, CH)
    rowmask = key_valid.astype(jnp.float32)[:, :, None, None]
    voxels = (8 * item_lengths).astype(jnp.float32)[:, None]
    sum_values = lax.optimization_barrier(jnp.sum(deconv * rowmask, axis=(1, 2)))
    sum_squares = lax.optimization_barrier(jnp.sum(deconv * deconv * rowmask, axis=(1, 2)))
    center = sum_values / voxels
    spread = lax.rsqrt(sum_squares / voxels - center * center + EPSILON)
    normal = (deconv - center[:, None, None, :]) * spread[:, None, None, :]
    return (rowmask * (scale_norm * normal + shift_norm)).reshape(group, L, 8 * CH)

def reference(tokens, lengths, gain_attn, bias_attn, query_w, query_b, key_w, value_w, value_b, out_w, out_b, gain_mlp, bias_mlp, up_w, up_b, down_w, down_b, deconv_w, scale_norm, shift_norm, cotangent):
    params = tuple((entry.astype(jnp.float32) for entry in (gain_attn, bias_attn, query_w, query_b, key_w, value_w, value_b, out_w, out_b, gain_mlp, bias_mlp, up_w, up_b, down_w, down_b, deconv_w, scale_norm, shift_norm)))
    group = math.gcd(ITEMS, 8)
    rounds = ITEMS // group

    def block(totals, inputs):
        token_part, length_part, cot_part = inputs

        def applied(token_values, *param_values):
            return forward(token_values, length_part, *param_values)
        result, pullback = jax.vjp(applied, token_part.astype(jnp.float32), *params)
        grads = pullback(cot_part.astype(jnp.float32))
        return (tuple((old + new for old, new in zip(totals, grads[1:]))), (result, grads[0]))
    zeros = tuple((jnp.zeros_like(entry) for entry in params))
    totals, outputs = lax.scan(block, zeros, (tokens.reshape(rounds, group, L, D), lengths.reshape(rounds, group), cotangent.reshape(rounds, group, L, 8 * CH)))
    volume = outputs[0].reshape(ITEMS, L, 8 * CH)
    grad_tokens = outputs[1].reshape(ITEMS * L, D)
    g_gain_attn, g_bias_attn, g_query_w, g_query_b, g_key_w, g_value_w, g_value_b, g_out_w, g_out_b, g_gain_mlp, g_bias_mlp, g_up_w, g_up_b, g_down_w, g_down_b, g_deconv_w, g_scale, g_shift = totals
    return (volume, grad_tokens, g_gain_attn, g_bias_attn, g_query_w, g_query_b, g_key_w, g_value_w, g_value_b, g_out_w, g_out_b, g_gain_mlp, g_bias_mlp, g_up_w, g_up_b, g_down_w, g_down_b, g_deconv_w, g_scale, g_shift)
```

```python
import functools

import jax
import jax.numpy as jnp
from jax import lax
from jax.experimental import pallas as pl
from jax.experimental.pallas import tpu as pltpu
from jax.sharding import PartitionSpec as P

HEAD_DIM = 64
CH = 128
EPSILON = 1e-05
SCALE = HEAD_DIM ** (-0.5)
F32 = jnp.float32
BF16 = jnp.bfloat16


def dot(left, right):
    return jnp.dot(left, right, preferred_element_type=F32)


def dot_rows(left, right):
    return lax.dot_general(left, right, (((0,), (0,)), ((), ())), preferred_element_type=F32)


def dot_cols(left, right):
    return lax.dot_general(left, right, (((1,), (1,)), ((), ())), preferred_element_type=F32)


def swap(value, axis, bit):
    size = lax.axis_size(axis)
    return lax.ppermute(value, axis, [(i, i ^ bit) for i in range(size)])


def norm_stats(values):
    center = values - jnp.mean(values, axis=-1, keepdims=True)
    inverse = lax.rsqrt(jnp.mean(center * center, axis=-1, keepdims=True) + EPSILON)
    return center * inverse, inverse


def norm_backward(upstream, normal, inverse, gain_vec):
    scaled = upstream * gain_vec
    mean_part = jnp.mean(scaled, axis=-1, keepdims=True)
    mean_cross = jnp.mean(scaled * normal, axis=-1, keepdims=True)
    return inverse * (scaled - mean_part - normal * mean_cross)


def head_cols(index, head, heads):
    start = (index * heads + head) * HEAD_DIM
    return slice(start, start + HEAD_DIM)


def attend_kernel(heads, seq, len_ref, qkv_ref, o_ref, lse_ref):
    length = len_ref[pl.program_id(0)]

    def run(span):
        valid = lax.broadcasted_iota(jnp.int32, (span, span), 0) < length
        for head in range(heads):
            query = qkv_ref[:span, head_cols(0, head, heads)] * jnp.asarray(SCALE, BF16)
            keys = qkv_ref[:span, head_cols(1, head, heads)]
            vals = qkv_ref[:span, head_cols(2, head, heads)]
            scores = jnp.where(valid, dot_cols(keys, query), -1e9)
            top = jnp.max(scores, axis=0, keepdims=True)
            raised = jnp.exp(scores - top)
            total = jnp.sum(raised, axis=0, keepdims=True)
            mixed = dot_rows(vals, raised.astype(BF16)) / total
            o_ref[:span, head_cols(0, head, heads)] = mixed.T.astype(BF16)
            lse_ref[0, head : head + 1, :span] = top + jnp.log(total)
        if span < seq:
            o_ref[span:, :] = jnp.zeros((seq - span, heads * HEAD_DIM), BF16)

    half = seq // 2

    @pl.when(length <= half)
    def _():
        run(half)

    @pl.when(length > half)
    def _():
        run(seq)


def attend(lengths, qkv, items, seq, heads):
    width = heads * HEAD_DIM
    flops = 4 * items * heads * seq * seq * HEAD_DIM
    return pl.pallas_call(
        functools.partial(attend_kernel, heads, seq),
        out_shape=(
            jax.ShapeDtypeStruct((items * seq, width), BF16),
            jax.ShapeDtypeStruct((items, 8, seq), F32),
        ),
        grid_spec=pltpu.PrefetchScalarGridSpec(
            num_scalar_prefetch=1,
            grid=(items,),
            in_specs=[pl.BlockSpec((seq, 3 * width), lambda i, n: (i, 0))],
            out_specs=(
                pl.BlockSpec((seq, width), lambda i, n: (i, 0)),
                pl.BlockSpec((1, 8, seq), lambda i, n: (i, 0, 0)),
            ),
        ),
        cost_estimate=pl.CostEstimate(
            flops=flops, transcendentals=items * heads * seq * seq, bytes_accessed=8 * items * seq * width
        ),
        name="attend",
    )(lengths, qkv)


def attend_back_kernel(heads, seq, len_ref, qkv_ref, do_ref, lse_ref, out_ref):
    length = len_ref[pl.program_id(0)]

    def run(span):
        valid = lax.broadcasted_iota(jnp.int32, (span, span), 0) < length
        for head in range(heads):
            query = qkv_ref[:span, head_cols(0, head, heads)] * jnp.asarray(SCALE, BF16)
            keys = qkv_ref[:span, head_cols(1, head, heads)]
            vals = qkv_ref[:span, head_cols(2, head, heads)]
            upstream = do_ref[:span, head_cols(0, head, heads)]
            scores = jnp.where(valid, dot_cols(keys, query), -1e9)
            prob = jnp.exp(scores - lse_ref[0, head : head + 1, :span])
            val_grad = dot(prob.astype(BF16), upstream)
            prob_grad = dot_cols(vals, upstream)
            product = prob * prob_grad
            row_term = jnp.sum(product, axis=0, keepdims=True)
            score_grad = (product - prob * row_term).astype(BF16)
            key_grad = dot(score_grad, query)
            query_grad = dot_rows(keys, score_grad) * SCALE
            out_ref[:span, head_cols(0, head, heads)] = query_grad.T.astype(BF16)
            out_ref[:span, head_cols(1, head, heads)] = key_grad.astype(BF16)
            out_ref[:span, head_cols(2, head, heads)] = val_grad.astype(BF16)
        if span < seq:
            out_ref[span:, :] = jnp.zeros((seq - span, 3 * heads * HEAD_DIM), BF16)

    half = seq // 2

    @pl.when(length <= half)
    def _():
        run(half)

    @pl.when(length > half)
    def _():
        run(seq)


def attend_back(lengths, qkv, upstream, logsum, items, seq, heads):
    width = heads * HEAD_DIM
    flops = 10 * items * heads * seq * seq * HEAD_DIM
    return pl.pallas_call(
        functools.partial(attend_back_kernel, heads, seq),
        out_shape=jax.ShapeDtypeStruct((items * seq, 3 * width), BF16),
        grid_spec=pltpu.PrefetchScalarGridSpec(
            num_scalar_prefetch=1,
            grid=(items,),
            in_specs=[
                pl.BlockSpec((seq, 3 * width), lambda i, n: (i, 0)),
                pl.BlockSpec((seq, width), lambda i, n: (i, 0)),
                pl.BlockSpec((1, 8, seq), lambda i, n: (i, 0, 0)),
            ],
            out_specs=pl.BlockSpec((seq, 3 * width), lambda i, n: (i, 0)),
        ),
        cost_estimate=pl.CostEstimate(
            flops=flops, transcendentals=items * heads * seq * seq, bytes_accessed=14 * items * seq * width
        ),
        name="attend_back",
    )(lengths, qkv, upstream, logsum)


def gather_mp(block):
    core = swap(block, "mp", 1)
    far = swap(block, "mp", 2)
    return [block, core, far, swap(far, "mp", 1)]


def exchange_mp(blocks):
    return [blocks[0]] + [swap(blocks[k], "mp", k) for k in (1, 2, 3)]


def scatter_sum_mp(blocks):
    first = swap(blocks[1].astype(BF16), "mp", 1)
    third = swap(blocks[3].astype(BF16), "mp", 1)
    passed = (blocks[2] + third.astype(F32)).astype(BF16)
    return blocks[0] + first.astype(F32) + swap(passed, "mp", 2).astype(F32)


def sum_dp(value):
    size = lax.axis_size("dp")
    index = lax.axis_index("dp")
    bits = []
    bit = 1
    while bit < size:
        bits.append(bit)
        bit *= 2
    current = value.astype(BF16)
    for bit in bits:
        half = current.shape[0] // 2
        high = (index & bit) > 0
        low_part, high_part = current[:half], current[half:]
        sent = jnp.where(high, low_part, high_part)
        kept = jnp.where(high, high_part, low_part)
        current = (kept.astype(F32) + swap(sent, "dp", bit).astype(F32)).astype(BF16)
    for bit in reversed(bits):
        high = (index & bit) > 0
        other = swap(current, "dp", bit)
        current = jnp.concatenate([jnp.where(high, other, current), jnp.where(high, current, other)], axis=0)
    return current.astype(F32)


def shards(
    tokens,
    lengths,
    gain_attn,
    bias_attn,
    query_w,
    query_b,
    key_w,
    value_w,
    value_b,
    out_w,
    out_b,
    gain_mlp,
    bias_mlp,
    up_w,
    up_b,
    down_w,
    down_b,
    deconv_w,
    scale_norm,
    shift_norm,
    cotangent,
):
    items, seq, width = tokens.shape
    rows = items * seq
    ways = lax.axis_size("mp")
    me = lax.axis_index("mp")
    share = rows // ways
    offset = me * share
    head_width = query_w.shape[1]
    heads = head_width // HEAD_DIM
    gain_one = gain_attn.astype(F32)
    gain_two = gain_mlp.astype(F32)
    scale_vec = scale_norm.astype(F32)

    def row_block(value, k):
        return lax.dynamic_slice_in_dim(value, (me ^ k) * share, share, 0)

    def place_rows(blocks, dtype):
        result = jnp.zeros((rows, blocks[0].shape[1]), dtype)
        for k in range(ways):
            result = lax.dynamic_update_slice_in_dim(result, blocks[k].astype(dtype), (me ^ k) * share, 0)
        return result

    out_full = jnp.concatenate(gather_mp(out_w), axis=0)
    up_blocks = gather_mp(up_w)
    up_bias = gather_mp(up_b.reshape(1, -1))
    down_blocks = gather_mp(down_w)
    deconv_full = jnp.concatenate(gather_mp(deconv_w), axis=1)
    cot_rows = cotangent.reshape(rows, -1)
    cot = jnp.concatenate(exchange_mp([row_block(cot_rows, k) for k in range(ways)]), axis=1)

    residual = tokens.reshape(rows, width).astype(F32)
    normal_one, inverse_one = norm_stats(residual)
    normed = (normal_one * gain_one + bias_attn.astype(F32)).astype(BF16)
    qkv_w = jnp.concatenate([query_w, key_w, value_w], axis=1)
    qkv_b = jnp.concatenate([query_b, jnp.zeros_like(query_b), value_b]).astype(F32)
    qkv = (dot(normed, qkv_w) + qkv_b).astype(BF16)
    mixture_heads, logsum = attend(lengths, qkv, items, seq, heads)
    mixture = jnp.concatenate(exchange_mp([row_block(mixture_heads, k) for k in range(ways)]), axis=1)

    my_tokens = lax.dynamic_slice_in_dim(tokens.reshape(rows, width), offset, share, 0).astype(F32)
    middle = my_tokens + dot(mixture, out_full) + out_b.astype(F32)
    normal_two, inverse_two = norm_stats(middle)
    normed_two = (normal_two * gain_two + bias_mlp.astype(F32)).astype(BF16)
    preacts = [dot(normed_two, up_blocks[k]) + up_bias[k].astype(F32) for k in range(ways)]
    actives = [jax.nn.gelu(u, approximate=False).astype(BF16) for u in preacts]
    output_rows = middle + down_b.astype(F32)
    for k in range(ways):
        output_rows = output_rows + dot(actives[k], down_blocks[k])
    output_low = output_rows.astype(BF16)
    deconv = dot(output_low, deconv_full)

    piece = share
    while seq % piece:
        piece //= 2 if piece % 2 == 0 else piece
    pieces = share // piece
    first_piece = me * pieces
    piece_start = (first_piece + jnp.arange(pieces)) * piece
    piece_item = piece_start // seq
    chosen = (piece_item[:, None] == jnp.arange(items)[None, :]).astype(F32)
    slot = (piece_start % seq)[:, None] + jnp.arange(piece)[None, :]
    piece_len = jnp.sum(chosen * lengths.astype(F32)[None, :], axis=1)
    rowmask = (slot.astype(F32) < piece_len[:, None]).astype(F32)[:, :, None, None]
    shape4 = (pieces, piece, -1, CH)
    deconv4 = deconv.reshape(shape4)
    upstream = cot.astype(F32).reshape(shape4) * rowmask
    masked = deconv4 * rowmask
    sums = jnp.stack(
        [
            jnp.sum(masked, axis=(1, 2)),
            jnp.sum(masked * deconv4, axis=(1, 2)),
            jnp.sum(upstream, axis=(1, 2)),
            jnp.sum(upstream * deconv4, axis=(1, 2)),
        ],
        axis=1,
    )
    sums = jnp.sum(chosen[:, :, None, None] * sums[:, None], axis=0).reshape(-1, CH)
    sums = sums + swap(sums, "mp", 1)
    sums = (sums + swap(sums, "mp", 2)).reshape(items, 4, CH)
    voxels = (8 * lengths).astype(F32)[:, None]
    center = sums[:, 0] / voxels
    spread = lax.rsqrt(sums[:, 1] / voxels - center * center + EPSILON)
    plain_sum = sums[:, 2]
    cross_sum = spread * (sums[:, 3] - center * plain_sum)
    scale_grad = jnp.sum(cross_sum, axis=0)
    shift_grad = jnp.sum(plain_sum, axis=0)

    def per_piece(values):
        return jnp.sum(chosen[:, :, None] * values[None], axis=1)[:, None, None, :]

    center_p = per_piece(center)
    spread_p = per_piece(spread)
    normal = (deconv4 - center_p) * spread_p
    volume_rows = (rowmask * (scale_vec * normal + shift_norm.astype(F32))).reshape(share, -1)
    deconv_grad = (
        rowmask
        * (spread_p * scale_vec)
        * (upstream - per_piece(plain_sum / voxels) - normal * per_piece(cross_sum / voxels))
    )
    deconv_grad = deconv_grad.reshape(share, -1).astype(BF16)
    block = volume_rows.shape[1] // ways
    volume_blocks = [volume_rows[:, k * block : (k + 1) * block].astype(BF16) for k in range(ways)]
    volume = place_rows(exchange_mp(volume_blocks), F32).reshape(items, seq, -1)

    output_grad = dot_cols(deconv_grad, deconv_full)
    output_grad_low = output_grad.astype(BF16)
    deconv_w_full = dot_rows(output_low, deconv_grad)
    deconv_w_grad = sum_dp(scatter_sum_mp([deconv_w_full[:, k * block : (k + 1) * block] for k in range(ways)]))
    normed_two_grad = jnp.zeros((share, width), F32)
    preact_grads = []
    for k in range(ways):
        active_grad = dot_cols(output_grad_low, down_blocks[k])
        unused, gelu_back = jax.vjp(lambda u: jax.nn.gelu(u, approximate=False), preacts[k])
        preact_grad = gelu_back(active_grad)[0].astype(BF16)
        preact_grads.append(preact_grad)
        normed_two_grad = normed_two_grad + dot_cols(preact_grad, up_blocks[k])
    down_w_grad = sum_dp(scatter_sum_mp([dot_rows(actives[k], output_grad_low) for k in range(ways)]))
    middle_grad = output_grad + norm_backward(normed_two_grad, normal_two, inverse_two, gain_two)
    middle_grad_low = middle_grad.astype(BF16)
    mixture_grad = dot_cols(middle_grad_low, out_full).astype(BF16)
    mixture_grad = place_rows(
        exchange_mp([mixture_grad[:, k * head_width : (k + 1) * head_width] for k in range(ways)]), BF16
    )
    up_w_grad = sum_dp(scatter_sum_mp([dot_rows(normed_two, preact_grads[k]) for k in range(ways)]))
    out_w_full = dot_rows(mixture, middle_grad_low)
    out_w_grad = sum_dp(scatter_sum_mp([out_w_full[k * head_width : (k + 1) * head_width] for k in range(ways)]))

    qkv_grad = attend_back(lengths, qkv, mixture_grad, logsum, items, seq, heads)
    qkv_w_grad = sum_dp(dot_rows(normed, qkv_grad))
    qkv_b_grad = jnp.sum(qkv_grad.astype(F32), axis=0)
    normed_part = dot_cols(qkv_grad, qkv_w)
    gain_one_grad = jnp.sum(normed_part * normal_one, axis=0)
    bias_one_grad = jnp.sum(normed_part, axis=0)
    normed_grad = scatter_sum_mp([row_block(normed_part, k) for k in range(ways)])
    my_normal, my_inverse = norm_stats(my_tokens)
    tokens_grad = middle_grad + norm_backward(normed_grad, my_normal, my_inverse, gain_one)

    up_b_parts = [jnp.sum(g.astype(F32), axis=0) for g in preact_grads]
    whole = jnp.stack(
        [
            gain_one_grad,
            bias_one_grad,
            jnp.sum(normed_two_grad * normal_two, axis=0),
            jnp.sum(normed_two_grad, axis=0),
            jnp.sum(middle_grad, axis=0),
            jnp.sum(output_grad, axis=0),
        ]
    )
    count = whole.shape[0]
    core = swap(jnp.concatenate([whole, up_b_parts[1][None], up_b_parts[3][None]], axis=0), "mp", 1)
    whole = whole + core[:count]
    far = swap(jnp.concatenate([whole, (up_b_parts[2] + core[count + 1])[None]], axis=0), "mp", 2)
    whole = whole + far[:count]
    up_b_grad = up_b_parts[0] + core[count] + far[count]
    flat = jnp.concatenate([whole.reshape(-1), up_b_grad, qkv_b_grad, scale_grad, shift_grad])
    lines = -(-flat.shape[0] // 1024) * 8
    flat = jnp.pad(flat, (0, lines * 128 - flat.shape[0])).reshape(lines, 128)
    bit = 1
    while bit < lax.axis_size("dp"):
        flat = flat + swap(flat, "dp", bit)
        bit *= 2
    flat = flat.reshape(-1)
    vectors = flat[: count * width].reshape(count, width)
    place = count * width
    up_b_grad = flat[place : place + up_b_grad.shape[0]]
    place += up_b_grad.shape[0]
    query_b_grad = flat[place : place + head_width]
    value_b_grad = flat[place + 2 * head_width : place + 3 * head_width]
    place += 3 * head_width
    scale_grad = flat[place : place + CH]
    shift_grad = flat[place + CH : place + 2 * CH]
    return (
        volume,
        tokens_grad,
        vectors[0],
        vectors[1],
        qkv_w_grad[:, :head_width],
        query_b_grad,
        qkv_w_grad[:, head_width : 2 * head_width],
        qkv_w_grad[:, 2 * head_width :],
        value_b_grad,
        out_w_grad,
        vectors[4],
        vectors[2],
        vectors[3],
        up_w_grad,
        up_b_grad,
        down_w_grad,
        vectors[5],
        deconv_w_grad,
        scale_grad,
        shift_grad,
    )


def solution(mesh):
    in_specs = (
        P("dp", None, None),
        P("dp"),
        P(),
        P(),
        P(None, "mp"),
        P("mp"),
        P(None, "mp"),
        P(None, "mp"),
        P("mp"),
        P("mp", None),
        P(),
        P(),
        P(),
        P(None, "mp"),
        P("mp"),
        P("mp", None),
        P(),
        P(None, "mp"),
        P(),
        P(),
        P("dp", None, "mp"),
    )
    out_specs = (
        P("dp", None, "mp"),
        P(("dp", "mp"), None),
        P(),
        P(),
        P(None, "mp"),
        P("mp"),
        P(None, "mp"),
        P(None, "mp"),
        P("mp"),
        P("mp", None),
        P(),
        P(),
        P(),
        P(None, "mp"),
        P("mp"),
        P("mp", None),
        P(),
        P(None, "mp"),
        P(),
        P(),
    )
    return jax.shard_map(shards, mesh=mesh, in_specs=in_specs, out_specs=out_specs, check_vma=False)
```

```python
import functools

import jax
import jax.numpy as jnp
from jax import lax
from jax.experimental import pallas as pl
from jax.experimental.pallas import tpu as pltpu
from jax.sharding import PartitionSpec as P

HEAD_DIM = 64
CH = 128
EPSILON = 1e-05
SCALE = HEAD_DIM ** (-0.5)
F32 = jnp.float32
BF16 = jnp.bfloat16
TILE = 256
PIECE = 128
PAD = 16
VECTORS = 6
COST = 1
VMEM_LIMIT = 56 * 1024 * 1024


def dot(left, right):
    return jnp.dot(left, right, preferred_element_type=F32)


def dot_rows(left, right):
    return lax.dot_general(left, right, (((0,), (0,)), ((), ())), preferred_element_type=F32)


def dot_cols(left, right):
    return lax.dot_general(left, right, (((1,), (1,)), ((), ())), preferred_element_type=F32)


def swap(value, axis, bit):
    size = lax.axis_size(axis)
    return lax.ppermute(value, axis, [(i, i ^ bit) for i in range(size)])


def norm_stats(values):
    center = values - jnp.mean(values, axis=-1, keepdims=True)
    inverse = lax.rsqrt(jnp.mean(center * center, axis=-1, keepdims=True) + EPSILON)
    return center * inverse, inverse


def norm_backward(upstream, normal, inverse, gain_vec):
    scaled = upstream * gain_vec
    mean_part = jnp.mean(scaled, axis=-1, keepdims=True)
    mean_cross = jnp.mean(scaled * normal, axis=-1, keepdims=True)
    return inverse * (scaled - mean_part - normal * mean_cross)


def vmem():
    return pl.BlockSpec(memory_space=pltpu.VMEM)


def anywhere():
    return pl.BlockSpec(memory_space=pl.ANY)


def smem():
    return pl.BlockSpec(memory_space=pltpu.SMEM)


def shape(dims, dtype):
    return jax.ShapeDtypeStruct(dims, dtype)


def join(*values):
    return lax.optimization_barrier(values)


def params(name, flops, moved):
    return dict(
        compiler_params=pltpu.CompilerParams(vmem_limit_bytes=VMEM_LIMIT),
        cost_estimate=pl.CostEstimate(flops=flops // COST, transcendentals=0, bytes_accessed=moved // COST),
        name=name,
    )


def head_cols(head):
    return slice(head * HEAD_DIM, (head + 1) * HEAD_DIM)


def tiles(width):
    return [slice(start, start + TILE) for start in range(0, width, TILE)]


def attend_kernel(
    items, heads, span_rows, info_ref, tok_ref, vec_ref, bias_ref, qw_ref, kw_ref, vw_ref,
    normed_ref, q_ref, k_ref, v_ref, lse_ref, near_ref, other_ref, o_ref
):
    seq = tok_ref.shape[0]
    item = pl.program_id(0)
    length = info_ref[item]
    for start in range(0, seq, PIECE):
        rows = slice(start, start + PIECE)
        normal, unused = norm_stats(tok_ref[rows, :].astype(F32))
        normed_ref[rows, :] = (normal * vec_ref[0:1, :] + vec_ref[1:2, :]).astype(BF16)
    normed = normed_ref[...]
    q_ref[...] = (dot(normed, qw_ref[...]) + bias_ref[0:1, :]).astype(BF16) * jnp.asarray(SCALE, BF16)
    k_ref[...] = dot(normed, kw_ref[...]).astype(BF16)
    v_ref[...] = (dot(normed, vw_ref[...]) + bias_ref[1:2, :]).astype(BF16)

    def run(span):
        valid = lax.broadcasted_iota(jnp.int32, (span, span), 0) < length
        for head in range(heads):
            cols = head_cols(head)
            scores = jnp.where(valid, dot_cols(k_ref[:span, cols], q_ref[:span, cols]), -1e9)
            top = jnp.max(scores, axis=0, keepdims=True)
            raised = jnp.exp(scores - top)
            total = jnp.sum(raised, axis=0, keepdims=True)
            mixed = dot_rows(v_ref[:span, cols], raised.astype(BF16)) / total
            o_ref[pl.ds(pl.multiple_of(item * seq, seq), span), cols] = mixed.T.astype(BF16)
            lse_ref[0, head : head + 1, :span] = top + jnp.log(total)
        if span < seq:
            o_ref[pl.ds(pl.multiple_of(item * seq + span, span), seq - span), :] = jnp.zeros(
                (seq - span, heads * HEAD_DIM), BF16
            )

    half = seq // 2

    @pl.when(length <= half)
    def _():
        run(half)

    @pl.when(length > half)
    def _():
        run(seq)

    @pl.when(item == items - 1)
    def _():
        start = info_ref[items] // 2 * span_rows
        near_ref[...] = o_ref[pl.ds(pl.multiple_of(start, PIECE), span_rows), :]
        other_ref[...] = o_ref[pl.ds(pl.multiple_of(span_rows - start, PIECE), span_rows), :]


def attend(info, rows2d, vecs, bias, query_w, key_w, value_w, items, seq):
    rows, width = rows2d.shape
    hw = query_w.shape[1]
    heads = hw // HEAD_DIM
    row_block = lambda cols: pl.BlockSpec((seq, cols), lambda i, n: (i, 0))
    whole = lambda dims: pl.BlockSpec(dims, lambda i, n: (0,) * len(dims))
    return pl.pallas_call(
        functools.partial(attend_kernel, items, heads, rows // 2),
        out_shape=[shape((rows, width), BF16)]
        + [shape((rows, hw), BF16)] * 3
        + [shape((items, 8, seq), F32)]
        + [shape((rows // 2, hw), BF16)] * 2,
        grid_spec=pltpu.PrefetchScalarGridSpec(
            num_scalar_prefetch=1,
            grid=(items,),
            in_specs=[row_block(width), whole(vecs.shape), whole(bias.shape)] + [whole((width, hw))] * 3,
            out_specs=[row_block(width)]
            + [row_block(hw)] * 3
            + [pl.BlockSpec((1, 8, seq), lambda i, n: (i, 0, 0))]
            + [whole((rows // 2, hw))] * 2,
            scratch_shapes=[pltpu.VMEM((rows, hw), BF16)],
        ),
        **params("attend", 6 * rows * width * hw + 4 * rows * seq * hw, 4 * rows * width),
    )(info, rows2d, vecs, bias, query_w, key_w, value_w)


def attend_back_kernel(
    items, heads, share, info_ref, tok_ref, normed_ref, q_ref, k_ref, v_ref, lse_ref, qw_ref, kw_ref, vw_ref,
    vec_in, low_in, near_ref, other_ref, *rest
):
    grad_ref, send_ref, keep_ref, pass_ref, sums_ref, do_ref, part_ref, grad_acc, dq_ref, dk_ref, dv_ref = rest
    seq = tok_ref.shape[0]
    hw = heads * HEAD_DIM
    item = pl.program_id(0)
    length = info_ref[item]
    me = info_ref[items]

    @pl.when(item == 0)
    def _():
        begin = me // 2 * 2 * share
        do_ref[pl.ds(pl.multiple_of(begin, PIECE), 2 * share), :] = near_ref[...]
        do_ref[pl.ds(pl.multiple_of(2 * share - begin, PIECE), 2 * share), :] = other_ref[...]
        sums_ref[...] = jnp.zeros_like(sums_ref)
        grad_acc[...] = jnp.zeros_like(grad_acc)

    def run(span):
        valid = lax.broadcasted_iota(jnp.int32, (span, span), 0) < length
        for head in range(heads):
            cols = head_cols(head)
            query, keys, vals = q_ref[:span, cols], k_ref[:span, cols], v_ref[:span, cols]
            upstream = do_ref[pl.ds(pl.multiple_of(item * seq, seq), span), cols]
            scores = jnp.where(valid, dot_cols(keys, query), -1e9)
            prob = jnp.exp(scores - lse_ref[0, head : head + 1, :span])
            dv_ref[:span, cols] = dot(prob.astype(BF16), upstream).astype(BF16)
            prob_grad = dot_cols(vals, upstream)
            product = prob * prob_grad
            row_term = jnp.sum(product, axis=0, keepdims=True)
            score_grad = (product - prob * row_term).astype(BF16)
            dk_ref[:span, cols] = dot(score_grad, query).astype(BF16)
            dq_ref[:span, cols] = (dot_rows(keys, score_grad) * SCALE).T.astype(BF16)
        start = pl.multiple_of(item * seq, seq)
        for index, ref in enumerate((dq_ref, dk_ref, dv_ref)):
            grad_acc[index * hw : (index + 1) * hw, :] += dot_rows(ref[:span, :], normed_ref[:span, :])
            if index != 1:
                sums_ref[2 + index : 3 + index, :hw] += jnp.sum(ref[:span, :].astype(F32), axis=0, keepdims=True)
        part = dot_cols(dq_ref[:span, :], qw_ref[...])
        part += dot_cols(dk_ref[:span, :], kw_ref[...])
        part += dot_cols(dv_ref[:span, :], vw_ref[...])
        part_ref[pl.ds(start, span), :] = part
        for base in range(0, span, PIECE):
            normal, unused = norm_stats(tok_ref[base : base + PIECE, :].astype(F32))
            piece = part_ref[pl.ds(pl.multiple_of(start + base, PIECE), PIECE), :]
            sums_ref[0:1, :] += jnp.sum(piece * normal, axis=0, keepdims=True)
            sums_ref[1:2, :] += jnp.sum(piece, axis=0, keepdims=True)
        if span < seq:
            part_ref[pl.ds(pl.multiple_of(start + span, span), seq - span), :] = jnp.zeros(
                (seq - span, part.shape[1]), F32
            )

    half = seq // 2

    @pl.when(length <= half)
    def _():
        run(half)

    @pl.when(length > half)
    def _():
        run(seq)

    @pl.when(item == items - 1)
    def _():
        grad_ref[...] = grad_acc[...].astype(BF16)

        def block(k):
            return part_ref[pl.ds(pl.multiple_of((me ^ k) * share, PIECE), share), :]

        keep_ref[...] = block(0)
        pass_ref[...] = block(2)
        send_ref[:share, :] = block(1).astype(BF16)
        send_ref[share : 2 * share, :] = block(3).astype(BF16)
        vectors = jnp.concatenate([sums_ref[0:2, :], 0.5 * vec_in[0:3, :], 0.5 * low_in[0:1, :]], axis=0)
        sums_ref[8 : 8 + VECTORS, :] = vectors
        send_ref[2 * share :, :] = jnp.concatenate([vectors, jnp.zeros((PAD - VECTORS, vectors.shape[1]), F32)], axis=0).astype(BF16)


def attend_back(
    info, rows2d, normed, q, k, v, lse, query_w, key_w, value_w, vec_in, low_in, near, other, items, seq, share
):
    rows, width = rows2d.shape
    hw = query_w.shape[1]
    heads = hw // HEAD_DIM
    row_block = lambda cols: pl.BlockSpec((seq, cols), lambda i, n: (i, 0))
    whole = lambda dims: pl.BlockSpec(dims, lambda i, n: (0,) * len(dims))
    return pl.pallas_call(
        functools.partial(attend_back_kernel, items, heads, share),
        out_shape=[
            shape((3 * hw, width), BF16),
            shape((2 * share + PAD, width), BF16),
            shape((share, width), F32),
            shape((share, width), F32),
            shape((16, width), F32),
        ],
        grid_spec=pltpu.PrefetchScalarGridSpec(
            num_scalar_prefetch=1,
            grid=(items,),
            in_specs=[row_block(width), row_block(width)]
            + [row_block(hw)] * 3
            + [pl.BlockSpec((1, 8, seq), lambda i, n: (i, 0, 0))]
            + [whole((width, hw))] * 3
            + [whole(vec_in.shape), whole(low_in.shape)]
            + [whole((2 * share, hw))] * 2,
            out_specs=[
                whole((3 * hw, width)),
                whole((2 * share + PAD, width)),
                whole((share, width)),
                whole((share, width)),
                whole((16, width)),
            ],
            scratch_shapes=[
                pltpu.VMEM((rows, hw), BF16),
                pltpu.VMEM((rows, width), F32),
                pltpu.VMEM((3 * hw, width), F32),
                pltpu.VMEM((seq, hw), BF16),
                pltpu.VMEM((seq, hw), BF16),
                pltpu.VMEM((seq, hw), BF16),
            ],
        ),
        **params("attend_back", 12 * rows * width * hw + 10 * rows * seq * hw, 8 * rows * width),
    )(info, rows2d, normed, q, k, v, lse, query_w, key_w, value_w, vec_in, low_in, near, other)


def load_all(pairs, sems):
    copies = [pltpu.make_async_copy(source, target, sems.at[i]) for i, (source, target) in enumerate(pairs)]
    for copy in copies:
        copy.start()
    return copies


def halves(count):
    return [slice(start, start + count // 2) for start in range(0, count, count // 2)]


def project_kernel(near_ref, far_ref, own_ref, pack_ref, out_ref, buf, sem):
    copy = pltpu.make_async_copy(pack_ref.at[pl.ds(0, buf.shape[0]), :], buf, sem)
    copy.start()
    copy.wait()
    for cols in tiles(out_ref.shape[1]):
        out_ref[:, cols] = (dot(near_ref[...], own_ref[:, cols]) + dot(far_ref[...], buf[:, cols])).astype(BF16)


def project(near, far, own, pack):
    span, hw = near.shape
    width = own.shape[1]
    return pl.pallas_call(
        project_kernel,
        out_shape=shape((span, width), BF16),
        in_specs=[vmem()] * 3 + [anywhere()],
        out_specs=vmem(),
        scratch_shapes=[pltpu.VMEM((hw, width), BF16), pltpu.SemaphoreType.DMA],
        **params("project", 4 * span * width * hw, 4 * span * width),
    )(near, far, own, pack)


def expand_kernel(items, hw, info_ref, tok_ref, vec_ref, part_ref, other_ref, up_ref, bias_ref, pack_ref, *rest):
    mid_ref, normed_ref, act_ref, slope_ref, wu, far_bias, tok_buf, sems = rest
    span, width = mid_ref.shape
    start = pl.multiple_of(info_ref[items] // 2 * span, PIECE)
    copies = load_all(
        [
            (tok_ref.at[pl.ds(start, span), :], tok_buf),
            (up_ref, wu.at[0]),
            (pack_ref.at[pl.ds(hw, width), :], wu.at[1]),
            (pack_ref.at[pl.ds(hw + width, PAD), :], far_bias),
        ],
        sems,
    )
    copies[0].wait()
    for base in range(0, span, PIECE):
        rows = slice(base, base + PIECE)
        mid = tok_buf[rows, :].astype(F32) + vec_ref[0:1, :] + part_ref[rows, :].astype(F32) + other_ref[rows, :].astype(F32)
        mid_ref[rows, :] = mid
        normal, unused = norm_stats(mid)
        normed_ref[rows, :] = (normal * vec_ref[1:2, :] + vec_ref[2:3, :]).astype(BF16)
    for copy in copies[1:]:
        copy.wait()

    def body(step, carry):
        block = step % 2
        rows = pl.ds(pl.multiple_of(step // 2 * (span // 2), PIECE), span // 2)
        for cols in tiles(width):
            own_bias, other_bias = bias_ref[0:1, cols], far_bias[:, cols].astype(F32)[0:1]
            preact = dot(normed_ref[rows, :], wu[block, :, cols]) + jnp.where(block == 0, own_bias, other_bias)
            normal_cdf = 0.5 * lax.erf(preact * (0.5**0.5)) + 0.5
            density = jnp.exp(preact * preact * -0.5) * 0.3989422804014327
            act_ref[block, rows, cols] = (preact * normal_cdf).astype(BF16)
            slope_ref[block, rows, cols] = (normal_cdf + preact * density).astype(BF16)
        return carry

    lax.fori_loop(0, 4, body, 0)


def expand(info, rows2d, vecs, part, other, up_w, bias, pack, items, hw):
    span, width = part.shape
    return pl.pallas_call(
        functools.partial(expand_kernel, items, hw),
        out_shape=[
            shape((span, width), F32),
            shape((span, width), BF16),
            shape((2, span, width), BF16),
            shape((2, span, width), BF16),
        ],
        in_specs=[smem(), anywhere(), vmem(), vmem(), vmem(), anywhere(), vmem(), anywhere()],
        out_specs=[vmem()] * 4,
        scratch_shapes=[
            pltpu.VMEM((2, width, width), BF16),
            pltpu.VMEM((PAD, width), BF16),
            pltpu.VMEM((span, width), BF16),
            pltpu.SemaphoreType.DMA((4,)),
        ],
        **params("expand", 4 * span * width * width, 14 * width * width),
    )(info, rows2d, vecs, part, other, up_w, bias, pack)


def contract_kernel(act_ref, down_ref, pack_ref, out_ref, wd, sems):
    span, width = out_ref.shape
    for copy in load_all([(down_ref, wd.at[0]), (pack_ref.at[pl.ds(0, width), :], wd.at[1])], sems):
        copy.wait()
    for cols in tiles(width):
        out_ref[:, cols] = (dot(act_ref[0], wd[0, :, cols]) + dot(act_ref[1], wd[1, :, cols])).astype(BF16)


def contract(act, down_w, pack):
    unused, span, width = act.shape
    return pl.pallas_call(
        contract_kernel,
        out_shape=shape((span, width), BF16),
        in_specs=[vmem(), anywhere(), anywhere()],
        out_specs=vmem(),
        scratch_shapes=[pltpu.VMEM((2, width, width), BF16), pltpu.SemaphoreType.DMA((2,))],
        **params("contract", 4 * span * width * width, 8 * width * width),
    )(act, down_w, pack)


def piece_place(info_ref, items, seq, span, index):
    piece = info_ref[items] // 2 * (span // PIECE) + index
    per_item = seq // PIECE
    item = piece // per_item
    length = info_ref[item]
    slot = lax.broadcasted_iota(jnp.int32, (PIECE, 1), 0) + (piece % per_item) * PIECE
    return item, length, (slot < length).astype(F32)


def convolve_kernel(items, seq, info_ref, vec_ref, mid_ref, part_ref, other_ref, conv_ref, pack_ref, cot_ref, far_cot, *rest):
    low_ref, z_ref, sums_ref, wc, cots, sems = rest
    span, width = mid_ref.shape
    block = wc.shape[1]
    start = pl.multiple_of(info_ref[items] // 2 * span, PIECE)
    copies = load_all(
        [
            (conv_ref.at[pl.ds(width, block), :], wc.at[0]),
            (pack_ref.at[pl.ds(width, block), :], wc.at[1]),
            (cot_ref.at[pl.ds(start, span), :], cots.at[0]),
            (far_cot, cots.at[1]),
        ],
        sems,
    )
    low_ref[...] = (
        mid_ref[...] + vec_ref[3:4, :] + part_ref[...].astype(F32) + other_ref[...].astype(F32)
    ).astype(BF16)
    for copy in copies:
        copy.wait()
    sums_ref[...] = jnp.zeros_like(sums_ref)
    for k in range(2):
        z_ref[k] = dot_cols(low_ref[...], wc[k])
        for index in range(span // PIECE):
            rows = slice(index * PIECE, (index + 1) * PIECE)
            item, unused, mask = piece_place(info_ref, items, seq, span, index)
            z = z_ref[k, rows, :]
            masked = z * mask
            upstream = cots[k, rows, :].astype(F32) * mask
            lines = [
                jnp.sum(part, axis=0, keepdims=True) for part in (masked, masked * z, upstream, upstream * z)
            ]
            total = jnp.concatenate(lines, axis=0)
            for base in range(0, block, CH):
                sums_ref[item] += total[:, base : base + CH]


def convolve(info, vecs, mid, part, other, own_pack, pack, cot_rows, far_cot, items, seq):
    span, width = mid.shape
    block = cot_rows.shape[1]
    return pl.pallas_call(
        functools.partial(convolve_kernel, items, seq),
        out_shape=[shape((span, width), BF16), shape((2, span, block), F32), shape((items, 4, CH), F32)],
        in_specs=[smem()] + [vmem()] * 4 + [anywhere()] * 4,
        out_specs=[vmem()] * 3,
        scratch_shapes=[
            pltpu.VMEM((2, block, width), BF16),
            pltpu.VMEM((2, span, block), BF16),
            pltpu.SemaphoreType.DMA((4,)),
        ],
        **params("convolve", 4 * span * width * block, 14 * width * width),
    )(info, vecs, mid, part, other, own_pack, pack, cot_rows, far_cot)


def norm_back_kernel(items, seq, info_ref, norm_ref, tot_ref, got_ref, z_ref, conv_ref, pack_ref, cot_ref, far_cot, *rest):
    near_ref, far_ref, dz_ref, out_ref, sums_ref, wc, cots, sems = rest
    span, width = out_ref.shape
    block = z_ref.shape[2]
    start = pl.multiple_of(info_ref[items] // 2 * span, PIECE)
    copies = load_all(
        [
            (conv_ref.at[pl.ds(width, block), :], wc.at[0]),
            (pack_ref.at[pl.ds(width, block), :], wc.at[1]),
            (cot_ref.at[pl.ds(start, span), :], cots.at[0]),
            (far_cot, cots.at[1]),
        ],
        sems,
    )
    scale, shift = norm_ref[0:1, :], norm_ref[1:2, :]

    def item_terms(item, length):
        count = (8 * length).astype(F32)
        total = tot_ref[item] + got_ref[item]
        center = total[0:1] / count
        spread = lax.rsqrt(total[1:2] / count - center * center + EPSILON)
        plain = total[2:3]
        cross = spread * (total[3:4] - center * plain)
        return count, center, spread, plain, cross

    sums_ref[...] = jnp.zeros_like(sums_ref)
    for item in range(items):
        unused, unused, unused, plain, cross = item_terms(item, info_ref[item])
        sums_ref[0:1, :CH] += cross
        sums_ref[0:1, CH : 2 * CH] += plain
    for copy in copies:
        copy.wait()
    for index in range(span // PIECE):
        rows = slice(index * PIECE, (index + 1) * PIECE)
        item, length, mask = piece_place(info_ref, items, seq, span, index)
        count, center, spread, plain, cross = item_terms(item, length)
        terms = [center, spread, plain / count, cross / count, scale, shift, spread * scale]
        wide = [jnp.concatenate([t] * (block // CH), axis=1) for t in terms]
        center, spread, plain, cross, scale_w, shift_w, factor = wide
        for k, vol_ref in enumerate((near_ref, far_ref)):
            normal = (z_ref[k, rows, :] - center) * spread
            vol_ref[rows, :] = (mask * (scale_w * normal + shift_w)).astype(BF16)
            upstream = cots[k, rows, :].astype(F32)
            dz_ref[k, rows, :] = (mask * factor * (upstream - plain - normal * cross)).astype(BF16)
    for cols in tiles(width):
        out_ref[:, cols] = (dot(dz_ref[0], wc[0, :, cols]) + dot(dz_ref[1], wc[1, :, cols])).astype(BF16)


def norm_back(info, norms, total, got, z, own_pack, pack, cot_rows, far_cot, items, seq):
    unused, span, block = z.shape
    width = pack.shape[1]
    return pl.pallas_call(
        functools.partial(norm_back_kernel, items, seq),
        out_shape=[
            shape((span, block), BF16),
            shape((span, block), BF16),
            shape((2, span, block), BF16),
            shape((span, width), BF16),
            shape((8, width), F32),
        ],
        in_specs=[smem()] + [vmem()] * 4 + [anywhere()] * 4,
        out_specs=[vmem()] * 5,
        scratch_shapes=[
            pltpu.VMEM((2, block, width), BF16),
            pltpu.VMEM((2, span, block), BF16),
            pltpu.SemaphoreType.DMA((4,)),
        ],
        **params("norm_back", 4 * span * width * block, 6 * width * width),
    )(info, norms, total, got, z, own_pack, pack, cot_rows, far_cot)


def mlp_back_kernel(hw, part_ref, other_ref, slope_ref, up_ref, down_ref, pack_a, pack_b, *rest):
    low_ref, du_ref, out_ref, sums_ref, up_sums, wu, wd, sems = rest
    span, width = out_ref.shape
    copies = load_all(
        [
            (down_ref, wd.at[0]),
            (pack_b.at[pl.ds(0, width), :], wd.at[1]),
            (up_ref, wu.at[0]),
            (pack_a.at[pl.ds(hw, width), :], wu.at[1]),
        ],
        sems,
    )
    sums_ref[...] = jnp.zeros_like(sums_ref)
    up_sums[...] = jnp.zeros_like(up_sums)
    for rows in halves(span):
        grad = part_ref[rows, :].astype(F32) + other_ref[rows, :].astype(F32)
        low_ref[rows, :] = grad.astype(BF16)
        sums_ref[0:1, :] += jnp.sum(grad, axis=0, keepdims=True)
    for copy in copies[:2]:
        copy.wait()

    def body(step, carry):
        block = step % 2
        rows = pl.ds(pl.multiple_of(step // 2 * (span // 2), PIECE), span // 2)
        for cols in tiles(width):
            grad = dot_cols(low_ref[rows, :], wd[block, cols, :]) * slope_ref[block, rows, cols].astype(F32)
            low = grad.astype(BF16)
            du_ref[block, rows, cols] = low
            up_sums[block, 0:1, cols] += jnp.sum(low.astype(F32), axis=0, keepdims=True)
        return carry

    lax.fori_loop(0, 4, body, 0)
    for copy in copies[2:]:
        copy.wait()
    for cols in tiles(width):
        out_ref[:, cols] = (dot_cols(du_ref[0], wu[0, cols, :]) + dot_cols(du_ref[1], wu[1, cols, :])).astype(BF16)


def mlp_back(part, other, slope, up_w, down_w, pack_a, pack_b, hw):
    span, width = part.shape
    return pl.pallas_call(
        functools.partial(mlp_back_kernel, hw),
        out_shape=[
            shape((span, width), BF16),
            shape((2, span, width), BF16),
            shape((span, width), BF16),
            shape((8, width), F32),
            shape((2, 8, width), F32),
        ],
        in_specs=[vmem()] * 3 + [anywhere()] * 4,
        out_specs=[vmem()] * 5,
        scratch_shapes=[
            pltpu.VMEM((2, width, width), BF16),
            pltpu.VMEM((2, width, width), BF16),
            pltpu.SemaphoreType.DMA((4,)),
        ],
        **params("mlp_back", 8 * span * width * width, 20 * width * width),
    )(part, other, slope, up_w, down_w, pack_a, pack_b)


def mid_back_kernel(items, share, info_ref, vec_ref, mid_ref, part_ref, other_ref, grad_ref, got_ref, out_w, pack_ref, *rest):
    near_ref, far_ref, em_ref, mine_ref, sums_ref, wo, dmid_ref, sem = rest
    span, width = mid_ref.shape
    copy = pltpu.make_async_copy(pack_ref.at[pl.ds(0, wo.shape[0]), :], wo, sem)
    copy.start()
    sums_ref[...] = jnp.zeros_like(sums_ref)
    for base in range(0, span, PIECE):
        rows = slice(base, base + PIECE)
        normal, inverse = norm_stats(mid_ref[rows, :])
        grad = grad_ref[rows, :].astype(F32) + got_ref[rows, :].astype(F32)
        dmid = part_ref[rows, :].astype(F32) + other_ref[rows, :].astype(F32)
        dmid += norm_backward(grad, normal, inverse, vec_ref[1:2, :])
        dmid_ref[rows, :] = dmid
        em_ref[rows, :] = dmid.astype(BF16)
        sums_ref[0:1, :] += jnp.sum(grad * normal, axis=0, keepdims=True)
        sums_ref[1:2, :] += jnp.sum(grad, axis=0, keepdims=True)
        sums_ref[2:3, :] += jnp.sum(dmid, axis=0, keepdims=True)
    copy.wait()
    far_ref[...] = dot_cols(em_ref[...], wo[...]).astype(BF16)
    near_ref[...] = dot_cols(em_ref[...], out_w[...]).astype(BF16)
    mine_ref[...] = dmid_ref[pl.ds(pl.multiple_of(info_ref[items] % 2 * share, PIECE), share), :]


def mid_back(info, vecs, mid, part, other, grad, got, out_w, pack, items):
    span, width = mid.shape
    hw = out_w.shape[0]
    return pl.pallas_call(
        functools.partial(mid_back_kernel, items, span // 2),
        out_shape=[
            shape((span, hw), BF16),
            shape((span, hw), BF16),
            shape((span, width), BF16),
            shape((span // 2, width), F32),
            shape((8, width), F32),
        ],
        in_specs=[smem()] + [vmem()] * 7 + [anywhere()],
        out_specs=[vmem()] * 5,
        scratch_shapes=[
            pltpu.VMEM((hw, width), BF16),
            pltpu.VMEM((span, width), F32),
            pltpu.SemaphoreType.DMA,
        ],
        **params("mid_back", 4 * span * width * hw, 12 * width * width),
    )(info, vecs, mid, part, other, grad, got, out_w, pack)


def grads_kernel(count, *refs):
    lefts, rights, outs = refs[:count], refs[count : 2 * count], refs[2 * count :]
    begin = 0
    for left, right in zip(lefts, rights):
        size = left.shape[-1]
        for block in range(2):
            for base in range(0, size, TILE):
                cols = slice(base, min(base + TILE, size))
                lhs = left[block, :, cols] if len(left.shape) == 3 else left[:, cols]
                rhs = right[block] if len(right.shape) == 3 else right[...]
                outs[block][begin + base : begin + cols.stop, :] = dot_rows(lhs, rhs).astype(BF16)
        begin += size


def grads(name, lefts, rights):
    span, width = rights[0].shape[-2:]
    size = sum(left.shape[-1] for left in lefts)
    return pl.pallas_call(
        functools.partial(grads_kernel, len(lefts)),
        out_shape=[shape((size, width), BF16)] * 2,
        in_specs=[vmem()] * (2 * len(lefts)),
        out_specs=[vmem()] * 2,
        **params(name, 4 * span * size * width, 8 * size * width),
    )(*lefts, *rights)


def add_low(left, right):
    return (left.astype(F32) + right.astype(F32)).astype(BF16)


def bit_of(axis, bit):
    return (lax.axis_index(axis) // bit) % 2


def take_half(value, high):
    half = value.shape[0] // 2
    return lax.dynamic_slice_in_dim(value, high * half, half, 0)


def put_half(mine, other, high):
    return jnp.concatenate([jnp.where(high > 0, other, mine), jnp.where(high > 0, mine, other)], axis=0)


def dp_bits():
    bits = [1]
    while 2 * bits[-1] < lax.axis_size("dp"):
        bits.append(2 * bits[-1])
    return bits


def sum_dp(current):
    for bit in dp_bits():
        high = bit_of("dp", bit)
        got = swap(take_half(current, 1 - high), "dp", bit)
        current = add_low(take_half(current, high), got)
    for bit in reversed(dp_bits()):
        current = put_half(current, swap(current, "dp", bit), bit_of("dp", bit))
    return current.astype(F32)


def shards(
    tokens, lengths, gain_attn, bias_attn, query_w, query_b, key_w, value_w, value_b, out_w, out_b, gain_mlp, bias_mlp,
    up_w, up_b, down_w, down_b, deconv_w, scale_norm, shift_norm, cotangent
):
    items, seq, width = tokens.shape
    rows = items * seq
    me = lax.axis_index("mp")
    share = rows // lax.axis_size("mp")
    span = rows // 2
    hw = query_w.shape[1]
    info = jnp.concatenate([lengths, me[None].astype(jnp.int32)])
    rows2d = tokens.reshape(rows, width)
    side = bit_of("dp", 1)
    chip = bit_of("mp", 2)

    bias_rows = jnp.broadcast_to(up_b[None, :], (PAD, up_b.shape[0]))
    pack_a = jnp.concatenate([out_w, up_w, bias_rows], axis=0)
    pack_b = jnp.concatenate([down_w, deconv_w.T], axis=0)
    half_a = swap(take_half(pack_a, side), "mp", 2)

    vecs_one = jnp.stack([gain_attn, bias_attn]).astype(F32)
    bias_one = jnp.stack([query_b, value_b]).astype(F32)
    normed, q, k, v, lse, near, other = attend(
        info, rows2d, vecs_one, bias_one, query_w, key_w, value_w, items, seq
    )
    half_a, near, other, pack_b = join(half_a, near, other, pack_b)
    far = swap(other, "mp", 2)
    rest_a = swap(half_a, "dp", 1)
    half_b = swap(take_half(pack_b, side), "mp", 2)
    cot_rows = cotangent.reshape(rows, -1)
    far, rest_a, half_b, cot_rows = join(far, rest_a, half_b, cot_rows)
    far_a = put_half(half_a, rest_a, side)
    far_cot = swap(lax.dynamic_slice_in_dim(cot_rows, (1 - chip) * span, span, 0), "mp", 2)
    rest_b = swap(half_b, "dp", 1)

    vecs = jnp.stack([out_b, gain_mlp, bias_mlp, down_b]).astype(F32)
    norms = jnp.stack([scale_norm, shift_norm]).astype(F32)
    part = project(near, far, out_w, far_a)
    mid, normed_two, act, slope = expand(
        info, rows2d, vecs, part, swap(part, "mp", 1), up_w, up_b[None].astype(F32), far_a, items, hw
    )
    act, rest_b, far_cot = join(act, rest_b, far_cot)
    far_b = put_half(half_b, rest_b, side)
    part = contract(act, down_w, far_b)
    low, z, sums = convolve(info, vecs, mid, part, swap(part, "mp", 1), pack_b, far_b, cot_rows, far_cot, items, seq)
    sums = sums + swap(sums, "mp", 1)
    vol_near, vol_far, dz, grad, norm_sums = norm_back(
        info, norms, sums, swap(sums, "mp", 2), z, pack_b, far_b, cot_rows, far_cot, items, seq
    )
    grad_got = swap(grad, "mp", 1)
    conv_own, conv_far = grads("conv_grad", [dz], [low])
    grad_got, conv_own, conv_far = join(grad_got, conv_own, conv_far)
    conv_got = swap(conv_far, "mp", 2)
    low_grad, du, back, low_sums, up_sums = mlp_back(grad, grad_got, slope, up_w, down_w, far_a, far_b, hw)
    low_grad, back, conv_got = join(low_grad, back, conv_got)
    back_got = swap(back, "mp", 1)
    down_own, down_far = grads("down_grad", [act], [low_grad])
    back_got, down_own, down_far = join(back_got, down_own, down_far)
    do_near, do_far, em, dmid, vec_sums = mid_back(info, vecs, mid, grad, grad_got, back, back_got, out_w, far_a, items)
    do_got = swap(do_far, "mp", 2)
    mixture = jnp.stack([near, far])
    up_own, up_far = grads("up_grad", [normed_two, mixture], [du, em])
    do_got, down_far, up_own, up_far = join(do_got, down_far, up_own, up_far)
    down_got = swap(down_far, "mp", 2)

    qkv_grad, sent, kept, passed, own_sums = attend_back(
        info, rows2d, normed, q, k, v, lse, query_w, key_w, value_w, vec_sums, low_sums, do_near, do_got, items, seq, share
    )
    qkv_grad, sent, down_got, up_far, vol_far = join(qkv_grad, sent, down_got, up_far, vol_far)
    down_total = sum_dp(jnp.concatenate([add_low(down_own, down_got), add_low(conv_own, conv_got)], axis=0))
    qkv_total = sum_dp(qkv_grad)
    up_total = sum_dp(add_low(up_own, swap(up_far, "mp", 2)))
    got = swap(sent, "mp", 1).astype(F32)
    whole = lax.reduce_precision(own_sums[8 : 8 + VECTORS], 8, 7)
    whole = lax.reduce_precision(whole + got[2 * share : 2 * share + VECTORS], 8, 7)
    lines = [passed + got[share : 2 * share], whole, up_sums[1, 0:1], jnp.zeros((1, width), F32)]
    second = swap(jnp.concatenate(lines, axis=0).astype(BF16), "mp", 2).astype(F32)
    normed_grad = kept + got[:share] + second[:share]
    whole = whole + second[share : share + VECTORS]
    up_b_grad = up_sums[0, 0:1] + second[share + VECTORS : share + VECTORS + 1]
    my_tokens = lax.dynamic_slice_in_dim(rows2d, me * share, share, 0).astype(F32)
    my_normal, my_inverse = norm_stats(my_tokens)
    tokens_grad = dmid + norm_backward(normed_grad, my_normal, my_inverse, gain_attn.astype(F32))
    vol_got = swap(vol_far, "mp", 2)
    volume = put_half(vol_near, vol_got, chip).astype(F32)

    lines = jnp.concatenate([whole, up_b_grad, own_sums[2:3], own_sums[4:5], norm_sums[0:1]], axis=0)
    for bit in dp_bits():
        lines = lines + swap(lines, "dp", bit)
    return (
        volume.reshape(items, seq, -1),
        tokens_grad,
        lines[0],
        lines[1],
        qkv_total[:hw].T,
        lines[VECTORS + 1, :hw],
        qkv_total[hw : 2 * hw].T,
        qkv_total[2 * hw :].T,
        lines[VECTORS + 2, :hw],
        up_total[width:],
        lines[4],
        lines[2],
        lines[3],
        up_total[:width],
        lines[VECTORS],
        down_total[:width],
        lines[5],
        down_total[width:].T,
        lines[VECTORS + 3, :CH],
        lines[VECTORS + 3, CH : 2 * CH],
    )


def solution(mesh):
    in_specs = (
        P("dp", None, None),
        P("dp"),
        P(),
        P(),
        P(None, "mp"),
        P("mp"),
        P(None, "mp"),
        P(None, "mp"),
        P("mp"),
        P("mp", None),
        P(),
        P(),
        P(),
        P(None, "mp"),
        P("mp"),
        P("mp", None),
        P(),
        P(None, "mp"),
        P(),
        P(),
        P("dp", None, "mp"),
    )
    out_specs = (
        P("dp", None, "mp"),
        P(("dp", "mp"), None),
        P(),
        P(),
        P(None, "mp"),
        P("mp"),
        P(None, "mp"),
        P(None, "mp"),
        P("mp"),
        P("mp", None),
        P(),
        P(),
        P(),
        P(None, "mp"),
        P("mp"),
        P("mp", None),
        P(),
        P(None, "mp"),
        P(),
        P(),
    )
    return jax.shard_map(shards, mesh=mesh, in_specs=in_specs, out_specs=out_specs, check_vma=False)
```

```python
import functools

import jax
import jax.numpy as jnp
from jax import lax
from jax.experimental import pallas as pl
from jax.experimental.pallas import tpu as pltpu
from jax.sharding import PartitionSpec as P

HEAD_DIM = 64
CH = 128
EPSILON = 1e-05
SCALE = HEAD_DIM ** (-0.5)
F32 = jnp.float32
BF16 = jnp.bfloat16
TILE = 256
PIECE = 128
PAD = 16
VECTORS = 6
OUT_B, GAIN_MLP, BIAS_MLP, DOWN_B, GAIN_ATTN, BIAS_ATTN, UP_B, MIXED = range(8)
COST = 1
VMEM_LIMIT = 56 * 1024 * 1024


def dot(left, right):
    return jnp.dot(left, right, preferred_element_type=F32)


def dot_rows(left, right):
    return lax.dot_general(left, right, (((0,), (0,)), ((), ())), preferred_element_type=F32)


def dot_cols(left, right):
    return lax.dot_general(left, right, (((1,), (1,)), ((), ())), preferred_element_type=F32)


def swap(value, axis, bit):
    size = lax.axis_size(axis)
    return lax.ppermute(value, axis, [(i, i ^ bit) for i in range(size)])


def norm_stats(values):
    center = values - jnp.mean(values, axis=-1, keepdims=True)
    inverse = lax.rsqrt(jnp.mean(center * center, axis=-1, keepdims=True) + EPSILON)
    return center * inverse, inverse


def norm_backward(upstream, normal, inverse, gain_vec):
    scaled = upstream * gain_vec
    mean_part = jnp.mean(scaled, axis=-1, keepdims=True)
    mean_cross = jnp.mean(scaled * normal, axis=-1, keepdims=True)
    return inverse * (scaled - mean_part - normal * mean_cross)


def vmem():
    return pl.BlockSpec(memory_space=pltpu.VMEM)


def anywhere():
    return pl.BlockSpec(memory_space=pl.ANY)


def row(index):
    return slice(index, index + 1)


def smem():
    return pl.BlockSpec(memory_space=pltpu.SMEM)


def shape(dims, dtype):
    return jax.ShapeDtypeStruct(dims, dtype)


def join(*values):
    return lax.optimization_barrier(values)


def params(name, flops, moved):
    return dict(
        compiler_params=pltpu.CompilerParams(vmem_limit_bytes=VMEM_LIMIT),
        cost_estimate=pl.CostEstimate(flops=flops // COST, transcendentals=0, bytes_accessed=moved // COST),
        name=name,
    )


def head_cols(head):
    return slice(head * HEAD_DIM, (head + 1) * HEAD_DIM)


def tiles(width):
    return [slice(start, start + TILE) for start in range(0, width, TILE)]


def chip_half():
    return lax.axis_index("mp") // 2


def x_side():
    return lax.axis_index("dp") % 2


def attend_kernel(
    items, heads, span_rows, info_ref, tok_ref, vec_ref, qw_ref, kw_ref, vw_ref,
    normed_ref, q_ref, k_ref, v_ref, lse_ref, near_ref, other_ref, o_ref
):
    seq = tok_ref.shape[0]
    item = pl.program_id(0)
    length = info_ref[item]
    for start in range(0, seq, PIECE):
        rows = slice(start, start + PIECE)
        normal, unused = norm_stats(tok_ref[rows, :].astype(F32))
        normed_ref[rows, :] = (normal * vec_ref[row(GAIN_ATTN), :] + vec_ref[row(BIAS_ATTN), :]).astype(BF16)
    normed = normed_ref[...]
    hw = q_ref.shape[1]
    q_ref[...] = (dot_cols(normed, qw_ref[...]) + vec_ref[row(MIXED), :hw]).astype(BF16) * jnp.asarray(SCALE, BF16)
    k_ref[...] = dot_cols(normed, kw_ref[...]).astype(BF16)
    v_ref[...] = (dot_cols(normed, vw_ref[...]) + vec_ref[row(MIXED), hw : 2 * hw]).astype(BF16)

    def run(span):
        valid = lax.broadcasted_iota(jnp.int32, (span, span), 0) < length
        for head in range(heads):
            cols = head_cols(head)
            scores = jnp.where(valid, dot_cols(k_ref[:span, cols], q_ref[:span, cols]), -1e9)
            top = jnp.max(scores, axis=0, keepdims=True)
            raised = jnp.exp(scores - top)
            total = jnp.sum(raised, axis=0, keepdims=True)
            mixed = dot_rows(v_ref[:span, cols], raised.astype(BF16)) / total
            o_ref[pl.ds(pl.multiple_of(item * seq, seq), span), cols] = mixed.T.astype(BF16)
            lse_ref[0, head : head + 1, :span] = top + jnp.log(total)
        if span < seq:
            o_ref[pl.ds(pl.multiple_of(item * seq + span, span), seq - span), :] = jnp.zeros(
                (seq - span, heads * HEAD_DIM), BF16
            )

    half = seq // 2

    @pl.when(length <= half)
    def _():
        run(half)

    @pl.when(length > half)
    def _():
        run(seq)

    @pl.when(item == items - 1)
    def _():
        start = chip_half() * span_rows
        near_ref[...] = o_ref[pl.ds(pl.multiple_of(start, PIECE), span_rows), :]
        other_ref[...] = o_ref[pl.ds(pl.multiple_of(span_rows - start, PIECE), span_rows), :]


def attend(info, rows2d, vecs, query_w, key_w, value_w, items, seq):
    rows, width = rows2d.shape
    hw = query_w.shape[0]
    heads = hw // HEAD_DIM
    row_block = lambda cols: pl.BlockSpec((seq, cols), lambda i, n: (i, 0))
    whole = lambda dims: pl.BlockSpec(dims, lambda i, n: (0,) * len(dims))
    return pl.pallas_call(
        functools.partial(attend_kernel, items, heads, rows // 2),
        out_shape=[shape((rows, width), BF16)]
        + [shape((rows, hw), BF16)] * 3
        + [shape((items, 8, seq), F32)]
        + [shape((rows // 2, hw), BF16)] * 2,
        grid_spec=pltpu.PrefetchScalarGridSpec(
            num_scalar_prefetch=1,
            grid=(items,),
            in_specs=[row_block(width), whole(vecs.shape)] + [whole((hw, width))] * 3,
            out_specs=[row_block(width)]
            + [row_block(hw)] * 3
            + [pl.BlockSpec((1, 8, seq), lambda i, n: (i, 0, 0))]
            + [whole((rows // 2, hw))] * 2,
            scratch_shapes=[pltpu.VMEM((rows, hw), BF16)],
        ),
        **params("attend", 6 * rows * width * hw + 4 * rows * seq * hw, 4 * rows * width),
    )(info, rows2d, vecs, query_w, key_w, value_w)


def attend_back_kernel(
    items, heads, share, len_ref, normed_ref, q_ref, k_ref, v_ref, lse_ref, near_ref, other_ref,
    dq_ref, dk_ref, dv_ref, grad_ref, sums_ref, do_ref, grad_acc
):
    seq = normed_ref.shape[0]
    hw = heads * HEAD_DIM
    item = pl.program_id(0)
    length = len_ref[item]

    @pl.when(item == 0)
    def _():
        begin = chip_half() * 2 * share
        do_ref[pl.ds(pl.multiple_of(begin, PIECE), 2 * share), :] = near_ref[...]
        do_ref[pl.ds(pl.multiple_of(2 * share - begin, PIECE), 2 * share), :] = other_ref[...]
        sums_ref[...] = jnp.zeros_like(sums_ref)
        grad_acc[...] = jnp.zeros_like(grad_acc)

    def run(span):
        valid = lax.broadcasted_iota(jnp.int32, (span, span), 0) < length
        for head in range(heads):
            cols = head_cols(head)
            query, keys, vals = q_ref[:span, cols], k_ref[:span, cols], v_ref[:span, cols]
            upstream = do_ref[pl.ds(pl.multiple_of(item * seq, seq), span), cols]
            scores = jnp.where(valid, dot_cols(keys, query), -1e9)
            prob = jnp.exp(scores - lse_ref[0, head : head + 1, :span])
            dv_ref[:span, cols] = dot(prob.astype(BF16), upstream).astype(BF16)
            prob_grad = dot_cols(vals, upstream)
            product = prob * prob_grad
            row_term = jnp.sum(product, axis=0, keepdims=True)
            score_grad = (product - prob * row_term).astype(BF16)
            dk_ref[:span, cols] = dot(score_grad, query).astype(BF16)
            dq_ref[:span, cols] = (dot_rows(keys, score_grad) * SCALE).T.astype(BF16)
        for index, ref in enumerate((dq_ref, dk_ref, dv_ref)):
            grad_acc[index * hw : (index + 1) * hw, :] += dot_rows(ref[:span, :], normed_ref[:span, :])
            if index != 1:
                sums_ref[row(index), :hw] += jnp.sum(ref[:span, :].astype(F32), axis=0, keepdims=True)
            if span < seq:
                ref[span:, :] = jnp.zeros((seq - span, hw), BF16)

    half = seq // 2

    @pl.when(length <= half)
    def _():
        run(half)

    @pl.when(length > half)
    def _():
        run(seq)

    @pl.when(item == items - 1)
    def _():
        grad_ref[...] = grad_acc[...].astype(BF16)


def attend_back(lengths, normed, q, k, v, lse, near, other, items, seq, share):
    rows, width = normed.shape
    hw = q.shape[1]
    heads = hw // HEAD_DIM
    row_block = lambda cols: pl.BlockSpec((seq, cols), lambda i, n: (i, 0))
    whole = lambda dims: pl.BlockSpec(dims, lambda i, n: (0,) * len(dims))
    return pl.pallas_call(
        functools.partial(attend_back_kernel, items, heads, share),
        out_shape=[shape((rows, hw), BF16)] * 3 + [shape((3 * hw, width), BF16), shape((8, width), F32)],
        grid_spec=pltpu.PrefetchScalarGridSpec(
            num_scalar_prefetch=1,
            grid=(items,),
            in_specs=[row_block(width)]
            + [row_block(hw)] * 3
            + [pl.BlockSpec((1, 8, seq), lambda i, n: (i, 0, 0))]
            + [whole((2 * share, hw))] * 2,
            out_specs=[row_block(hw)] * 3 + [whole((3 * hw, width)), whole((8, width))],
            scratch_shapes=[pltpu.VMEM((rows, hw), BF16), pltpu.VMEM((3 * hw, width), F32)],
        ),
        **params("attend_back", 6 * rows * width * hw + 10 * rows * seq * hw, 8 * rows * width),
    )(lengths, normed, q, k, v, lse, near, other)


def normed_back_kernel(
    items, share, len_ref, tok_ref, dq_ref, dk_ref, dv_ref, qw_ref, kw_ref, vw_ref, vec_in, low_in,
    send_ref, keep_ref, pass_ref, sums_ref, part_ref
):
    seq = tok_ref.shape[0]
    item = pl.program_id(0)
    length = len_ref[item]
    me = lax.axis_index("mp")

    @pl.when(item == 0)
    def _():
        sums_ref[...] = jnp.zeros_like(sums_ref)

    def run(span):
        start = pl.multiple_of(item * seq, seq)
        for base in range(0, span, PIECE):
            rows = slice(base, base + PIECE)
            piece = dot(dq_ref[rows, :], qw_ref[...]) + dot(dk_ref[rows, :], kw_ref[...]) + dot(dv_ref[rows, :], vw_ref[...])
            part_ref[pl.ds(pl.multiple_of(start + base, PIECE), PIECE), :] = piece
            normal, unused = norm_stats(tok_ref[rows, :].astype(F32))
            sums_ref[row(0), :] += jnp.sum(piece * normal, axis=0, keepdims=True)
            sums_ref[row(1), :] += jnp.sum(piece, axis=0, keepdims=True)
        if span < seq:
            part_ref[pl.ds(pl.multiple_of(start + span, span), seq - span), :] = jnp.zeros(
                (seq - span, part_ref.shape[1]), F32
            )

    half = seq // 2

    @pl.when(length <= half)
    def _():
        run(half)

    @pl.when(length > half)
    def _():
        run(seq)

    @pl.when(item == items - 1)
    def _():
        def block(k):
            return part_ref[pl.ds(pl.multiple_of((me ^ k) * share, PIECE), share), :]

        keep_ref[...] = block(0)
        pass_ref[...] = block(2)
        send_ref[:share, :] = block(1).astype(BF16)
        send_ref[share : 2 * share, :] = block(3).astype(BF16)
        sums_ref[2:5, :] = 0.5 * vec_in[0:3, :]
        sums_ref[5:6, :] = 0.5 * low_in[0:1, :]
        vectors = sums_ref[0:VECTORS, :]
        send_ref[2 * share :, :] = jnp.concatenate(
            [vectors, jnp.zeros((PAD - VECTORS, vectors.shape[1]), F32)], axis=0
        ).astype(BF16)


def normed_back(lengths, rows2d, dq, dk, dv, query_w, key_w, value_w, vec_in, low_in, items, seq, share):
    rows, width = rows2d.shape
    hw = query_w.shape[0]
    row_block = lambda cols: pl.BlockSpec((seq, cols), lambda i, n: (i, 0))
    whole = lambda dims: pl.BlockSpec(dims, lambda i, n: (0,) * len(dims))
    return pl.pallas_call(
        functools.partial(normed_back_kernel, items, share),
        out_shape=[
            shape((2 * share + PAD, width), BF16),
            shape((share, width), F32),
            shape((share, width), F32),
            shape((8, width), F32),
        ],
        grid_spec=pltpu.PrefetchScalarGridSpec(
            num_scalar_prefetch=1,
            grid=(items,),
            in_specs=[row_block(width)]
            + [row_block(hw)] * 3
            + [whole((hw, width))] * 3
            + [whole(vec_in.shape), whole(low_in.shape)],
            out_specs=[
                whole((2 * share + PAD, width)),
                whole((share, width)),
                whole((share, width)),
                whole((8, width)),
            ],
            scratch_shapes=[pltpu.VMEM((rows, width), F32)],
        ),
        **params("normed_back", 6 * rows * width * hw, 8 * rows * width),
    )(lengths, rows2d, dq, dk, dv, query_w, key_w, value_w, vec_in, low_in)


def load_all(pairs, sems):
    copies = [pltpu.make_async_copy(source, target, sems.at[i]) for i, (source, target) in enumerate(pairs)]
    for copy in copies:
        copy.start()
    return copies


def halves(count):
    return [slice(start, start + count // 2) for start in range(0, count, count // 2)]


def project_kernel(near_ref, far_ref, own_ref, pack_ref, out_ref):
    hw = own_ref.shape[0]
    for cols in tiles(out_ref.shape[1]):
        out_ref[:, cols] = (dot(near_ref[...], own_ref[:, cols]) + dot(far_ref[...], pack_ref[:hw, cols])).astype(BF16)


def project(near, far, own, pack):
    span, hw = near.shape
    width = own.shape[1]
    return pl.pallas_call(
        project_kernel,
        out_shape=shape((span, width), BF16),
        in_specs=[vmem()] * 4,
        out_specs=vmem(),
        **params("project", 4 * span * width * hw, 4 * span * width),
    )(near, far, own, pack)


def up_pairs(up_ref, up_parts, wu):
    part = up_ref.shape[0] // 4
    side = x_side()
    pairs = [(up_ref, wu.at[0])]
    for index, piece in enumerate(up_parts):
        half = side if index < 2 else 1 - side
        start = half * 2 * part + index % 2 * part
        pairs.append((piece, wu.at[1, pl.ds(pl.multiple_of(start, 64), part), :]))
    return pairs


def down_pairs(down_ref, down_parts, wd):
    part = down_parts[0].shape[0]
    side = x_side()
    rest = down_ref.shape[0] - 2 * part
    return [
        (down_ref, wd.at[0]),
        (down_parts[0], wd.at[1, pl.ds(pl.multiple_of(side * part, PIECE), part), :]),
        (down_parts[1], wd.at[1, pl.ds(pl.multiple_of((1 - side) * part, PIECE), part), :]),
        (down_parts[2].at[pl.ds(0, rest), :], wd.at[1, pl.ds(2 * part, rest), :]),
    ]


def conv_pairs(conv_ref, last_part, wc):
    block = wc.shape[1]
    return [(conv_ref, wc.at[0]), (last_part.at[pl.ds(last_part.shape[0] - block, block), :], wc.at[1])]


def cot_pairs(cot_ref, far_cot, cots):
    span = cots.shape[1]
    start = pl.multiple_of(chip_half() * span, PIECE)
    return [(cot_ref.at[pl.ds(start, span), :], cots.at[0]), (far_cot, cots.at[1])]


def expand_kernel(tok_ref, vec_ref, part_ref, other_ref, out_far, up_ref, *rest):
    up_parts = rest[:4]
    mid_ref, normed_ref, act_ref, slope_ref, wu, tok_buf, sems = rest[4:]
    span, width = mid_ref.shape
    start = pl.multiple_of(chip_half() * span, PIECE)
    copies = load_all([(tok_ref.at[pl.ds(start, span), :], tok_buf)] + up_pairs(up_ref, up_parts, wu), sems)
    copies[0].wait()
    for base in range(0, span, PIECE):
        rows = slice(base, base + PIECE)
        mid = tok_buf[rows, :].astype(F32) + vec_ref[row(OUT_B), :] + part_ref[rows, :].astype(F32) + other_ref[rows, :].astype(F32)
        mid_ref[rows, :] = mid
        normal, unused = norm_stats(mid)
        normed_ref[rows, :] = (normal * vec_ref[row(GAIN_MLP), :] + vec_ref[row(BIAS_MLP), :]).astype(BF16)
    for copy in copies[1:]:
        copy.wait()
    hw = out_far.shape[0] - PAD

    def body(step, carry):
        block = step % 2
        rows = pl.ds(pl.multiple_of(step // 2 * (span // 2), PIECE), span // 2)
        for cols in tiles(width):
            own_bias, other_bias = vec_ref[row(UP_B), cols], out_far[hw:, cols].astype(F32)[0:1]
            preact = dot(normed_ref[rows, :], wu[block, :, cols]) + jnp.where(block == 0, own_bias, other_bias)
            normal_cdf = 0.5 * lax.erf(preact * (0.5**0.5)) + 0.5
            density = jnp.exp(preact * preact * -0.5) * 0.3989422804014327
            act_ref[block, rows, cols] = (preact * normal_cdf).astype(BF16)
            slope_ref[block, rows, cols] = (normal_cdf + preact * density).astype(BF16)
        return carry

    lax.fori_loop(0, 4, body, 0)


def expand(rows2d, vecs, part, other, out_far, up_w, up_parts):
    span, width = part.shape
    return pl.pallas_call(
        expand_kernel,
        out_shape=[
            shape((span, width), F32),
            shape((span, width), BF16),
            shape((2, span, width), BF16),
            shape((2, span, width), BF16),
        ],
        in_specs=[anywhere()] + [vmem()] * 4 + [anywhere()] * 5,
        out_specs=[vmem()] * 4,
        scratch_shapes=[
            pltpu.VMEM((2, width, width), BF16),
            pltpu.VMEM((span, width), BF16),
            pltpu.SemaphoreType.DMA((6,)),
        ],
        **params("expand", 4 * span * width * width, 14 * width * width),
    )(rows2d, vecs, part, other, out_far, up_w, *up_parts)


def contract_kernel(act_ref, down_ref, *rest):
    down_parts = rest[:3]
    out_ref, wd, sems = rest[3:]
    for copy in load_all(down_pairs(down_ref, down_parts, wd), sems):
        copy.wait()
    for cols in tiles(out_ref.shape[1]):
        out_ref[:, cols] = (dot(act_ref[0], wd[0, :, cols]) + dot(act_ref[1], wd[1, :, cols])).astype(BF16)


def contract(act, down_w, down_parts):
    unused, span, width = act.shape
    return pl.pallas_call(
        contract_kernel,
        out_shape=shape((span, width), BF16),
        in_specs=[vmem()] + [anywhere()] * 4,
        out_specs=vmem(),
        scratch_shapes=[pltpu.VMEM((2, width, width), BF16), pltpu.SemaphoreType.DMA((4,))],
        **params("contract", 4 * span * width * width, 8 * width * width),
    )(act, down_w, *down_parts)


def piece_place(info_ref, items, seq, span, index):
    piece = chip_half() * (span // PIECE) + index
    per_item = seq // PIECE
    item = piece // per_item
    length = info_ref[item]
    slot = lax.broadcasted_iota(jnp.int32, (PIECE, 1), 0) + (piece % per_item) * PIECE
    return item, length, (slot < length).astype(F32)


def convolve_kernel(items, seq, info_ref, vec_ref, mid_ref, part_ref, other_ref, conv_ref, pack_ref, cot_ref, far_cot, *rest):
    low_ref, z_ref, sums_ref, wc, cots, sems = rest
    span, width = mid_ref.shape
    block = wc.shape[1]
    copies = load_all(conv_pairs(conv_ref, pack_ref, wc) + cot_pairs(cot_ref, far_cot, cots), sems)
    low_ref[...] = (
        mid_ref[...] + vec_ref[row(DOWN_B), :] + part_ref[...].astype(F32) + other_ref[...].astype(F32)
    ).astype(BF16)
    for copy in copies:
        copy.wait()
    sums_ref[...] = jnp.zeros_like(sums_ref)
    for k in range(2):
        z_ref[k] = dot_cols(low_ref[...], wc[k])
        for index in range(span // PIECE):
            rows = slice(index * PIECE, (index + 1) * PIECE)
            item, unused, mask = piece_place(info_ref, items, seq, span, index)
            z = z_ref[k, rows, :]
            masked = z * mask
            upstream = cots[k, rows, :].astype(F32) * mask
            lines = [
                jnp.sum(part, axis=0, keepdims=True) for part in (masked, masked * z, upstream, upstream * z)
            ]
            total = jnp.concatenate(lines, axis=0)
            for base in range(0, block, CH):
                sums_ref[item] += total[:, base : base + CH]


def convolve(info, vecs, mid, part, other, conv_w, last_part, cot_rows, far_cot, items, seq):
    span, width = mid.shape
    block = cot_rows.shape[1]
    return pl.pallas_call(
        functools.partial(convolve_kernel, items, seq),
        out_shape=[shape((span, width), BF16), shape((2, span, block), F32), shape((items, 4, CH), F32)],
        in_specs=[smem()] + [vmem()] * 4 + [anywhere()] * 4,
        out_specs=[vmem()] * 3,
        scratch_shapes=[
            pltpu.VMEM((2, block, width), BF16),
            pltpu.VMEM((2, span, block), BF16),
            pltpu.SemaphoreType.DMA((4,)),
        ],
        **params("convolve", 4 * span * width * block, 14 * width * width),
    )(info, vecs, mid, part, other, conv_w, last_part, cot_rows, far_cot)


def norm_back_kernel(items, seq, norm_at, info_ref, norm_ref, tot_ref, got_ref, z_ref, conv_ref, pack_ref, cot_ref, far_cot, *rest):
    near_ref, far_ref, dz_ref, out_ref, sums_ref, wc, cots, sems = rest
    span, width = out_ref.shape
    block = z_ref.shape[2]
    copies = load_all(conv_pairs(conv_ref, pack_ref, wc) + cot_pairs(cot_ref, far_cot, cots), sems)
    scale = norm_ref[row(MIXED), norm_at : norm_at + CH]
    shift = norm_ref[row(MIXED), norm_at + CH : norm_at + 2 * CH]

    def item_terms(item, length):
        count = (8 * length).astype(F32)
        total = tot_ref[item] + got_ref[item]
        center = total[0:1] / count
        spread = lax.rsqrt(total[1:2] / count - center * center + EPSILON)
        plain = total[2:3]
        cross = spread * (total[3:4] - center * plain)
        return count, center, spread, plain, cross

    sums_ref[...] = jnp.zeros_like(sums_ref)
    for item in range(items):
        unused, unused, unused, plain, cross = item_terms(item, info_ref[item])
        sums_ref[0:1, :CH] += cross
        sums_ref[0:1, CH : 2 * CH] += plain
    for copy in copies:
        copy.wait()
    for index in range(span // PIECE):
        rows = slice(index * PIECE, (index + 1) * PIECE)
        item, length, mask = piece_place(info_ref, items, seq, span, index)
        count, center, spread, plain, cross = item_terms(item, length)
        terms = [center, spread, plain / count, cross / count, scale, shift, spread * scale]
        wide = [jnp.concatenate([t] * (block // CH), axis=1) for t in terms]
        center, spread, plain, cross, scale_w, shift_w, factor = wide
        for k, vol_ref in enumerate((near_ref, far_ref)):
            normal = (z_ref[k, rows, :] - center) * spread
            vol_ref[rows, :] = (mask * (scale_w * normal + shift_w)).astype(BF16)
            upstream = cots[k, rows, :].astype(F32)
            dz_ref[k, rows, :] = (mask * factor * (upstream - plain - normal * cross)).astype(BF16)
    for cols in tiles(width):
        out_ref[:, cols] = (dot(dz_ref[0], wc[0, :, cols]) + dot(dz_ref[1], wc[1, :, cols])).astype(BF16)


def norm_back(info, vecs, total, got, z, conv_w, last_part, cot_rows, far_cot, items, seq, norm_at):
    unused, span, block = z.shape
    width = conv_w.shape[1]
    return pl.pallas_call(
        functools.partial(norm_back_kernel, items, seq, norm_at),
        out_shape=[
            shape((span, block), BF16),
            shape((span, block), BF16),
            shape((2, span, block), BF16),
            shape((span, width), BF16),
            shape((8, width), F32),
        ],
        in_specs=[smem()] + [vmem()] * 4 + [anywhere()] * 4,
        out_specs=[vmem()] * 5,
        scratch_shapes=[
            pltpu.VMEM((2, block, width), BF16),
            pltpu.VMEM((2, span, block), BF16),
            pltpu.SemaphoreType.DMA((4,)),
        ],
        **params("norm_back", 4 * span * width * block, 6 * width * width),
    )(info, vecs, total, got, z, conv_w, last_part, cot_rows, far_cot)


def mlp_back_kernel(part_ref, other_ref, slope_ref, up_ref, down_ref, *rest):
    up_parts, down_parts = rest[:4], rest[4:7]
    low_ref, du_ref, out_ref, sums_ref, up_sums, wu, wd, sems = rest[7:]
    span, width = out_ref.shape
    copies = load_all(down_pairs(down_ref, down_parts, wd) + up_pairs(up_ref, up_parts, wu), sems)
    sums_ref[...] = jnp.zeros_like(sums_ref)
    up_sums[...] = jnp.zeros_like(up_sums)
    for rows in halves(span):
        grad = part_ref[rows, :].astype(F32) + other_ref[rows, :].astype(F32)
        low_ref[rows, :] = grad.astype(BF16)
        sums_ref[0:1, :] += jnp.sum(grad, axis=0, keepdims=True)
    for copy in copies[:4]:
        copy.wait()

    def body(step, carry):
        block = step % 2
        rows = pl.ds(pl.multiple_of(step // 2 * (span // 2), PIECE), span // 2)
        for cols in tiles(width):
            grad = dot_cols(low_ref[rows, :], wd[block, cols, :]) * slope_ref[block, rows, cols].astype(F32)
            low = grad.astype(BF16)
            du_ref[block, rows, cols] = low
            up_sums[block, 0:1, cols] += jnp.sum(low.astype(F32), axis=0, keepdims=True)
        return carry

    lax.fori_loop(0, 4, body, 0)
    for copy in copies[4:]:
        copy.wait()
    for cols in tiles(width):
        out_ref[:, cols] = (dot_cols(du_ref[0], wu[0, cols, :]) + dot_cols(du_ref[1], wu[1, cols, :])).astype(BF16)


def mlp_back(part, other, slope, up_w, down_w, up_parts, down_parts):
    span, width = part.shape
    return pl.pallas_call(
        mlp_back_kernel,
        out_shape=[
            shape((span, width), BF16),
            shape((2, span, width), BF16),
            shape((span, width), BF16),
            shape((8, width), F32),
            shape((2, 8, width), F32),
        ],
        in_specs=[vmem()] * 3 + [anywhere()] * 9,
        out_specs=[vmem()] * 5,
        scratch_shapes=[
            pltpu.VMEM((2, width, width), BF16),
            pltpu.VMEM((2, width, width), BF16),
            pltpu.SemaphoreType.DMA((9,)),
        ],
        **params("mlp_back", 8 * span * width * width, 20 * width * width),
    )(part, other, slope, up_w, down_w, *up_parts, *down_parts)


def mid_back_kernel(share, vec_ref, mid_ref, part_ref, other_ref, grad_ref, got_ref, out_w, pack_ref, *rest):
    near_ref, far_ref, em_ref, mine_ref, sums_ref, dmid_ref = rest
    span, width = mid_ref.shape
    sums_ref[...] = jnp.zeros_like(sums_ref)
    for base in range(0, span, PIECE):
        rows = slice(base, base + PIECE)
        normal, inverse = norm_stats(mid_ref[rows, :])
        grad = grad_ref[rows, :].astype(F32) + got_ref[rows, :].astype(F32)
        dmid = part_ref[rows, :].astype(F32) + other_ref[rows, :].astype(F32)
        dmid += norm_backward(grad, normal, inverse, vec_ref[row(GAIN_MLP), :])
        dmid_ref[rows, :] = dmid
        em_ref[rows, :] = dmid.astype(BF16)
        sums_ref[0:1, :] += jnp.sum(grad * normal, axis=0, keepdims=True)
        sums_ref[1:2, :] += jnp.sum(grad, axis=0, keepdims=True)
        sums_ref[2:3, :] += jnp.sum(dmid, axis=0, keepdims=True)
    far_ref[...] = dot_cols(em_ref[...], pack_ref[: out_w.shape[0], :]).astype(BF16)
    near_ref[...] = dot_cols(em_ref[...], out_w[...]).astype(BF16)
    mine_ref[...] = dmid_ref[pl.ds(pl.multiple_of(lax.axis_index("mp") % 2 * share, PIECE), share), :]


def mid_back(vecs, mid, part, other, grad, got, out_w, pack):
    span, width = mid.shape
    hw = out_w.shape[0]
    return pl.pallas_call(
        functools.partial(mid_back_kernel, span // 2),
        out_shape=[
            shape((span, hw), BF16),
            shape((span, hw), BF16),
            shape((span, width), BF16),
            shape((span // 2, width), F32),
            shape((8, width), F32),
        ],
        in_specs=[vmem()] * 8,
        out_specs=[vmem()] * 5,
        scratch_shapes=[pltpu.VMEM((span, width), F32)],
        **params("mid_back", 4 * span * width * hw, 12 * width * width),
    )(vecs, mid, part, other, grad, got, out_w, pack)


def grads_kernel(count, *refs):
    lefts, rights, out_ref = refs[:count], refs[count : 2 * count], refs[2 * count]
    begin = 0
    for left, right in zip(lefts, rights):
        size = left.shape[-1]
        for block in range(2):
            for base in range(0, size, TILE):
                cols = slice(base, min(base + TILE, size))
                lhs = left[block, :, cols] if len(left.shape) == 3 else left[:, cols]
                rhs = right[block] if len(right.shape) == 3 else right[...]
                out_ref[block, begin + base : begin + cols.stop, :] = dot_rows(lhs, rhs).astype(BF16)
        begin += size


def grads(name, lefts, rights):
    span, width = rights[0].shape[-2:]
    size = sum(left.shape[-1] for left in lefts)
    return pl.pallas_call(
        functools.partial(grads_kernel, len(lefts)),
        out_shape=shape((2, size, width), BF16),
        in_specs=[vmem()] * (2 * len(lefts)),
        out_specs=vmem(),
        **params(name, 4 * span * size * width, 8 * size * width),
    )(*lefts, *rights)


def add_low(left, right):
    return (left.astype(F32) + right.astype(F32)).astype(BF16)


def bit_of(axis, bit):
    return (lax.axis_index(axis) // bit) % 2


def take_half(value, high):
    half = value.shape[0] // 2
    return lax.dynamic_slice_in_dim(value, high * half, half, 0)


def put_half(mine, other, high):
    return jnp.concatenate([jnp.where(high > 0, other, mine), jnp.where(high > 0, mine, other)], axis=0)


def late_bits():
    bits = []
    bit = 4
    while bit < lax.axis_size("dp"):
        bits.append(bit)
        bit *= 2
    return bits


LINKS = {"y": ("mp", 2), "x": ("dp", 1), "z": ("dp", 2)}


def send_together(requests):
    results = [None] * len(requests)
    for link, (axis, bit) in LINKS.items():
        picked = [i for i, (where, unused) in enumerate(requests) if where == link]
        if not picked:
            continue
        sent = [requests[i][1] for i in picked]
        got = swap(sent[0] if len(sent) == 1 else jnp.concatenate(sent, axis=0), axis, bit)
        begin = 0
        for i, piece in zip(picked, sent):
            results[i] = got[begin : begin + piece.shape[0]]
            begin += piece.shape[0]
    return results


def reduce_round(moves, extra=()):
    kept, requests = [], []
    for lane, link in moves:
        if link == "y":
            kept.append(lane[0:1])
            requests.append((link, lane[1]))
            continue
        half = lane.shape[1] // 2
        high = bit_of(*LINKS[link])
        kept.append(lax.dynamic_slice_in_dim(lane, high * half, half, 1))
        sent = lax.dynamic_slice_in_dim(lane, (1 - high) * half, half, 1)
        requests.append((link, sent.reshape(-1, lane.shape[2])))
    got = send_together(requests + list(extra))
    lanes = [add_low(keep, piece.reshape(keep.shape)) for keep, piece in zip(kept, got)]
    return lanes, got[len(moves) :]


def finish_start(lanes):
    return jnp.concatenate([lane[0] for lane in lanes], axis=0)


def finish_reduce(current, bit):
    high = bit_of("dp", bit)
    return add_low(take_half(current, high), swap(take_half(current, 1 - high), "dp", bit))


def finish_gather(current, bit):
    return put_half(current, swap(current, "dp", bit), bit_of("dp", bit))


def finish_split(current, sizes):
    pieces, begin = [], 0
    for size in sizes:
        pieces.append(current[begin : begin + size].reshape(1, 1, size, -1))
        begin += size
    return pieces


def gather_round(moves):
    requests = [(link, piece.reshape(-1, piece.shape[-1])) for piece, link in moves]
    got = send_together(requests)
    results = []
    for (piece, link), other in zip(moves, got):
        results.append(both(piece, other.reshape(piece.shape), bit_of(*LINKS[link]), 0 if link == "x" else 1))
    return results


def both(mine, other, high, axis):
    return jnp.concatenate([jnp.where(high > 0, other, mine), jnp.where(high > 0, mine, other)], axis=axis)


def gather_nested(order, piece):
    return piece.reshape(-1, piece.shape[-1]) if order == "xz" else piece.swapaxes(0, 1).reshape(-1, piece.shape[-1])


def shards(
    tokens, lengths, gain_attn, bias_attn, query_w, query_b, key_w, value_w, value_b, out_w, out_b, gain_mlp, bias_mlp,
    up_w, up_b, down_w, down_b, deconv_w, scale_norm, shift_norm, cotangent
):
    items, seq, width = tokens.shape
    rows = items * seq
    me = lax.axis_index("mp")
    share = rows // lax.axis_size("mp")
    span = rows // 2
    hw = query_w.shape[1]
    rows2d = tokens.reshape(rows, width)
    side = bit_of("dp", 1)
    chip = bit_of("mp", 2)
    mixed = jnp.concatenate([query_b, value_b, scale_norm, shift_norm])
    mixed = jnp.pad(mixed, (0, width - mixed.shape[0]))
    vecs = jnp.concatenate([out_b, gain_mlp, bias_mlp, down_b, gain_attn, bias_attn, up_b, mixed])
    vecs = vecs.astype(F32).reshape(8, width)
    weights = [query_w.T, key_w.T, value_w.T]
    conv_w = deconv_w.T

    bias_rows = jnp.broadcast_to(up_b[None, :], (PAD, width))
    out_far = swap(jnp.concatenate([out_w, bias_rows], axis=0), "mp", 2)
    part_rows = width // 4
    up_parts = [
        swap(lax.dynamic_slice_in_dim(up_w, side * 2 * part_rows + i * part_rows, part_rows, 0), "mp", 2) for i in range(2)
    ]

    normed, q, k, v, lse, near, other = attend(lengths, rows2d, vecs, *weights, items, seq)
    out_far, near, other, *up_parts = join(out_far, near, other, *up_parts)
    far = swap(other, "mp", 2)
    there = swap(up_parts[0], "dp", 1)
    far, there, down_w, conv_w, *up_parts = join(far, there, down_w, conv_w, *up_parts)
    up_parts.append(there)
    there = swap(up_parts[1], "dp", 1)
    down_here = swap(take_half(down_w[: width * 2 // 3], side), "mp", 2)

    part = project(near, far, out_w, out_far)
    part, there, down_here, down_w, conv_w = join(part, there, down_here, down_w, conv_w)
    up_parts.append(there)
    down_parts = [down_here, swap(down_here, "dp", 1)]
    down_parts.append(swap(jnp.concatenate([down_w[width * 2 // 3 :], conv_w], axis=0), "mp", 2))
    mid, normed_two, act, slope = expand(rows2d, vecs, part, swap(part, "mp", 1), out_far, up_w, up_parts)
    cot_rows = cotangent.reshape(rows, -1)
    act, cot_rows, *down_parts = join(act, cot_rows, *down_parts)
    far_cot = swap(lax.dynamic_slice_in_dim(cot_rows, (1 - chip) * span, span, 0), "mp", 2)
    part = contract(act, down_w, down_parts)
    part, far_cot = join(part, far_cot)
    low, z, sums = convolve(
        lengths, vecs, mid, part, swap(part, "mp", 1), conv_w, down_parts[2], cot_rows, far_cot, items, seq
    )
    sums = sums + swap(sums, "mp", 1)
    vol_near, vol_far, dz, grad, norm_sums = norm_back(
        lengths, vecs, sums, swap(sums, "mp", 2), z, conv_w, down_parts[2], cot_rows, far_cot, items, seq, 2 * hw
    )
    grad_got = swap(grad, "mp", 1)
    conv = grads("conv_grad", [dz], [low])
    grad_got, conv = join(grad_got, conv)
    (conv,), unused = reduce_round([(conv, "y")])
    low_grad, du, back, low_sums, up_sums = mlp_back(grad, grad_got, slope, up_w, down_w, up_parts, down_parts)
    low_grad, back, conv = join(low_grad, back, conv)
    back_got = swap(back, "mp", 1)
    down = grads("down_grad", [act], [low_grad])
    (conv,), unused = reduce_round([(conv, "x")])
    back_got, down, conv = join(back_got, down, conv)
    cut = width // 3
    lanes = [down[:, i * cut : (i + 1) * cut] for i in range(3)]
    lanes, unused = reduce_round(list(zip(lanes, "yxz")))
    do_near, do_far, em, dmid, vec_sums = mid_back(vecs, mid, grad, grad_got, back, back_got, out_w, out_far)
    do_far, em, *lanes = join(do_far, em, *lanes)
    do_got = swap(do_far, "mp", 2)
    (*lanes, conv), unused = reduce_round(list(zip(lanes + [conv], "xzyz")))
    mixture = jnp.stack([near, far])
    up = grads("up_grad", [normed_two, mixture], [du, em])
    do_got, up, conv, *lanes = join(do_got, up, conv, *lanes)
    cut = up.shape[1] // 3
    up_lanes = [up[:, i * cut : (i + 1) * cut] for i in range(3)]
    lanes, unused = reduce_round(list(zip(lanes + up_lanes, "zyxyxz")))

    *dqkv, qkv_grad, bias_sums = attend_back(lengths, normed, q, k, v, lse, do_near, do_got, items, seq, share)
    qkv_grad, conv, vol_far, *rest = join(qkv_grad, conv, vol_far, *dqkv, *lanes)
    dqkv, lanes = rest[:3], rest[3:]
    lanes, up_lanes = lanes[:3] + [conv], lanes[3:]
    sizes = [lane.shape[1] for lane in lanes]
    first = finish_start(lanes)
    for bit in late_bits():
        first = finish_reduce(first, bit)
    cut = qkv_grad.shape[0] * 4 // 9
    up_lanes += [qkv_grad[None, :cut], qkv_grad[None, cut:]]
    up_lanes, unused = reduce_round(list(zip(up_lanes, "xzyxz")))
    sent, kept, passed, own_sums = normed_back(
        lengths, rows2d, *dqkv, *weights, vec_sums, low_sums, items, seq, share
    )
    vol_got = swap(vol_far, "mp", 2)
    first, sent, vol_got, *up_lanes = join(first, sent, vol_got, *up_lanes)
    for bit in reversed(late_bits()):
        first = finish_gather(first, bit)
    got = swap(sent, "mp", 1)
    up_lanes, unused = reduce_round(list(zip(up_lanes, "zyxzx")))
    first, got, *up_lanes = join(first, got, *up_lanes)
    got = got.astype(F32)
    lanes = gather_round(list(zip(finish_split(first, sizes), "zxxz")))
    up_sizes = [lane.shape[1] for lane in up_lanes]
    last = finish_start(up_lanes)
    for bit in late_bits():
        last = finish_reduce(last, bit)
    whole = lax.reduce_precision(own_sums[:VECTORS], 8, 7)
    whole = lax.reduce_precision(whole + got[2 * share : 2 * share + VECTORS], 8, 7)
    lines = [passed + got[share : 2 * share], whole, up_sums[1, 0:1], jnp.zeros((1, width), F32)]
    second = swap(jnp.concatenate(lines, axis=0).astype(BF16), "mp", 2)
    last, second, *lanes = join(last, second, *lanes)
    second = second.astype(F32)
    lanes = gather_round(list(zip(lanes, "xzzx")))
    for bit in reversed(late_bits()):
        last = finish_gather(last, bit)
    whole = whole + second[share : share + VECTORS]
    up_b_grad = up_sums[0, 0:1] + second[share + VECTORS : share + VECTORS + 1]
    lines = jnp.concatenate([whole, up_b_grad, bias_sums[0:1], bias_sums[2:3], norm_sums[0:1]], axis=0)
    lines = lines + swap(lines, "dp", 1)
    last, lines, *lanes = join(last, lines, *lanes)
    lines = lines + swap(lines, "dp", 2)
    up_lanes = gather_round(list(zip(finish_split(last, up_sizes), "zzxxx")))
    lines, *up_lanes = join(lines, *up_lanes)
    for bit in late_bits():
        lines = lines + swap(lines, "dp", bit)
    up_lanes = gather_round(list(zip(up_lanes, "xxzzz")))
    normed_grad = kept + got[:share] + second[:share]
    my_tokens = lax.dynamic_slice_in_dim(rows2d, me * share, share, 0).astype(F32)
    my_normal, my_inverse = norm_stats(my_tokens)
    tokens_grad = dmid + norm_backward(normed_grad, my_normal, my_inverse, gain_attn.astype(F32))
    volume = put_half(vol_near, vol_got, chip).astype(F32)
    down_total = [gather_nested(order, lane) for order, lane in zip(("xz", "xz", "zx"), lanes)]
    down_total = jnp.concatenate(down_total, axis=0).astype(F32)
    conv_total = gather_nested("xz", lanes[3]).astype(F32)
    totals = [gather_nested(order, lane).astype(F32) for order, lane in zip(("xz", "xz", "zx", "xz", "zx"), up_lanes)]
    up_total = jnp.concatenate(totals[:3], axis=0)
    qkv_total = jnp.concatenate(totals[3:], axis=0)
    return (
        volume.reshape(items, seq, -1),
        tokens_grad,
        lines[0],
        lines[1],
        qkv_total[:hw].T,
        lines[VECTORS + 1, :hw],
        qkv_total[hw : 2 * hw].T,
        qkv_total[2 * hw :].T,
        lines[VECTORS + 2, :hw],
        up_total[width:],
        lines[4],
        lines[2],
        lines[3],
        up_total[:width],
        lines[VECTORS],
        down_total,
        lines[5],
        conv_total.T,
        lines[VECTORS + 3, :CH],
        lines[VECTORS + 3, CH : 2 * CH],
    )


def solution(mesh):
    in_specs = (
        P("dp", None, None),
        P("dp"),
        P(),
        P(),
        P(None, "mp"),
        P("mp"),
        P(None, "mp"),
        P(None, "mp"),
        P("mp"),
        P("mp", None),
        P(),
        P(),
        P(),
        P(None, "mp"),
        P("mp"),
        P("mp", None),
        P(),
        P(None, "mp"),
        P(),
        P(),
        P("dp", None, "mp"),
    )
    out_specs = (
        P("dp", None, "mp"),
        P(("dp", "mp"), None),
        P(),
        P(),
        P(None, "mp"),
        P("mp"),
        P(None, "mp"),
        P(None, "mp"),
        P("mp"),
        P("mp", None),
        P(),
        P(),
        P(),
        P(None, "mp"),
        P("mp"),
        P("mp", None),
        P(),
        P(None, "mp"),
        P(),
        P(),
    )
    return jax.shard_map(shards, mesh=mesh, in_specs=in_specs, out_specs=out_specs, check_vma=False)
```

```python
import functools

import jax
import jax.numpy as jnp
from jax import lax
from jax.experimental import pallas as pl
from jax.experimental.pallas import tpu as pltpu
from jax.sharding import PartitionSpec as P

HEAD_DIM = 64
CH = 128
EPSILON = 1e-05
SCALE = HEAD_DIM ** (-0.5)
F32 = jnp.float32
BF16 = jnp.bfloat16
TILE = 256
PIECE = 128
PAD = 16
VECTORS = 6
OUT_B, GAIN_MLP, BIAS_MLP, DOWN_B, GAIN_ATTN, BIAS_ATTN, UP_B, MIXED = range(8)
COST = 1
MIB = 1024 * 1024


def dot(left, right):
    return jnp.dot(left, right, preferred_element_type=F32)


def dot_rows(left, right):
    return lax.dot_general(left, right, (((0,), (0,)), ((), ())), preferred_element_type=F32)


def dot_cols(left, right):
    return lax.dot_general(left, right, (((1,), (1,)), ((), ())), preferred_element_type=F32)


def swap(value, axis, bit):
    size = lax.axis_size(axis)
    return lax.ppermute(value, axis, [(i, i ^ bit) for i in range(size)])


def norm_stats(values):
    center = values - jnp.mean(values, axis=-1, keepdims=True)
    inverse = lax.rsqrt(jnp.mean(center * center, axis=-1, keepdims=True) + EPSILON)
    return center * inverse, inverse


def norm_backward(upstream, normal, inverse, gain_vec):
    scaled = upstream * gain_vec
    mean_part = jnp.mean(scaled, axis=-1, keepdims=True)
    mean_cross = jnp.mean(scaled * normal, axis=-1, keepdims=True)
    return inverse * (scaled - mean_part - normal * mean_cross)


def vmem():
    return pl.BlockSpec(memory_space=pltpu.VMEM)


def anywhere():
    return pl.BlockSpec(memory_space=pl.ANY)


def row(index):
    return slice(index, index + 1)


def smem():
    return pl.BlockSpec(memory_space=pltpu.SMEM)


def shape(dims, dtype):
    return jax.ShapeDtypeStruct(dims, dtype)


def join(*values):
    return lax.optimization_barrier(values)


def in_hbm(*values):
    return [pltpu.with_memory_space_constraint(value, pltpu.HBM) for value in values]


def params(name, flops, moved, mebibytes=24):
    return dict(
        compiler_params=pltpu.CompilerParams(vmem_limit_bytes=mebibytes * MIB),
        cost_estimate=pl.CostEstimate(flops=flops // COST, transcendentals=0, bytes_accessed=moved // COST),
        name=name,
    )


def head_cols(head):
    return slice(head * HEAD_DIM, (head + 1) * HEAD_DIM)


def tiles(width):
    return [slice(start, start + TILE) for start in range(0, width, TILE)]


def chip_half():
    return lax.axis_index("mp") // 2


def x_side():
    return lax.axis_index("dp") % 2


def attend_kernel(
    items, heads, span_rows, info_ref, tok_ref, vec_ref, qw_ref, kw_ref, vw_ref,
    normed_ref, q_ref, k_ref, v_ref, lse_ref, near_ref, other_ref, o_ref
):
    seq = tok_ref.shape[0]
    item = pl.program_id(0)
    length = info_ref[item]
    for start in range(0, seq, PIECE):
        rows = slice(start, start + PIECE)
        normal, unused = norm_stats(tok_ref[rows, :].astype(F32))
        normed_ref[rows, :] = (normal * vec_ref[row(GAIN_ATTN), :] + vec_ref[row(BIAS_ATTN), :]).astype(BF16)
    normed = normed_ref[...]
    hw = q_ref.shape[1]
    q_ref[...] = (dot_cols(normed, qw_ref[...]) + vec_ref[row(MIXED), :hw]).astype(BF16) * jnp.asarray(SCALE, BF16)
    k_ref[...] = dot_cols(normed, kw_ref[...]).astype(BF16)
    v_ref[...] = (dot_cols(normed, vw_ref[...]) + vec_ref[row(MIXED), hw : 2 * hw]).astype(BF16)

    def run(span):
        valid = lax.broadcasted_iota(jnp.int32, (span, span), 0) < length
        for head in range(heads):
            cols = head_cols(head)
            scores = jnp.where(valid, dot_cols(k_ref[:span, cols], q_ref[:span, cols]), -1e9)
            top = jnp.max(scores, axis=0, keepdims=True)
            raised = jnp.exp(scores - top)
            total = jnp.sum(raised, axis=0, keepdims=True)
            mixed = dot_rows(v_ref[:span, cols], raised.astype(BF16)) / total
            o_ref[pl.ds(pl.multiple_of(item * seq, seq), span), cols] = mixed.T.astype(BF16)
            lse_ref[0, head : head + 1, :span] = top + jnp.log(total)
        if span < seq:
            o_ref[pl.ds(pl.multiple_of(item * seq + span, span), seq - span), :] = jnp.zeros(
                (seq - span, heads * HEAD_DIM), BF16
            )

    half = seq // 2

    @pl.when(length <= half)
    def _():
        run(half)

    @pl.when(length > half)
    def _():
        run(seq)

    @pl.when(item == items - 1)
    def _():
        start = chip_half() * span_rows
        near_ref[...] = o_ref[pl.ds(pl.multiple_of(start, PIECE), span_rows), :]
        other_ref[...] = o_ref[pl.ds(pl.multiple_of(span_rows - start, PIECE), span_rows), :]


def attend(info, rows2d, vecs, query_w, key_w, value_w, items, seq):
    rows, width = rows2d.shape
    hw = query_w.shape[0]
    heads = hw // HEAD_DIM
    row_block = lambda cols: pl.BlockSpec((seq, cols), lambda i, n: (i, 0))
    whole = lambda dims: pl.BlockSpec(dims, lambda i, n: (0,) * len(dims))
    return pl.pallas_call(
        functools.partial(attend_kernel, items, heads, rows // 2),
        out_shape=[pltpu.HBM((rows, width), BF16)]
        + [pltpu.HBM((rows, hw), BF16)] * 3
        + [pltpu.HBM((items, 8, seq), F32)]
        + [shape((rows // 2, hw), BF16)] * 2,
        grid_spec=pltpu.PrefetchScalarGridSpec(
            num_scalar_prefetch=1,
            grid=(items,),
            in_specs=[row_block(width), whole(vecs.shape)] + [whole((hw, width))] * 3,
            out_specs=[row_block(width)]
            + [row_block(hw)] * 3
            + [pl.BlockSpec((1, 8, seq), lambda i, n: (i, 0, 0))]
            + [whole((rows // 2, hw))] * 2,
            scratch_shapes=[pltpu.VMEM((rows, hw), BF16)],
        ),
        **params("attend", 6 * rows * width * hw + 4 * rows * seq * hw, 4 * rows * width),
    )(info, *in_hbm(rows2d, vecs, query_w, key_w, value_w))


def attend_back_kernel(
    items, heads, share, len_ref, normed_ref, q_ref, k_ref, v_ref, lse_ref, near_ref, other_ref,
    dq_ref, dk_ref, dv_ref, grad_ref, sums_ref, do_ref, grad_acc
):
    seq = normed_ref.shape[0]
    hw = heads * HEAD_DIM
    item = pl.program_id(0)
    length = len_ref[item]

    @pl.when(item == 0)
    def _():
        begin = chip_half() * 2 * share
        do_ref[pl.ds(pl.multiple_of(begin, PIECE), 2 * share), :] = near_ref[...]
        do_ref[pl.ds(pl.multiple_of(2 * share - begin, PIECE), 2 * share), :] = other_ref[...]
        sums_ref[...] = jnp.zeros_like(sums_ref)
        grad_acc[...] = jnp.zeros_like(grad_acc)

    def run(span):
        valid = lax.broadcasted_iota(jnp.int32, (span, span), 0) < length
        for head in range(heads):
            cols = head_cols(head)
            query, keys, vals = q_ref[:span, cols], k_ref[:span, cols], v_ref[:span, cols]
            upstream = do_ref[pl.ds(pl.multiple_of(item * seq, seq), span), cols]
            scores = jnp.where(valid, dot_cols(keys, query), -1e9)
            prob = jnp.exp(scores - lse_ref[0, head : head + 1, :span])
            dv_ref[:span, cols] = dot(prob.astype(BF16), upstream).astype(BF16)
            prob_grad = dot_cols(vals, upstream)
            product = prob * prob_grad
            row_term = jnp.sum(product, axis=0, keepdims=True)
            score_grad = (product - prob * row_term).astype(BF16)
            dk_ref[:span, cols] = dot(score_grad, query).astype(BF16)
            dq_ref[:span, cols] = (dot_rows(keys, score_grad) * SCALE).T.astype(BF16)
        for index, ref in enumerate((dq_ref, dk_ref, dv_ref)):
            grad_acc[index * hw : (index + 1) * hw, :] += dot_rows(ref[:span, :], normed_ref[:span, :])
            if index != 1:
                sums_ref[row(index), :hw] += jnp.sum(ref[:span, :].astype(F32), axis=0, keepdims=True)
            if span < seq:
                ref[span:, :] = jnp.zeros((seq - span, hw), BF16)

    half = seq // 2

    @pl.when(length <= half)
    def _():
        run(half)

    @pl.when(length > half)
    def _():
        run(seq)

    @pl.when(item == items - 1)
    def _():
        grad_ref[...] = grad_acc[...].astype(BF16)


def attend_back(lengths, normed, q, k, v, lse, near, other, items, seq, share):
    rows, width = normed.shape
    hw = q.shape[1]
    heads = hw // HEAD_DIM
    row_block = lambda cols: pl.BlockSpec((seq, cols), lambda i, n: (i, 0))
    whole = lambda dims: pl.BlockSpec(dims, lambda i, n: (0,) * len(dims))
    return pl.pallas_call(
        functools.partial(attend_back_kernel, items, heads, share),
        out_shape=[pltpu.HBM((rows, hw), BF16)] * 3 + [shape((3 * hw, width), BF16), shape((8, width), F32)],
        grid_spec=pltpu.PrefetchScalarGridSpec(
            num_scalar_prefetch=1,
            grid=(items,),
            in_specs=[row_block(width)]
            + [row_block(hw)] * 3
            + [pl.BlockSpec((1, 8, seq), lambda i, n: (i, 0, 0))]
            + [whole((2 * share, hw))] * 2,
            out_specs=[row_block(hw)] * 3 + [whole((3 * hw, width)), whole((8, width))],
            scratch_shapes=[pltpu.VMEM((rows, hw), BF16), pltpu.VMEM((3 * hw, width), F32)],
        ),
        **params("attend_back", 6 * rows * width * hw + 10 * rows * seq * hw, 8 * rows * width),
    )(lengths, *in_hbm(normed, q, k, v, lse, near, other))


def normed_back_kernel(
    items, share, len_ref, tok_ref, dq_ref, dk_ref, dv_ref, qw_ref, kw_ref, vw_ref, vec_in, low_in,
    send_ref, keep_ref, pass_ref, sums_ref, part_ref
):
    seq = tok_ref.shape[0]
    item = pl.program_id(0)
    length = len_ref[item]
    me = lax.axis_index("mp")

    @pl.when(item == 0)
    def _():
        sums_ref[...] = jnp.zeros_like(sums_ref)

    def run(span):
        start = pl.multiple_of(item * seq, seq)
        for base in range(0, span, PIECE):
            rows = slice(base, base + PIECE)
            piece = dot(dq_ref[rows, :], qw_ref[...]) + dot(dk_ref[rows, :], kw_ref[...]) + dot(dv_ref[rows, :], vw_ref[...])
            part_ref[pl.ds(pl.multiple_of(start + base, PIECE), PIECE), :] = piece
            normal, unused = norm_stats(tok_ref[rows, :].astype(F32))
            sums_ref[row(0), :] += jnp.sum(piece * normal, axis=0, keepdims=True)
            sums_ref[row(1), :] += jnp.sum(piece, axis=0, keepdims=True)
        if span < seq:
            part_ref[pl.ds(pl.multiple_of(start + span, span), seq - span), :] = jnp.zeros(
                (seq - span, part_ref.shape[1]), F32
            )

    half = seq // 2

    @pl.when(length <= half)
    def _():
        run(half)

    @pl.when(length > half)
    def _():
        run(seq)

    @pl.when(item == items - 1)
    def _():
        def block(k):
            return part_ref[pl.ds(pl.multiple_of((me ^ k) * share, PIECE), share), :]

        keep_ref[...] = block(0)
        pass_ref[...] = block(2)
        send_ref[:share, :] = block(1).astype(BF16)
        send_ref[share : 2 * share, :] = block(3).astype(BF16)
        sums_ref[2:5, :] = 0.5 * vec_in[0:3, :]
        sums_ref[5:6, :] = 0.5 * low_in[0:1, :]
        vectors = sums_ref[0:VECTORS, :]
        send_ref[2 * share :, :] = jnp.concatenate(
            [vectors, jnp.zeros((PAD - VECTORS, vectors.shape[1]), F32)], axis=0
        ).astype(BF16)


def normed_back(lengths, rows2d, dq, dk, dv, query_w, key_w, value_w, vec_in, low_in, items, seq, share):
    rows, width = rows2d.shape
    hw = query_w.shape[0]
    row_block = lambda cols: pl.BlockSpec((seq, cols), lambda i, n: (i, 0))
    whole = lambda dims: pl.BlockSpec(dims, lambda i, n: (0,) * len(dims))
    return pl.pallas_call(
        functools.partial(normed_back_kernel, items, share),
        out_shape=[
            shape((2 * share + PAD, width), BF16),
            shape((share, width), F32),
            shape((share, width), F32),
            shape((8, width), F32),
        ],
        grid_spec=pltpu.PrefetchScalarGridSpec(
            num_scalar_prefetch=1,
            grid=(items,),
            in_specs=[row_block(width)]
            + [row_block(hw)] * 3
            + [whole((hw, width))] * 3
            + [whole(vec_in.shape), whole(low_in.shape)],
            out_specs=[
                whole((2 * share + PAD, width)),
                whole((share, width)),
                whole((share, width)),
                whole((8, width)),
            ],
            scratch_shapes=[pltpu.VMEM((rows, width), F32)],
        ),
        **params("normed_back", 6 * rows * width * hw, 8 * rows * width),
    )(lengths, *in_hbm(rows2d, dq, dk, dv, query_w, key_w, value_w, vec_in, low_in))


def load_all(pairs, sems):
    copies = [pltpu.make_async_copy(source, target, sems.at[i]) for i, (source, target) in enumerate(pairs)]
    for copy in copies:
        copy.start()
    return copies


def halves(count):
    return [slice(start, start + count // 2) for start in range(0, count, count // 2)]


def project_kernel(near_ref, far_ref, own_ref, pack_ref, out_ref):
    hw = own_ref.shape[0]
    for cols in tiles(out_ref.shape[1]):
        out_ref[:, cols] = (dot(near_ref[...], own_ref[:, cols]) + dot(far_ref[...], pack_ref[:hw, cols])).astype(BF16)


def project(near, far, own, pack):
    span, hw = near.shape
    width = own.shape[1]
    return pl.pallas_call(
        project_kernel,
        out_shape=shape((span, width), BF16),
        in_specs=[vmem()] * 4,
        out_specs=vmem(),
        **params("project", 4 * span * width * hw, 4 * span * width),
    )(near, far, *in_hbm(own), pack)


def up_pairs(up_ref, up_parts, wu):
    part = up_ref.shape[0] // 4
    side = x_side()
    pairs = [(up_ref, wu.at[0])]
    for index, piece in enumerate(up_parts):
        half = side if index < 2 else 1 - side
        start = half * 2 * part + index % 2 * part
        pairs.append((piece, wu.at[1, pl.ds(pl.multiple_of(start, 64), part), :]))
    return pairs


def down_pairs(down_ref, down_parts, wd):
    part = down_parts[0].shape[0]
    side = x_side()
    rest = down_ref.shape[0] - 2 * part
    return [
        (down_ref, wd.at[0]),
        (down_parts[0], wd.at[1, pl.ds(pl.multiple_of(side * part, PIECE), part), :]),
        (down_parts[1], wd.at[1, pl.ds(pl.multiple_of((1 - side) * part, PIECE), part), :]),
        (down_parts[2].at[pl.ds(0, rest), :], wd.at[1, pl.ds(2 * part, rest), :]),
    ]


def conv_pairs(conv_ref, last_part, wc):
    block = wc.shape[1]
    return [(conv_ref, wc.at[0]), (last_part.at[pl.ds(last_part.shape[0] - block, block), :], wc.at[1])]


def cot_pairs(cot_ref, far_cot, cots):
    span = cots.shape[1]
    start = pl.multiple_of(chip_half() * span, PIECE)
    return [(cot_ref.at[pl.ds(start, span), :], cots.at[0]), (far_cot, cots.at[1])]


def expand_kernel(tok_ref, vec_ref, part_ref, other_ref, out_far, up_ref, *rest):
    up_parts = rest[:4]
    mid_ref, normed_ref, act_ref, slope_ref, wu, tok_buf, sems = rest[4:]
    span, width = mid_ref.shape
    start = pl.multiple_of(chip_half() * span, PIECE)
    copies = load_all([(tok_ref.at[pl.ds(start, span), :], tok_buf)] + up_pairs(up_ref, up_parts, wu), sems)
    copies[0].wait()
    for base in range(0, span, PIECE):
        rows = slice(base, base + PIECE)
        mid = tok_buf[rows, :].astype(F32) + vec_ref[row(OUT_B), :] + part_ref[rows, :].astype(F32) + other_ref[rows, :].astype(F32)
        mid_ref[rows, :] = mid
        normal, unused = norm_stats(mid)
        normed_ref[rows, :] = (normal * vec_ref[row(GAIN_MLP), :] + vec_ref[row(BIAS_MLP), :]).astype(BF16)
    for copy in copies[1:]:
        copy.wait()
    hw = out_far.shape[0] - PAD

    def body(step, carry):
        block = step % 2
        rows = pl.ds(pl.multiple_of(step // 2 * (span // 2), PIECE), span // 2)
        for cols in tiles(width):
            own_bias, other_bias = vec_ref[row(UP_B), cols], out_far[hw:, cols].astype(F32)[0:1]
            preact = dot(normed_ref[rows, :], wu[block, :, cols]) + jnp.where(block == 0, own_bias, other_bias)
            normal_cdf = 0.5 * lax.erf(preact * (0.5**0.5)) + 0.5
            density = jnp.exp(preact * preact * -0.5) * 0.3989422804014327
            act_ref[block, rows, cols] = (preact * normal_cdf).astype(BF16)
            slope_ref[block, rows, cols] = (normal_cdf + preact * density).astype(BF16)
        return carry

    lax.fori_loop(0, 4, body, 0)


def expand(rows2d, vecs, part, other, out_far, up_w, up_parts):
    span, width = part.shape
    return pl.pallas_call(
        expand_kernel,
        out_shape=[
            shape((span, width), F32),
            shape((span, width), BF16),
            shape((2, span, width), BF16),
            shape((2, span, width), BF16),
        ],
        in_specs=[anywhere()] + [vmem()] * 4 + [anywhere()] * 5,
        out_specs=[vmem()] * 4,
        scratch_shapes=[
            pltpu.VMEM((2, width, width), BF16),
            pltpu.VMEM((span, width), BF16),
            pltpu.SemaphoreType.DMA((6,)),
        ],
        **params("expand", 4 * span * width * width, 14 * width * width),
    )(*in_hbm(rows2d, vecs), part, other, *in_hbm(out_far, up_w, *up_parts))


def contract_kernel(act_ref, down_ref, *rest):
    down_parts = rest[:3]
    out_ref, wd, sems = rest[3:]
    for copy in load_all(down_pairs(down_ref, down_parts, wd), sems):
        copy.wait()
    for cols in tiles(out_ref.shape[1]):
        out_ref[:, cols] = (dot(act_ref[0], wd[0, :, cols]) + dot(act_ref[1], wd[1, :, cols])).astype(BF16)


def contract(act, down_w, down_parts):
    unused, span, width = act.shape
    return pl.pallas_call(
        contract_kernel,
        out_shape=shape((span, width), BF16),
        in_specs=[vmem()] + [anywhere()] * 4,
        out_specs=vmem(),
        scratch_shapes=[pltpu.VMEM((2, width, width), BF16), pltpu.SemaphoreType.DMA((4,))],
        **params("contract", 4 * span * width * width, 8 * width * width),
    )(act, *in_hbm(down_w, *down_parts))


def piece_place(info_ref, items, seq, span, index):
    piece = chip_half() * (span // PIECE) + index
    per_item = seq // PIECE
    item = piece // per_item
    length = info_ref[item]
    slot = lax.broadcasted_iota(jnp.int32, (PIECE, 1), 0) + (piece % per_item) * PIECE
    return item, length, (slot < length).astype(F32)


def convolve_kernel(items, seq, info_ref, vec_ref, mid_ref, part_ref, other_ref, conv_ref, pack_ref, cot_ref, far_cot, *rest):
    low_ref, z_ref, sums_ref, wc, cots, sems = rest
    span, width = mid_ref.shape
    block = wc.shape[1]
    copies = load_all(conv_pairs(conv_ref, pack_ref, wc) + cot_pairs(cot_ref, far_cot, cots), sems)
    low_ref[...] = (
        mid_ref[...] + vec_ref[row(DOWN_B), :] + part_ref[...].astype(F32) + other_ref[...].astype(F32)
    ).astype(BF16)
    for copy in copies:
        copy.wait()
    sums_ref[...] = jnp.zeros_like(sums_ref)
    for k in range(2):
        z_ref[k] = dot_cols(low_ref[...], wc[k])
        for index in range(span // PIECE):
            rows = slice(index * PIECE, (index + 1) * PIECE)
            item, unused, mask = piece_place(info_ref, items, seq, span, index)
            z = z_ref[k, rows, :]
            masked = z * mask
            upstream = cots[k, rows, :].astype(F32) * mask
            lines = [
                jnp.sum(part, axis=0, keepdims=True) for part in (masked, masked * z, upstream, upstream * z)
            ]
            total = jnp.concatenate(lines, axis=0)
            for base in range(0, block, CH):
                sums_ref[item] += total[:, base : base + CH]


def convolve(info, vecs, mid, part, other, conv_w, last_part, cot_rows, far_cot, items, seq):
    span, width = mid.shape
    block = cot_rows.shape[1]
    return pl.pallas_call(
        functools.partial(convolve_kernel, items, seq),
        out_shape=[shape((span, width), BF16), shape((2, span, block), F32), shape((items, 4, CH), F32)],
        in_specs=[smem()] + [vmem()] * 4 + [anywhere()] * 4,
        out_specs=[vmem()] * 3,
        scratch_shapes=[
            pltpu.VMEM((2, block, width), BF16),
            pltpu.VMEM((2, span, block), BF16),
            pltpu.SemaphoreType.DMA((4,)),
        ],
        **params("convolve", 4 * span * width * block, 14 * width * width),
    )(info, *in_hbm(vecs), mid, part, other, *in_hbm(conv_w, last_part, cot_rows, far_cot))


def norm_back_kernel(items, seq, norm_at, info_ref, norm_ref, tot_ref, got_ref, z_ref, conv_ref, pack_ref, cot_ref, far_cot, *rest):
    near_ref, far_ref, dz_ref, out_ref, sums_ref, wc, cots, sems = rest
    span, width = out_ref.shape
    block = z_ref.shape[2]
    copies = load_all(conv_pairs(conv_ref, pack_ref, wc) + cot_pairs(cot_ref, far_cot, cots), sems)
    scale = norm_ref[row(MIXED), norm_at : norm_at + CH]
    shift = norm_ref[row(MIXED), norm_at + CH : norm_at + 2 * CH]

    def item_terms(item, length):
        count = (8 * length).astype(F32)
        total = tot_ref[item] + got_ref[item]
        center = total[0:1] / count
        spread = lax.rsqrt(total[1:2] / count - center * center + EPSILON)
        plain = total[2:3]
        cross = spread * (total[3:4] - center * plain)
        return count, center, spread, plain, cross

    sums_ref[...] = jnp.zeros_like(sums_ref)
    for item in range(items):
        unused, unused, unused, plain, cross = item_terms(item, info_ref[item])
        sums_ref[0:1, :CH] += cross
        sums_ref[0:1, CH : 2 * CH] += plain
    for copy in copies:
        copy.wait()
    for index in range(span // PIECE):
        rows = slice(index * PIECE, (index + 1) * PIECE)
        item, length, mask = piece_place(info_ref, items, seq, span, index)
        count, center, spread, plain, cross = item_terms(item, length)
        terms = [center, spread, plain / count, cross / count, scale, shift, spread * scale]
        wide = [jnp.concatenate([t] * (block // CH), axis=1) for t in terms]
        center, spread, plain, cross, scale_w, shift_w, factor = wide
        for k, vol_ref in enumerate((near_ref, far_ref)):
            normal = (z_ref[k, rows, :] - center) * spread
            vol_ref[rows, :] = (mask * (scale_w * normal + shift_w)).astype(BF16)
            upstream = cots[k, rows, :].astype(F32)
            dz_ref[k, rows, :] = (mask * factor * (upstream - plain - normal * cross)).astype(BF16)
    for cols in tiles(width):
        out_ref[:, cols] = (dot(dz_ref[0], wc[0, :, cols]) + dot(dz_ref[1], wc[1, :, cols])).astype(BF16)


def norm_back(info, vecs, total, got, z, conv_w, last_part, cot_rows, far_cot, items, seq, norm_at):
    unused, span, block = z.shape
    width = conv_w.shape[1]
    return pl.pallas_call(
        functools.partial(norm_back_kernel, items, seq, norm_at),
        out_shape=[
            shape((span, block), BF16),
            shape((span, block), BF16),
            shape((2, span, block), BF16),
            shape((span, width), BF16),
            shape((8, width), F32),
        ],
        in_specs=[smem()] + [vmem()] * 4 + [anywhere()] * 4,
        out_specs=[vmem()] * 5,
        scratch_shapes=[
            pltpu.VMEM((2, block, width), BF16),
            pltpu.VMEM((2, span, block), BF16),
            pltpu.SemaphoreType.DMA((4,)),
        ],
        **params("norm_back", 4 * span * width * block, 6 * width * width),
    )(info, *in_hbm(vecs), total, got, z, *in_hbm(conv_w, last_part, cot_rows, far_cot))


def mlp_back_kernel(part_ref, other_ref, slope_ref, up_ref, down_ref, *rest):
    up_parts, down_parts = rest[:4], rest[4:7]
    low_ref, du_ref, out_ref, sums_ref, up_sums, wu, wd, sems = rest[7:]
    span, width = out_ref.shape
    copies = load_all(down_pairs(down_ref, down_parts, wd) + up_pairs(up_ref, up_parts, wu), sems)
    sums_ref[...] = jnp.zeros_like(sums_ref)
    up_sums[...] = jnp.zeros_like(up_sums)
    for rows in halves(span):
        grad = part_ref[rows, :].astype(F32) + other_ref[rows, :].astype(F32)
        low_ref[rows, :] = grad.astype(BF16)
        sums_ref[0:1, :] += jnp.sum(grad, axis=0, keepdims=True)
    for copy in copies[:4]:
        copy.wait()

    def body(step, carry):
        block = step % 2
        rows = pl.ds(pl.multiple_of(step // 2 * (span // 2), PIECE), span // 2)
        for cols in tiles(width):
            grad = dot_cols(low_ref[rows, :], wd[block, cols, :]) * slope_ref[block, rows, cols].astype(F32)
            low = grad.astype(BF16)
            du_ref[block, rows, cols] = low
            up_sums[block, 0:1, cols] += jnp.sum(low.astype(F32), axis=0, keepdims=True)
        return carry

    lax.fori_loop(0, 4, body, 0)
    for copy in copies[4:]:
        copy.wait()
    for cols in tiles(width):
        out_ref[:, cols] = (dot_cols(du_ref[0], wu[0, cols, :]) + dot_cols(du_ref[1], wu[1, cols, :])).astype(BF16)


def mlp_back(part, other, slope, up_w, down_w, up_parts, down_parts):
    span, width = part.shape
    return pl.pallas_call(
        mlp_back_kernel,
        out_shape=[
            shape((span, width), BF16),
            shape((2, span, width), BF16),
            shape((span, width), BF16),
            shape((8, width), F32),
            shape((2, 8, width), F32),
        ],
        in_specs=[vmem()] * 3 + [anywhere()] * 9,
        out_specs=[vmem()] * 5,
        scratch_shapes=[
            pltpu.VMEM((2, width, width), BF16),
            pltpu.VMEM((2, width, width), BF16),
            pltpu.SemaphoreType.DMA((9,)),
        ],
        **params("mlp_back", 8 * span * width * width, 20 * width * width),
    )(part, other, slope, *in_hbm(up_w, down_w, *up_parts, *down_parts))


def mid_back_kernel(share, vec_ref, mid_ref, part_ref, other_ref, grad_ref, got_ref, out_w, pack_ref, *rest):
    near_ref, far_ref, em_ref, mine_ref, sums_ref, dmid_ref = rest
    span, width = mid_ref.shape
    sums_ref[...] = jnp.zeros_like(sums_ref)
    for base in range(0, span, PIECE):
        rows = slice(base, base + PIECE)
        normal, inverse = norm_stats(mid_ref[rows, :])
        grad = grad_ref[rows, :].astype(F32) + got_ref[rows, :].astype(F32)
        dmid = part_ref[rows, :].astype(F32) + other_ref[rows, :].astype(F32)
        dmid += norm_backward(grad, normal, inverse, vec_ref[row(GAIN_MLP), :])
        dmid_ref[rows, :] = dmid
        em_ref[rows, :] = dmid.astype(BF16)
        sums_ref[0:1, :] += jnp.sum(grad * normal, axis=0, keepdims=True)
        sums_ref[1:2, :] += jnp.sum(grad, axis=0, keepdims=True)
        sums_ref[2:3, :] += jnp.sum(dmid, axis=0, keepdims=True)
    far_ref[...] = dot_cols(em_ref[...], pack_ref[: out_w.shape[0], :]).astype(BF16)
    near_ref[...] = dot_cols(em_ref[...], out_w[...]).astype(BF16)
    mine_ref[...] = dmid_ref[pl.ds(pl.multiple_of(lax.axis_index("mp") % 2 * share, PIECE), share), :]


def mid_back(vecs, mid, part, other, grad, got, out_w, pack):
    span, width = mid.shape
    hw = out_w.shape[0]
    return pl.pallas_call(
        functools.partial(mid_back_kernel, span // 2),
        out_shape=[
            shape((span, hw), BF16),
            shape((span, hw), BF16),
            shape((span, width), BF16),
            shape((span // 2, width), F32),
            shape((8, width), F32),
        ],
        in_specs=[vmem()] * 8,
        out_specs=[vmem()] * 5,
        scratch_shapes=[pltpu.VMEM((span, width), F32)],
        **params("mid_back", 4 * span * width * hw, 12 * width * width),
    )(*in_hbm(vecs), mid, part, other, grad, got, *in_hbm(out_w, pack))


LINKS = {"y": ("mp", 2), "x": ("dp", 1), "z": ("dp", 2)}


class Lane:
    def __init__(self, blocks, rows, parts, link):
        self.blocks, self.rows, self.parts, self.link = blocks, rows, parts, link


class Kept:
    def __init__(self, blocks, rows, array, link, place):
        self.blocks, self.rows, self.array, self.link, self.place = blocks, rows, array, link, place


def high_of(link):
    axis, bit = LINKS[link]
    return (lax.axis_index(axis) // bit) % 2


def aligned(value, rows):
    return value if isinstance(value, int) else pl.multiple_of(value, rows & -rows)


def up_grad_kernel(normed_ref, near_ref, far_ref, du_ref, em_ref, out_ref):
    width = em_ref.shape[1]
    total = out_ref.shape[0] // 2
    for block, mixed in enumerate((near_ref, far_ref)):
        at = block * total
        for cols in tiles(width):
            out_ref[at + cols.start : at + cols.stop, :] = dot_rows(normed_ref[:, cols], du_ref[block]).astype(BF16)
        out_ref[at + width : at + total, :] = dot_rows(mixed[...], em_ref[...]).astype(BF16)


def up_grad(normed, near, far, du, em):
    span, width = em.shape
    size = width + near.shape[1]
    return pl.pallas_call(
        up_grad_kernel,
        out_shape=shape((2 * size, width), BF16),
        in_specs=[vmem()] * 5,
        out_specs=vmem(),
        **params("up_grad", 4 * span * size * width, 8 * size * width),
    )(normed, near, far, du, em)


def emit_kernel(count, inputs, lanes, links, *refs):
    lefts, rights = refs[:count], refs[count : 2 * count]
    sources = list(refs[2 * count : 2 * count + inputs])
    outs = refs[2 * count + inputs :]
    if count:
        product, outs = outs[-1], outs[:-1]
        sources = [product] + sources
        total = product.shape[0] // 2
        begin = 0
        for left, right in zip(lefts, rights):
            size = left.shape[-1]
            for block in range(2):
                for base in range(0, size, TILE):
                    cols = slice(base, min(base + TILE, size))
                    lhs = left[block, :, cols] if len(left.shape) == 3 else left[:, cols]
                    rhs = right[block] if len(right.shape) == 3 else right[...]
                    at = block * total + begin
                    product[at + base : at + cols.stop, :] = dot_rows(lhs, rhs).astype(BF16)
            begin += size
    sends = dict(zip(links, outs))
    kept = iter(outs[len(links) :])
    last = outs[-1]
    places = dict.fromkeys(list(links) + [None], 0)

    for lane in lanes:

        def total_of(block, start, size):
            values = [
                sources[index][pl.ds(aligned(base + block * stride + start, size), size), :]
                for index, base, stride in lane.parts
            ]
            if len(values) == 1:
                return values[0]
            return (values[0].astype(F32) + values[1].astype(F32)).astype(BF16)

        place = places[lane.link]
        if lane.link is None:
            last[place : place + lane.rows, :] = total_of(0, 0, lane.rows)
            places[None] += lane.rows
            continue
        send, keep = sends[lane.link], next(kept)
        if lane.link == "y":
            send[place : place + lane.rows, :] = total_of(1, 0, lane.rows)
            keep[...] = total_of(0, 0, lane.rows)
            places["y"] += lane.rows
            continue
        half = lane.rows // 2
        high = high_of(lane.link)
        for block in range(lane.blocks):
            rows = slice(block * half, (block + 1) * half)
            keep[rows, :] = total_of(block, high * half, half)
            send[place + rows.start : place + rows.stop, :] = total_of(block, (1 - high) * half, half)
        places[lane.link] += lane.blocks * half


def emit(name, lefts, rights, inputs, lanes, width):
    places = dict.fromkeys(list(LINKS) + [None], 0)
    kept = []
    for lane in lanes:
        sent = lane.blocks * lane.rows // 2 if lane.link else lane.rows
        if lane.link:
            blocks, rows = (1, lane.rows) if lane.link == "y" else (lane.blocks, lane.rows // 2)
            kept.append(Kept(blocks, rows, None, lane.link, places[lane.link]))
        places[lane.link] += sent
    links = [link for link in LINKS if places[link]]
    out_rows = [places[link] for link in links] + [k.blocks * k.rows for k in kept]
    if places[None]:
        out_rows.append(places[None])
    size = sum(left.shape[-1] for left in lefts)
    span = rights[0].shape[-2] if rights else 0
    results = pl.pallas_call(
        functools.partial(emit_kernel, len(lefts), len(inputs), lanes, links),
        out_shape=[shape((rows, width), BF16) for rows in out_rows],
        in_specs=[vmem()] * (2 * len(lefts) + len(inputs)),
        out_specs=[vmem()] * len(out_rows),
        scratch_shapes=[pltpu.VMEM((2 * size, width), BF16)] if lefts else [],
        **params(name, 4 * span * size * width, 8 * size * width),
    )(*lefts, *rights, *inputs)
    for keep, array in zip(kept, results[len(links) :]):
        keep.array = array
    return dict(zip(links, results)), kept, results[-1] if places[None] else None


def send_all(sends):
    return {link: swap(value, *LINKS[link]) for link, value in sends.items()}


def turn(name, kept, got, links, width, fresh=()):
    inputs = [k.array for k in kept] + list(got.values()) + [lane[0] for lane in fresh]
    came = {link: len(kept) + i for i, link in enumerate(got)}
    lanes = []
    for i, (k, link) in enumerate(zip(kept, links)):
        lanes.append(Lane(k.blocks, k.rows, [(i, 0, k.rows), (came[k.link], k.place, k.rows)], link))
    for i, (lane, link) in enumerate(zip(fresh, links[len(kept) :])):
        lanes.append(Lane(lane[3], lane[4], [(len(kept) + len(got) + i, lane[1], lane[2])], link))
    return emit(name, [], [], inputs, lanes, width)


def spread_kernel(lanes, cuts, flip, *refs):
    first, gots, outs, total = refs[0], refs[1:5], refs[5:-1], refs[-1]
    bits = {"x": high_of("x"), "z": high_of("z")}
    places = [0, 0]
    sizes = [sum(lane[1] for lane in lanes if lane[3] == group) for group in range(2)]
    for base, rows, order, group in lanes:
        at = places[group]
        places[group] += rows
        near, far = ("z", "x") if group == 0 else ("x", "z")
        got_near, got_far = gots[2 * group], gots[2 * group + 1]
        offset = at + (sizes[0] if group else 0)
        pieces = [
            (first[offset : offset + rows, :], ()),
            (got_near[at : at + rows, :], (near,)),
            (got_far[at : at + rows, :], (far,)),
            (got_far[sizes[group] + at : sizes[group] + at + rows, :], (near, far)),
        ]
        for value, flipped in pieces:
            index = [1 - bits[link] if link in flipped else bits[link] for link in order]
            start = base + (index[0] * 2 + index[1]) * rows
            total[pl.ds(aligned(start, rows), rows), :] = value.astype(F32)
    begin = 0
    for i, (out, size) in enumerate(zip(outs, cuts)):
        value = total[begin : begin + size, :]
        out[...] = value.T if i in flip else value
        begin += size


def spread(name, lanes, cuts, flip, first, gots):
    width = first.shape[1]
    return pl.pallas_call(
        functools.partial(spread_kernel, lanes, cuts, flip),
        out_shape=[shape((width, size) if i in flip else (size, width), F32) for i, size in enumerate(cuts)],
        in_specs=[vmem()] * 5,
        out_specs=[vmem()] * len(cuts),
        scratch_shapes=[pltpu.VMEM((sum(cuts), width), F32)],
        **params(name, 0, 8 * sum(cuts) * width),
    )(first, *gots)


def add_low(left, right):
    return (left.astype(F32) + right.astype(F32)).astype(BF16)


def bit_of(axis, bit):
    return (lax.axis_index(axis) // bit) % 2


def take_half(value, high):
    half = value.shape[0] // 2
    return lax.dynamic_slice_in_dim(value, high * half, half, 0)


def put_half(mine, other, high):
    return jnp.concatenate([jnp.where(high > 0, other, mine), jnp.where(high > 0, mine, other)], axis=0)


def late_bits():
    bits = []
    bit = 4
    while bit < lax.axis_size("dp"):
        bits.append(bit)
        bit *= 2
    return bits


def finish_reduce(current, bit):
    high = bit_of("dp", bit)
    return add_low(take_half(current, high), swap(take_half(current, 1 - high), "dp", bit))


def finish_gather(current, bit):
    return put_half(current, swap(current, "dp", bit), bit_of("dp", bit))


def shards(
    tokens, lengths, gain_attn, bias_attn, query_w, query_b, key_w, value_w, value_b, out_w, out_b, gain_mlp, bias_mlp,
    up_w, up_b, down_w, down_b, deconv_w, scale_norm, shift_norm, cotangent
):
    items, seq, width = tokens.shape
    rows = items * seq
    me = lax.axis_index("mp")
    share = rows // lax.axis_size("mp")
    span = rows // 2
    hw = query_w.shape[1]
    rows2d = tokens.reshape(rows, width)
    side = bit_of("dp", 1)
    chip = bit_of("mp", 2)
    mixed = jnp.concatenate([query_b, value_b, scale_norm, shift_norm])
    mixed = jnp.pad(mixed, (0, width - mixed.shape[0]))
    vecs = jnp.concatenate([out_b, gain_mlp, bias_mlp, down_b, gain_attn, bias_attn, up_b, mixed])
    vecs = vecs.astype(F32).reshape(8, width)
    weights = [query_w.T, key_w.T, value_w.T]
    conv_w = deconv_w.T

    bias_rows = jnp.broadcast_to(up_b[None, :], (PAD, width))
    out_far = swap(jnp.concatenate([out_w, bias_rows], axis=0), "mp", 2)
    part_rows = width // 4
    up_parts = [
        swap(lax.dynamic_slice_in_dim(up_w, side * 2 * part_rows + i * part_rows, part_rows, 0), "mp", 2) for i in range(2)
    ]

    normed, q, k, v, lse, near, other = attend(lengths, rows2d, vecs, *weights, items, seq)
    out_far, near, other, *up_parts = join(out_far, near, other, *up_parts)
    far = swap(other, "mp", 2)
    there = swap(up_parts[0], "dp", 1)
    far, there, down_w, conv_w, *up_parts = join(far, there, down_w, conv_w, *up_parts)
    up_parts.append(there)
    there = swap(up_parts[1], "dp", 1)
    down_here = swap(take_half(down_w[: width * 2 // 3], side), "mp", 2)

    part = project(near, far, out_w, out_far)
    part, there, down_here, down_w, conv_w = join(part, there, down_here, down_w, conv_w)
    up_parts.append(there)
    down_parts = [down_here, swap(down_here, "dp", 1)]
    down_parts.append(swap(jnp.concatenate([down_w[width * 2 // 3 :], conv_w], axis=0), "mp", 2))
    mid, normed_two, act, slope = expand(rows2d, vecs, part, swap(part, "mp", 1), out_far, up_w, up_parts)
    cot_rows = cotangent.reshape(rows, -1)
    act, cot_rows, *down_parts = join(act, cot_rows, *down_parts)
    far_cot = swap(lax.dynamic_slice_in_dim(cot_rows, (1 - chip) * span, span, 0), "mp", 2)
    part = contract(act, down_w, down_parts)
    part, far_cot = join(part, far_cot)
    low, z, sums = convolve(
        lengths, vecs, mid, part, swap(part, "mp", 1), conv_w, down_parts[2], cot_rows, far_cot, items, seq
    )
    sums = sums + swap(sums, "mp", 1)
    vol_near, vol_far, dz, grad, norm_sums = norm_back(
        lengths, vecs, sums, swap(sums, "mp", 2), z, conv_w, down_parts[2], cot_rows, far_cot, items, seq, 2 * hw
    )
    grad_got = swap(grad, "mp", 1)
    sends, conv, unused = emit("conv_grad", [dz], [low], [], [Lane(2, conv_w.shape[0], [(0, 0, conv_w.shape[0])], "y")], width)
    grad_got, conv[0].array, sends["y"] = join(grad_got, conv[0].array, sends["y"])
    came = send_all(sends)
    low_grad, du, back, low_sums, up_sums = mlp_back(grad, grad_got, slope, up_w, down_w, up_parts, down_parts)
    low_grad, back, came["y"] = join(low_grad, back, came["y"])
    back_got = swap(back, "mp", 1)
    cut = width // 3
    half = conv_w.shape[0] // 2
    lanes = [Lane(2, cut, [(0, i * cut, width)], link) for i, link in enumerate("yxz")]
    lanes += [Lane(1, half, [(1, i * half, 0), (2, i * half, 0)], link) for i, link in enumerate("xz")]
    sends, kept, unused = emit("down_grad", [act], [low_grad], [conv[0].array, came["y"]], lanes, width)
    back_got, sends["y"], sends["x"], sends["z"] = join(back_got, sends["y"], sends["x"], sends["z"])
    came = send_all(sends)
    do_near, do_far, em, dmid, vec_sums = mid_back(vecs, mid, grad, grad_got, back, back_got, out_w, out_far)
    do_far, em, came["y"], came["x"], came["z"] = join(do_far, em, came["y"], came["x"], came["z"])
    do_got = swap(do_far, "mp", 2)
    sends, kept, unused = turn("turn_one", kept, came, "xzyzx", width)
    came = send_all(sends)
    up = up_grad(normed_two, near, far, du, em)
    up, came["y"], came["x"], came["z"] = join(up, came["y"], came["x"], came["z"])
    size = up.shape[0] // 2
    cut = size // 3
    fresh = [(up, i * cut, size, 2, cut) for i in range(3)]
    sends, kept, early = turn("turn_two", kept, came, ["z", "y", "x", None, None, "y", "x", "z"], width, fresh)
    do_got, sends["y"], sends["x"], sends["z"] = join(do_got, sends["y"], sends["x"], sends["z"])
    came = send_all(sends)

    *dqkv, qkv_grad, bias_sums = attend_back(lengths, normed, q, k, v, lse, do_near, do_got, items, seq, share)
    qkv_grad, vol_far, came["y"], came["x"], came["z"], *dqkv = join(
        qkv_grad, vol_far, came["y"], came["x"], came["z"], *dqkv
    )
    cut = qkv_grad.shape[0] * 4 // 9
    fresh = [(qkv_grad, 0, 0, 1, cut), (qkv_grad, cut, 0, 1, qkv_grad.shape[0] - cut)]
    sends, kept, first = turn(
        "turn_three", kept, came, [None, None, None, "x", "z", "y", "x", "z"], width, fresh
    )
    sizes = [first.shape[0] // 3] * 3 + [early.shape[0] // 2] * 2
    first = jnp.concatenate([first[: sizes[0]], early, first[sizes[0] :]], axis=0)
    for bit in late_bits():
        first = finish_reduce(first, bit)
    came = send_all(sends)
    sent, own, passed, own_sums = normed_back(
        lengths, rows2d, *dqkv, *weights, vec_sums, low_sums, items, seq, share
    )
    vol_got = swap(vol_far, "mp", 2)
    first, sent, vol_got, came["y"], came["x"], came["z"] = join(first, sent, vol_got, came["y"], came["x"], came["z"])
    for bit in reversed(late_bits()):
        first = finish_gather(first, bit)
    got = swap(sent, "mp", 1)
    sends, kept, unused = turn("turn_four", kept, came, "zyxzx", width)
    came = send_all(sends)
    first, got, came["y"], came["x"], came["z"] = join(first, got, came["y"], came["x"], came["z"])
    got = got.astype(F32)
    unused, unused, last = turn("turn_five", kept, came, [None] * 5, width)
    last_sizes = [k.blocks * k.rows for k in kept]
    for bit in late_bits():
        last = finish_reduce(last, bit)
    edge = sum(sizes[:1] + sizes[3:])
    sent_near = [first[:edge], first[edge:]]
    near_got = [swap(sent_near[0], "dp", 2), swap(sent_near[1], "dp", 1)]
    whole = lax.reduce_precision(own_sums[:VECTORS], 8, 7)
    whole = lax.reduce_precision(whole + got[2 * share : 2 * share + VECTORS], 8, 7)
    lines = [passed + got[share : 2 * share], whole, up_sums[1, 0:1], jnp.zeros((1, width), F32)]
    second = swap(jnp.concatenate(lines, axis=0).astype(BF16), "mp", 2)
    last, second, *near_got = join(last, second, *near_got)
    second = second.astype(F32)
    far_got = [
        swap(jnp.concatenate([sent_near[0], near_got[0]], axis=0), "dp", 1),
        swap(jnp.concatenate([sent_near[1], near_got[1]], axis=0), "dp", 2),
    ]
    for bit in reversed(late_bits()):
        last = finish_gather(last, bit)
    whole = whole + second[share : share + VECTORS]
    up_b_grad = up_sums[0, 0:1] + second[share + VECTORS : share + VECTORS + 1]
    lines = jnp.concatenate([whole, up_b_grad, bias_sums[0:1], bias_sums[2:3], norm_sums[0:1]], axis=0)
    lines = lines + swap(lines, "dp", 1)
    last, lines, *far_got = join(last, lines, *far_got)
    edge = sum(last_sizes[:2])
    sent_last = [last[:edge], last[edge:]]
    last_got = [swap(sent_last[0], "dp", 2), swap(sent_last[1], "dp", 1)]
    lines = lines + swap(lines, "dp", 2)
    third = width // 3
    down_total, conv_total = spread(
        "spread_one",
        [
            (0, sizes[0], "xz", 0),
            (width, sizes[3], "xz", 0),
            (width + half, sizes[4], "zx", 0),
            (third, sizes[1], "xz", 1),
            (2 * third, sizes[2], "zx", 1),
        ],
        [width, 2 * half],
        [1],
        first,
        [near_got[0], far_got[0], near_got[1], far_got[1]],
    )
    lines, *last_got = join(lines, *last_got)
    for bit in late_bits():
        lines = lines + swap(lines, "dp", bit)
    last_far = [
        swap(jnp.concatenate([sent_last[0], last_got[0]], axis=0), "dp", 1),
        swap(jnp.concatenate([sent_last[1], last_got[1]], axis=0), "dp", 2),
    ]
    base = width + hw
    up_total, out_total, query_total, key_total, value_total = spread(
        "spread_two",
        [
            (0, last_sizes[0], "xz", 0),
            (base // 3, last_sizes[1], "xz", 0),
            (base // 3 * 2, last_sizes[2], "zx", 1),
            (base, last_sizes[3], "xz", 1),
            (base + cut, last_sizes[4], "zx", 1),
        ],
        [width, hw, hw, hw, hw],
        [],
        last,
        [last_got[0], last_far[0], last_got[1], last_far[1]],
    )
    normed_grad = own + got[:share] + second[:share]
    my_tokens = lax.dynamic_slice_in_dim(rows2d, me * share, share, 0).astype(F32)
    my_normal, my_inverse = norm_stats(my_tokens)
    tokens_grad = dmid + norm_backward(normed_grad, my_normal, my_inverse, gain_attn.astype(F32))
    volume = put_half(vol_near, vol_got, chip).astype(F32)
    return (
        volume.reshape(items, seq, -1),
        tokens_grad,
        lines[0],
        lines[1],
        query_total.T,
        lines[VECTORS + 1, :hw],
        key_total.T,
        value_total.T,
        lines[VECTORS + 2, :hw],
        out_total,
        lines[4],
        lines[2],
        lines[3],
        up_total,
        lines[VECTORS],
        down_total,
        lines[5],
        conv_total,
        lines[VECTORS + 3, :CH],
        lines[VECTORS + 3, CH : 2 * CH],
    )


def solution(mesh):
    in_specs = (
        P("dp", None, None),
        P("dp"),
        P(),
        P(),
        P(None, "mp"),
        P("mp"),
        P(None, "mp"),
        P(None, "mp"),
        P("mp"),
        P("mp", None),
        P(),
        P(),
        P(),
        P(None, "mp"),
        P("mp"),
        P("mp", None),
        P(),
        P(None, "mp"),
        P(),
        P(),
        P("dp", None, "mp"),
    )
    out_specs = (
        P("dp", None, "mp"),
        P(("dp", "mp"), None),
        P(),
        P(),
        P(None, "mp"),
        P("mp"),
        P(None, "mp"),
        P(None, "mp"),
        P("mp"),
        P("mp", None),
        P(),
        P(),
        P(),
        P(None, "mp"),
        P("mp"),
        P("mp", None),
        P(),
        P(None, "mp"),
        P(),
        P(),
    )
    return jax.shard_map(shards, mesh=mesh, in_specs=in_specs, out_specs=out_specs, check_vma=False)
```

```python
import functools

import jax
import jax.numpy as jnp
from jax import lax
from jax.experimental import pallas as pl
from jax.experimental.pallas import tpu as pltpu
from jax.sharding import PartitionSpec as P

HEAD_DIM = 64
CH = 128
EPSILON = 1e-05
SCALE = HEAD_DIM ** (-0.5)
F32 = jnp.float32
BF16 = jnp.bfloat16
TILE = 256
PIECE = 128
PAD = 16
VECTORS = 6
OUT_B, GAIN_MLP, BIAS_MLP, DOWN_B, GAIN_ATTN, BIAS_ATTN, UP_B, MIXED = range(8)
COST = 1
MIB = 1024 * 1024


def dot(left, right):
    return jnp.dot(left, right, preferred_element_type=F32)


def dot_rows(left, right):
    return lax.dot_general(left, right, (((0,), (0,)), ((), ())), preferred_element_type=F32)


def dot_cols(left, right):
    return lax.dot_general(left, right, (((1,), (1,)), ((), ())), preferred_element_type=F32)


def swap(value, axis, bit):
    size = lax.axis_size(axis)
    return lax.ppermute(value, axis, [(i, i ^ bit) for i in range(size)])


def norm_stats(values):
    center = values - jnp.mean(values, axis=-1, keepdims=True)
    inverse = lax.rsqrt(jnp.mean(center * center, axis=-1, keepdims=True) + EPSILON)
    return center * inverse, inverse


def norm_backward(upstream, normal, inverse, gain_vec):
    scaled = upstream * gain_vec
    mean_part = jnp.mean(scaled, axis=-1, keepdims=True)
    mean_cross = jnp.mean(scaled * normal, axis=-1, keepdims=True)
    return inverse * (scaled - mean_part - normal * mean_cross)


def vmem():
    return pl.BlockSpec(memory_space=pltpu.VMEM)


def anywhere():
    return pl.BlockSpec(memory_space=pl.ANY)


def row(index):
    return slice(index, index + 1)


def smem():
    return pl.BlockSpec(memory_space=pltpu.SMEM)


def shape(dims, dtype):
    return jax.ShapeDtypeStruct(dims, dtype)


def join(*values):
    return lax.optimization_barrier(values)


def in_hbm(*values):
    return [pltpu.with_memory_space_constraint(value, pltpu.HBM) for value in values]


def params(name, flops, moved, mebibytes=24):
    return dict(
        compiler_params=pltpu.CompilerParams(vmem_limit_bytes=mebibytes * MIB),
        cost_estimate=pl.CostEstimate(flops=flops // COST, transcendentals=0, bytes_accessed=moved // COST),
        name=name,
    )


def over_pieces(count, step):
    def body(index, carry):
        step(index, pl.ds(pl.multiple_of(index * PIECE, PIECE), PIECE))
        return carry

    lax.fori_loop(0, count // PIECE, body, 0)


def head_cols(head):
    return slice(head * HEAD_DIM, (head + 1) * HEAD_DIM)


def tiles(width):
    return [slice(start, start + TILE) for start in range(0, width, TILE)]


def chip_half():
    return lax.axis_index("mp") // 2


def x_side():
    return lax.axis_index("dp") % 2


def attend_kernel(
    items, heads, span_rows, info_ref, tok_ref, vec_ref, qw_ref, kw_ref, vw_ref,
    normed_ref, q_ref, k_ref, v_ref, lse_ref, near_ref, other_ref, o_ref
):
    seq = tok_ref.shape[0]
    item = pl.program_id(0)
    length = info_ref[item]
    for start in range(0, seq, PIECE):
        rows = slice(start, start + PIECE)
        normal, unused = norm_stats(tok_ref[rows, :].astype(F32))
        normed_ref[rows, :] = (normal * vec_ref[row(GAIN_ATTN), :] + vec_ref[row(BIAS_ATTN), :]).astype(BF16)
    normed = normed_ref[...]
    hw = q_ref.shape[1]
    q_ref[...] = (dot_cols(normed, qw_ref[...]) + vec_ref[row(MIXED), :hw]).astype(BF16) * jnp.asarray(SCALE, BF16)
    k_ref[...] = dot_cols(normed, kw_ref[...]).astype(BF16)
    v_ref[...] = (dot_cols(normed, vw_ref[...]) + vec_ref[row(MIXED), hw : 2 * hw]).astype(BF16)

    def run(span):
        valid = lax.broadcasted_iota(jnp.int32, (span, span), 0) < length
        for head in range(heads):
            cols = head_cols(head)
            scores = jnp.where(valid, dot_cols(k_ref[:span, cols], q_ref[:span, cols]), -1e9)
            top = jnp.max(scores, axis=0, keepdims=True)
            raised = jnp.exp(scores - top)
            total = jnp.sum(raised, axis=0, keepdims=True)
            mixed = dot_rows(v_ref[:span, cols], raised.astype(BF16)) / total
            o_ref[pl.ds(pl.multiple_of(item * seq, seq), span), cols] = mixed.T.astype(BF16)
            lse_ref[0, head : head + 1, :span] = top + jnp.log(total)
        if span < seq:
            o_ref[pl.ds(pl.multiple_of(item * seq + span, span), seq - span), :] = jnp.zeros(
                (seq - span, heads * HEAD_DIM), BF16
            )

    half = seq // 2

    @pl.when(length <= half)
    def _():
        run(half)

    @pl.when(length > half)
    def _():
        run(seq)

    @pl.when(item == items - 1)
    def _():
        start = chip_half() * span_rows
        near_ref[...] = o_ref[pl.ds(pl.multiple_of(start, PIECE), span_rows), :]
        other_ref[...] = o_ref[pl.ds(pl.multiple_of(span_rows - start, PIECE), span_rows), :]


def attend(info, rows2d, vecs, query_w, key_w, value_w, items, seq):
    rows, width = rows2d.shape
    hw = query_w.shape[0]
    heads = hw // HEAD_DIM
    row_block = lambda cols: pl.BlockSpec((seq, cols), lambda i, n: (i, 0))
    whole = lambda dims: pl.BlockSpec(dims, lambda i, n: (0,) * len(dims))
    return pl.pallas_call(
        functools.partial(attend_kernel, items, heads, rows // 2),
        out_shape=[pltpu.HBM((rows, width), BF16)]
        + [pltpu.HBM((rows, hw), BF16)] * 3
        + [pltpu.HBM((items, 8, seq), F32)]
        + [shape((rows // 2, hw), BF16)] * 2,
        grid_spec=pltpu.PrefetchScalarGridSpec(
            num_scalar_prefetch=1,
            grid=(items,),
            in_specs=[row_block(width), whole(vecs.shape)] + [whole((hw, width))] * 3,
            out_specs=[row_block(width)]
            + [row_block(hw)] * 3
            + [pl.BlockSpec((1, 8, seq), lambda i, n: (i, 0, 0))]
            + [whole((rows // 2, hw))] * 2,
            scratch_shapes=[pltpu.VMEM((rows, hw), BF16)],
        ),
        **params("attend", 6 * rows * width * hw + 4 * rows * seq * hw, 4 * rows * width),
    )(info, *in_hbm(rows2d, vecs, query_w, key_w, value_w))


def attend_back_kernel(
    items, heads, share, len_ref, normed_ref, q_ref, k_ref, v_ref, lse_ref, near_ref, other_ref,
    dq_ref, dk_ref, dv_ref, grad_ref, sums_ref, do_ref, grad_acc
):
    seq = normed_ref.shape[0]
    hw = heads * HEAD_DIM
    item = pl.program_id(0)
    length = len_ref[item]

    @pl.when(item == 0)
    def _():
        begin = chip_half() * 2 * share
        do_ref[pl.ds(pl.multiple_of(begin, PIECE), 2 * share), :] = near_ref[...]
        do_ref[pl.ds(pl.multiple_of(2 * share - begin, PIECE), 2 * share), :] = other_ref[...]
        sums_ref[...] = jnp.zeros_like(sums_ref)
        grad_acc[...] = jnp.zeros_like(grad_acc)

    def run(span):
        valid = lax.broadcasted_iota(jnp.int32, (span, span), 0) < length
        for head in range(heads):
            cols = head_cols(head)
            query, keys, vals = q_ref[:span, cols], k_ref[:span, cols], v_ref[:span, cols]
            upstream = do_ref[pl.ds(pl.multiple_of(item * seq, seq), span), cols]
            scores = jnp.where(valid, dot_cols(keys, query), -1e9)
            prob = jnp.exp(scores - lse_ref[0, head : head + 1, :span])
            dv_ref[:span, cols] = dot(prob.astype(BF16), upstream).astype(BF16)
            prob_grad = dot_cols(vals, upstream)
            product = prob * prob_grad
            row_term = jnp.sum(product, axis=0, keepdims=True)
            score_grad = (product - prob * row_term).astype(BF16)
            dk_ref[:span, cols] = dot(score_grad, query).astype(BF16)
            dq_ref[:span, cols] = (dot_rows(keys, score_grad) * SCALE).T.astype(BF16)
        for index, ref in enumerate((dq_ref, dk_ref, dv_ref)):
            grad_acc[index * hw : (index + 1) * hw, :] += dot_rows(ref[:span, :], normed_ref[:span, :])
            if index != 1:
                sums_ref[row(index), :hw] += jnp.sum(ref[:span, :].astype(F32), axis=0, keepdims=True)
            if span < seq:
                ref[span:, :] = jnp.zeros((seq - span, hw), BF16)

    half = seq // 2

    @pl.when(length <= half)
    def _():
        run(half)

    @pl.when(length > half)
    def _():
        run(seq)

    @pl.when(item == items - 1)
    def _():
        grad_ref[...] = grad_acc[...].astype(BF16)


def attend_back(lengths, normed, q, k, v, lse, near, other, items, seq, share):
    rows, width = normed.shape
    hw = q.shape[1]
    heads = hw // HEAD_DIM
    row_block = lambda cols: pl.BlockSpec((seq, cols), lambda i, n: (i, 0))
    whole = lambda dims: pl.BlockSpec(dims, lambda i, n: (0,) * len(dims))
    return pl.pallas_call(
        functools.partial(attend_back_kernel, items, heads, share),
        out_shape=[pltpu.HBM((rows, hw), BF16)] * 3 + [shape((3 * hw, width), BF16), shape((8, width), F32)],
        grid_spec=pltpu.PrefetchScalarGridSpec(
            num_scalar_prefetch=1,
            grid=(items,),
            in_specs=[row_block(width)]
            + [row_block(hw)] * 3
            + [pl.BlockSpec((1, 8, seq), lambda i, n: (i, 0, 0))]
            + [whole((2 * share, hw))] * 2,
            out_specs=[row_block(hw)] * 3 + [whole((3 * hw, width)), whole((8, width))],
            scratch_shapes=[pltpu.VMEM((rows, hw), BF16), pltpu.VMEM((3 * hw, width), F32)],
        ),
        **params("attend_back", 6 * rows * width * hw + 10 * rows * seq * hw, 8 * rows * width),
    )(lengths, *in_hbm(normed, q, k, v, lse, near, other))


def normed_back_kernel(
    items, share, len_ref, tok_ref, dq_ref, dk_ref, dv_ref, qw_ref, kw_ref, vw_ref, vec_in, low_in,
    send_ref, keep_ref, pass_ref, sums_ref, part_ref
):
    seq = tok_ref.shape[0]
    item = pl.program_id(0)
    length = len_ref[item]
    me = lax.axis_index("mp")

    @pl.when(item == 0)
    def _():
        sums_ref[...] = jnp.zeros_like(sums_ref)

    def run(span):
        start = pl.multiple_of(item * seq, seq)

        def back_rows(index, rows):
            piece = dot(dq_ref[rows, :], qw_ref[...]) + dot(dk_ref[rows, :], kw_ref[...]) + dot(dv_ref[rows, :], vw_ref[...])
            part_ref[pl.ds(pl.multiple_of(start + index * PIECE, PIECE), PIECE), :] = piece
            normal, unused = norm_stats(tok_ref[rows, :].astype(F32))
            sums_ref[row(0), :] += jnp.sum(piece * normal, axis=0, keepdims=True)
            sums_ref[row(1), :] += jnp.sum(piece, axis=0, keepdims=True)

        over_pieces(span, back_rows)
        if span < seq:
            part_ref[pl.ds(pl.multiple_of(start + span, span), seq - span), :] = jnp.zeros(
                (seq - span, part_ref.shape[1]), F32
            )

    half = seq // 2

    @pl.when(length <= half)
    def _():
        run(half)

    @pl.when(length > half)
    def _():
        run(seq)

    @pl.when(item == items - 1)
    def _():
        def block(k):
            return part_ref[pl.ds(pl.multiple_of((me ^ k) * share, PIECE), share), :]

        keep_ref[...] = block(0)
        pass_ref[...] = block(2)
        send_ref[:share, :] = block(1).astype(BF16)
        send_ref[share : 2 * share, :] = block(3).astype(BF16)
        sums_ref[2:5, :] = 0.5 * vec_in[0:3, :]
        sums_ref[5:6, :] = 0.5 * low_in[0:1, :]
        vectors = sums_ref[0:VECTORS, :]
        send_ref[2 * share :, :] = jnp.concatenate(
            [vectors, jnp.zeros((PAD - VECTORS, vectors.shape[1]), F32)], axis=0
        ).astype(BF16)


def normed_back(lengths, rows2d, dq, dk, dv, query_w, key_w, value_w, vec_in, low_in, items, seq, share):
    rows, width = rows2d.shape
    hw = query_w.shape[0]
    row_block = lambda cols: pl.BlockSpec((seq, cols), lambda i, n: (i, 0))
    whole = lambda dims: pl.BlockSpec(dims, lambda i, n: (0,) * len(dims))
    return pl.pallas_call(
        functools.partial(normed_back_kernel, items, share),
        out_shape=[
            shape((2 * share + PAD, width), BF16),
            pltpu.HBM((share, width), F32),
            pltpu.HBM((share, width), F32),
            shape((8, width), F32),
        ],
        grid_spec=pltpu.PrefetchScalarGridSpec(
            num_scalar_prefetch=1,
            grid=(items,),
            in_specs=[row_block(width)]
            + [row_block(hw)] * 3
            + [whole((hw, width))] * 3
            + [whole(vec_in.shape), whole(low_in.shape)],
            out_specs=[
                whole((2 * share + PAD, width)),
                whole((share, width)),
                whole((share, width)),
                whole((8, width)),
            ],
            scratch_shapes=[pltpu.VMEM((rows, width), F32)],
        ),
        **params("normed_back", 6 * rows * width * hw, 8 * rows * width),
    )(lengths, *in_hbm(rows2d, dq, dk, dv, query_w, key_w, value_w, vec_in, low_in))


def load_all(pairs, sems):
    copies = [pltpu.make_async_copy(source, target, sems.at[i]) for i, (source, target) in enumerate(pairs)]
    for copy in copies:
        copy.start()
    return copies


def halves(count):
    return [slice(start, start + count // 2) for start in range(0, count, count // 2)]


def project_kernel(near_ref, far_ref, own_ref, pack_ref, out_ref):
    hw = own_ref.shape[0]
    for cols in tiles(out_ref.shape[1]):
        out_ref[:, cols] = (dot(near_ref[...], own_ref[:, cols]) + dot(far_ref[...], pack_ref[:hw, cols])).astype(BF16)


def project(near, far, own, pack):
    span, hw = near.shape
    width = own.shape[1]
    return pl.pallas_call(
        project_kernel,
        out_shape=shape((span, width), BF16),
        in_specs=[vmem()] * 4,
        out_specs=vmem(),
        **params("project", 4 * span * width * hw, 4 * span * width),
    )(near, far, *in_hbm(own), pack)


def quad_pairs(own_ref, parts, buf, begin=0):
    rows = own_ref.shape[0] // 4
    mine = lax.axis_index("dp") % 4
    pairs = [(own_ref, buf.at[0])]
    for index, part in enumerate(parts):
        count = rows // 2 if len(parts) == 5 and index > 2 else rows
        start = (mine ^ min(index, 3)) * rows + (count if index == 4 else 0)
        pairs.append((part.at[pl.ds(begin, count), :], buf.at[1, pl.ds(pl.multiple_of(start, 32), count), :]))
    return pairs


def conv_pairs(conv_ref, parts, wc):
    return quad_pairs(conv_ref, parts, wc, parts[0].shape[0] - conv_ref.shape[0] // 4)


def cot_pairs(cot_ref, far_cot, cots):
    span = cots.shape[1]
    start = pl.multiple_of(chip_half() * span, PIECE)
    return [(cot_ref.at[pl.ds(start, span), :], cots.at[0]), (far_cot, cots.at[1])]


def expand_kernel(tok_ref, vec_ref, part_ref, other_ref, out_far, up_ref, *rest):
    up_parts = rest[:5]
    mid_ref, normed_ref, act_ref, slope_ref, wu, tok_buf, sems = rest[5:]
    span, width = mid_ref.shape
    start = pl.multiple_of(chip_half() * span, PIECE)
    copies = load_all([(tok_ref.at[pl.ds(start, span), :], tok_buf)] + quad_pairs(up_ref, up_parts, wu), sems)
    copies[0].wait()

    def add_rows(index, rows):
        mid = tok_buf[rows, :].astype(F32) + vec_ref[row(OUT_B), :] + part_ref[rows, :].astype(F32) + other_ref[rows, :].astype(F32)
        mid_ref[rows, :] = mid
        normal, unused = norm_stats(mid)
        normed_ref[rows, :] = (normal * vec_ref[row(GAIN_MLP), :] + vec_ref[row(BIAS_MLP), :]).astype(BF16)

    over_pieces(span, add_rows)
    for copy in copies[1:]:
        copy.wait()
    hw = out_far.shape[0] - PAD

    def body(step, carry):
        block = step % 2
        rows = pl.ds(pl.multiple_of(step // 2 * (span // 2), PIECE), span // 2)
        for cols in tiles(width):
            own_bias, other_bias = vec_ref[row(UP_B), cols], out_far[hw:, cols].astype(F32)[0:1]
            preact = dot(normed_ref[rows, :], wu[block, :, cols]) + jnp.where(block == 0, own_bias, other_bias)
            normal_cdf = 0.5 * lax.erf(preact * (0.5**0.5)) + 0.5
            density = jnp.exp(preact * preact * -0.5) * 0.3989422804014327
            act_ref[block, rows, cols] = (preact * normal_cdf).astype(BF16)
            slope_ref[block, rows, cols] = (normal_cdf + preact * density).astype(BF16)
        return carry

    lax.fori_loop(0, 4, body, 0)


def expand(rows2d, vecs, part, other, out_far, up_w, up_parts):
    span, width = part.shape
    return pl.pallas_call(
        expand_kernel,
        out_shape=[
            shape((span, width), F32),
            shape((span, width), BF16),
            shape((2, span, width), BF16),
            shape((2, span, width), BF16),
        ],
        in_specs=[anywhere()] + [vmem()] * 4 + [anywhere()] * 6,
        out_specs=[vmem()] * 4,
        scratch_shapes=[
            pltpu.VMEM((2, width, width), BF16),
            pltpu.VMEM((span, width), BF16),
            pltpu.SemaphoreType.DMA((7,)),
        ],
        **params("expand", 4 * span * width * width, 14 * width * width),
    )(*in_hbm(rows2d, vecs), part, other, *in_hbm(out_far, up_w, *up_parts))


def contract_kernel(act_ref, down_ref, *rest):
    down_parts = rest[:4]
    out_ref, wd, sems = rest[4:]
    for copy in load_all(quad_pairs(down_ref, down_parts, wd), sems):
        copy.wait()
    for cols in tiles(out_ref.shape[1]):
        out_ref[:, cols] = (dot(act_ref[0], wd[0, :, cols]) + dot(act_ref[1], wd[1, :, cols])).astype(BF16)


def contract(act, down_w, down_parts):
    unused, span, width = act.shape
    return pl.pallas_call(
        contract_kernel,
        out_shape=shape((span, width), BF16),
        in_specs=[vmem()] + [anywhere()] * 5,
        out_specs=vmem(),
        scratch_shapes=[pltpu.VMEM((2, width, width), BF16), pltpu.SemaphoreType.DMA((5,))],
        **params("contract", 4 * span * width * width, 8 * width * width),
    )(act, *in_hbm(down_w, *down_parts))


def piece_place(info_ref, items, seq, span, index):
    piece = chip_half() * (span // PIECE) + index
    per_item = seq // PIECE
    item = piece // per_item
    length = info_ref[item]
    slot = lax.broadcasted_iota(jnp.int32, (PIECE, 1), 0) + (piece % per_item) * PIECE
    return item, length, (slot < length).astype(F32)


def convolve_kernel(items, seq, info_ref, vec_ref, mid_ref, part_ref, other_ref, conv_ref, *rest):
    parts, (cot_ref, far_cot) = rest[:4], rest[4:6]
    low_ref, z_ref, sums_ref, wc, cots, sems = rest[6:]
    span, width = mid_ref.shape
    block = wc.shape[1]
    copies = load_all(conv_pairs(conv_ref, parts, wc) + cot_pairs(cot_ref, far_cot, cots), sems)
    low_ref[...] = (
        mid_ref[...] + vec_ref[row(DOWN_B), :] + part_ref[...].astype(F32) + other_ref[...].astype(F32)
    ).astype(BF16)
    for copy in copies:
        copy.wait()
    sums_ref[...] = jnp.zeros_like(sums_ref)
    for k in range(2):
        z_ref[k] = dot_cols(low_ref[...], wc[k])

        def add_sums(index, rows):
            item, unused, mask = piece_place(info_ref, items, seq, span, index)
            z = z_ref[k, rows, :]
            masked = z * mask
            upstream = cots[k, rows, :].astype(F32) * mask
            lines = [
                jnp.sum(part, axis=0, keepdims=True) for part in (masked, masked * z, upstream, upstream * z)
            ]
            total = jnp.concatenate(lines, axis=0)
            for base in range(0, block, CH):
                sums_ref[item] += total[:, base : base + CH]

        over_pieces(span, add_sums)


def convolve(info, vecs, mid, part, other, conv_w, parts, cot_rows, far_cot, items, seq):
    span, width = mid.shape
    block = cot_rows.shape[1]
    return pl.pallas_call(
        functools.partial(convolve_kernel, items, seq),
        out_shape=[shape((span, width), BF16), shape((2, span, block), F32), shape((items, 4, CH), F32)],
        in_specs=[smem()] + [vmem()] * 4 + [anywhere()] * 7,
        out_specs=[vmem()] * 3,
        scratch_shapes=[
            pltpu.VMEM((2, block, width), BF16),
            pltpu.VMEM((2, span, block), BF16),
            pltpu.SemaphoreType.DMA((7,)),
        ],
        **params("convolve", 4 * span * width * block, 14 * width * width),
    )(info, *in_hbm(vecs), mid, part, other, *in_hbm(conv_w, *parts, cot_rows, far_cot))


def norm_back_kernel(items, seq, norm_at, info_ref, norm_ref, tot_ref, got_ref, z_ref, conv_ref, *rest):
    parts, (cot_ref, far_cot) = rest[:4], rest[4:6]
    near_ref, far_ref, dz_ref, out_ref, sums_ref, wc, cots, sems = rest[6:]
    span, width = out_ref.shape
    block = z_ref.shape[2]
    copies = load_all(conv_pairs(conv_ref, parts, wc) + cot_pairs(cot_ref, far_cot, cots), sems)
    scale = norm_ref[row(MIXED), norm_at : norm_at + CH]
    shift = norm_ref[row(MIXED), norm_at + CH : norm_at + 2 * CH]

    def item_terms(item, length):
        count = (8 * length).astype(F32)
        total = tot_ref[item] + got_ref[item]
        center = total[0:1] / count
        spread = lax.rsqrt(total[1:2] / count - center * center + EPSILON)
        plain = total[2:3]
        cross = spread * (total[3:4] - center * plain)
        return count, center, spread, plain, cross

    sums_ref[...] = jnp.zeros_like(sums_ref)
    for item in range(items):
        unused, unused, unused, plain, cross = item_terms(item, info_ref[item])
        sums_ref[0:1, :CH] += cross
        sums_ref[0:1, CH : 2 * CH] += plain
    for copy in copies:
        copy.wait()

    def back_rows(index, rows):
        item, length, mask = piece_place(info_ref, items, seq, span, index)
        count, center, spread, plain, cross = item_terms(item, length)
        terms = [center, spread, plain / count, cross / count, scale, shift, spread * scale]
        wide = [jnp.concatenate([t] * (block // CH), axis=1) for t in terms]
        center, spread, plain, cross, scale_w, shift_w, factor = wide
        for k, vol_ref in enumerate((near_ref, far_ref)):
            normal = (z_ref[k, rows, :] - center) * spread
            vol_ref[rows, :] = (mask * (scale_w * normal + shift_w)).astype(BF16)
            upstream = cots[k, rows, :].astype(F32)
            dz_ref[k, rows, :] = (mask * factor * (upstream - plain - normal * cross)).astype(BF16)

    over_pieces(span, back_rows)
    for cols in tiles(width):
        out_ref[:, cols] = (dot(dz_ref[0], wc[0, :, cols]) + dot(dz_ref[1], wc[1, :, cols])).astype(BF16)


def norm_back(info, vecs, total, got, z, conv_w, parts, cot_rows, far_cot, items, seq, norm_at):
    unused, span, block = z.shape
    width = conv_w.shape[1]
    return pl.pallas_call(
        functools.partial(norm_back_kernel, items, seq, norm_at),
        out_shape=[
            shape((span, block), BF16),
            shape((span, block), BF16),
            shape((2, span, block), BF16),
            shape((span, width), BF16),
            shape((8, width), F32),
        ],
        in_specs=[smem()] + [vmem()] * 4 + [anywhere()] * 7,
        out_specs=[vmem()] * 5,
        scratch_shapes=[
            pltpu.VMEM((2, block, width), BF16),
            pltpu.VMEM((2, span, block), BF16),
            pltpu.SemaphoreType.DMA((7,)),
        ],
        **params("norm_back", 4 * span * width * block, 6 * width * width),
    )(info, *in_hbm(vecs), total, got, z, *in_hbm(conv_w, *parts, cot_rows, far_cot))


def mlp_back_kernel(part_ref, other_ref, slope_ref, up_ref, down_ref, *rest):
    up_parts, down_parts = rest[:5], rest[5:9]
    du_ref, out_ref, sums_ref, up_sums, low_ref, wu, wd, sems = rest[9:]
    span, width = out_ref.shape
    copies = load_all(quad_pairs(down_ref, down_parts, wd) + quad_pairs(up_ref, up_parts, wu), sems)
    sums_ref[...] = jnp.zeros_like(sums_ref)
    up_sums[...] = jnp.zeros_like(up_sums)
    for rows in halves(span):
        grad = part_ref[rows, :].astype(F32) + other_ref[rows, :].astype(F32)
        low_ref[rows, :] = grad.astype(BF16)
        sums_ref[0:1, :] += jnp.sum(grad, axis=0, keepdims=True)
    for copy in copies[:5]:
        copy.wait()

    def body(step, carry):
        block = step % 2
        rows = pl.ds(pl.multiple_of(step // 2 * (span // 2), PIECE), span // 2)
        for cols in tiles(width):
            grad = dot_cols(low_ref[rows, :], wd[block, cols, :]) * slope_ref[block, rows, cols].astype(F32)
            low = grad.astype(BF16)
            du_ref[block, rows, cols] = low
            up_sums[block, 0:1, cols] += jnp.sum(low.astype(F32), axis=0, keepdims=True)
        return carry

    lax.fori_loop(0, 4, body, 0)
    for copy in copies[5:]:
        copy.wait()
    for cols in tiles(width):
        out_ref[:, cols] = (dot_cols(du_ref[0], wu[0, cols, :]) + dot_cols(du_ref[1], wu[1, cols, :])).astype(BF16)


def mlp_back(part, other, slope, up_w, down_w, up_parts, down_parts):
    span, width = part.shape
    return pl.pallas_call(
        mlp_back_kernel,
        out_shape=[
            shape((2, span, width), BF16),
            shape((span, width), BF16),
            shape((8, width), F32),
            shape((2, 8, width), F32),
        ],
        in_specs=[vmem()] * 3 + [anywhere()] * 11,
        out_specs=[vmem()] * 4,
        scratch_shapes=[
            pltpu.VMEM((span, width), BF16),
            pltpu.VMEM((2, width, width), BF16),
            pltpu.VMEM((2, width, width), BF16),
            pltpu.SemaphoreType.DMA((11,)),
        ],
        **params("mlp_back", 8 * span * width * width, 20 * width * width),
    )(part, other, slope, *in_hbm(up_w, down_w, *up_parts, *down_parts))


def mid_back_kernel(share, vec_ref, mid_ref, part_ref, other_ref, grad_ref, got_ref, out_w, pack_ref, *rest):
    near_ref, far_ref, em_ref, mine_ref, sums_ref, dmid_ref = rest
    span, width = mid_ref.shape
    sums_ref[...] = jnp.zeros_like(sums_ref)

    def back_rows(index, rows):
        normal, inverse = norm_stats(mid_ref[rows, :])
        grad = grad_ref[rows, :].astype(F32) + got_ref[rows, :].astype(F32)
        dmid = part_ref[rows, :].astype(F32) + other_ref[rows, :].astype(F32)
        dmid += norm_backward(grad, normal, inverse, vec_ref[row(GAIN_MLP), :])
        dmid_ref[rows, :] = dmid
        em_ref[rows, :] = dmid.astype(BF16)
        sums_ref[0:1, :] += jnp.sum(grad * normal, axis=0, keepdims=True)
        sums_ref[1:2, :] += jnp.sum(grad, axis=0, keepdims=True)
        sums_ref[2:3, :] += jnp.sum(dmid, axis=0, keepdims=True)

    over_pieces(span, back_rows)
    far_ref[...] = dot_cols(em_ref[...], pack_ref[: out_w.shape[0], :]).astype(BF16)
    near_ref[...] = dot_cols(em_ref[...], out_w[...]).astype(BF16)
    mine_ref[...] = dmid_ref[pl.ds(pl.multiple_of(lax.axis_index("mp") % 2 * share, PIECE), share), :]


def mid_back(vecs, mid, part, other, grad, got, out_w, pack):
    span, width = mid.shape
    hw = out_w.shape[0]
    return pl.pallas_call(
        functools.partial(mid_back_kernel, span // 2),
        out_shape=[
            shape((span, hw), BF16),
            shape((span, hw), BF16),
            shape((span, width), BF16),
            shape((span // 2, width), F32),
            shape((8, width), F32),
        ],
        in_specs=[vmem()] * 8,
        out_specs=[vmem()] * 5,
        scratch_shapes=[pltpu.VMEM((span, width), F32)],
        **params("mid_back", 4 * span * width * hw, 12 * width * width),
    )(*in_hbm(vecs), mid, part, other, grad, got, *in_hbm(out_w, pack))


LINKS = {"y": ("mp", 2), "x": ("dp", 1), "z": ("dp", 2)}


class Lane:
    def __init__(self, blocks, rows, parts, link):
        self.blocks, self.rows, self.parts, self.link = blocks, rows, parts, link


class Kept:
    def __init__(self, blocks, rows, array, link, place):
        self.blocks, self.rows, self.array, self.link, self.place = blocks, rows, array, link, place


def high_of(link):
    axis, bit = LINKS[link]
    return (lax.axis_index(axis) // bit) % 2


def aligned(value, rows):
    return value if isinstance(value, int) else pl.multiple_of(value, rows & -rows)


def product_rows(left, right, block, out_ref, at):
    size = left.shape[-1]
    for base in range(0, size, TILE):
        cols = slice(base, min(base + TILE, size))
        lhs = left[block, :, cols] if len(left.shape) == 3 else left[:, cols]
        rhs = right[block] if len(right.shape) == 3 else right[...]
        out_ref[at + base : at + cols.stop, :] = dot_rows(lhs, rhs).astype(BF16)


def products_kernel(lefts, *refs):
    right, out_ref = refs[-2:]
    size = out_ref.shape[0] // 2
    for block in range(2):
        product_rows(refs[block] if lefts == 2 else refs[0], right, block, out_ref, block * size)


def products(name, lefts, right):
    span, width = right.shape[-2:]
    size = lefts[0].shape[-1]
    return pl.pallas_call(
        functools.partial(products_kernel, len(lefts)),
        out_shape=shape((2 * size, width), BF16),
        in_specs=[vmem()] * (len(lefts) + 1),
        out_specs=vmem(),
        **params(name, 4 * span * size * width, 8 * size * width),
    )(*lefts, right)


def emit_kernel(count, inputs, lanes, links, *refs):
    lefts, rights = refs[:count], refs[count : 2 * count]
    sources = list(refs[2 * count : 2 * count + inputs])
    outs = refs[2 * count + inputs :]
    if count:
        product, outs = outs[-1], outs[:-1]
        sources = [product] + sources
        total = product.shape[0] // 2
        begin = 0
        for left, right in zip(lefts, rights):
            for block in range(2):
                product_rows(left, right, block, product, block * total + begin)
            begin += left.shape[-1]
    sends = dict(zip(links, outs))
    kept = iter(outs[len(links) :])
    last = outs[-1]
    places = dict.fromkeys(list(links) + [None], 0)

    for lane in lanes:

        def total_of(block, start, size):
            values = [
                sources[index][pl.ds(aligned(base + block * stride + start, size), size), :]
                for index, base, stride in lane.parts
            ]
            if len(values) == 1:
                return values[0]
            return (values[0].astype(F32) + values[1].astype(F32)).astype(BF16)

        place = places[lane.link]
        if lane.link is None:
            last[place : place + lane.rows, :] = total_of(0, 0, lane.rows)
            places[None] += lane.rows
            continue
        send, keep = sends[lane.link], next(kept)
        if lane.link == "y":
            send[place : place + lane.rows, :] = total_of(1, 0, lane.rows)
            keep[...] = total_of(0, 0, lane.rows)
            places["y"] += lane.rows
            continue
        half = lane.rows // 2
        high = high_of(lane.link)
        for block in range(lane.blocks):
            rows = slice(block * half, (block + 1) * half)
            keep[rows, :] = total_of(block, high * half, half)
            send[place + rows.start : place + rows.stop, :] = total_of(block, (1 - high) * half, half)
        places[lane.link] += lane.blocks * half


def emit(name, lefts, rights, inputs, lanes, width, far=False):
    places = dict.fromkeys(list(LINKS) + [None], 0)
    kept = []
    for lane in lanes:
        sent = lane.blocks * lane.rows // 2 if lane.link else lane.rows
        if lane.link:
            blocks, rows = (1, lane.rows) if lane.link == "y" else (lane.blocks, lane.rows // 2)
            kept.append(Kept(blocks, rows, None, lane.link, places[lane.link]))
        places[lane.link] += sent
    links = [link for link in LINKS if places[link]]
    out_rows = [places[link] for link in links] + [k.blocks * k.rows for k in kept]
    if places[None]:
        out_rows.append(places[None])
    size = sum(left.shape[-1] for left in lefts)
    span = rights[0].shape[-2] if rights else 0
    results = pl.pallas_call(
        functools.partial(emit_kernel, len(lefts), len(inputs), lanes, links),
        out_shape=[
            pltpu.HBM((rows, width), BF16) if far and len(links) <= i < len(links) + len(kept) else shape((rows, width), BF16)
            for i, rows in enumerate(out_rows)
        ],
        in_specs=[vmem()] * (2 * len(lefts) + len(inputs)),
        out_specs=[vmem()] * len(out_rows),
        scratch_shapes=[pltpu.VMEM((2 * size, width), BF16)] if lefts else [],
        **params(name, 4 * span * size * width, 8 * size * width),
    )(*lefts, *rights, *inputs)
    for keep, array in zip(kept, results[len(links) :]):
        keep.array = array
        keep.far = far
    return dict(zip(links, results)), kept, results[-1] if places[None] else None


def send_all(sends):
    return {link: swap(value, *LINKS[link]) for link, value in sends.items()}


def turn(name, kept, got, links, width, fresh=(), far=False):
    inputs = [k.array for k in kept] + list(got.values()) + [lane[0] for lane in fresh]
    inputs = [in_hbm(v)[0] if k.far else v for k, v in zip(kept, inputs)] + inputs[len(kept) :]
    came = {link: len(kept) + i for i, link in enumerate(got)}
    lanes = []
    for i, (k, link) in enumerate(zip(kept, links)):
        lanes.append(Lane(k.blocks, k.rows, [(i, 0, k.rows), (came[k.link], k.place, k.rows)], link))
    for i, (lane, link) in enumerate(zip(fresh, links[len(kept) :])):
        lanes.append(Lane(lane[3], lane[4], [(len(kept) + len(got) + i, lane[1], lane[2])], link))
    return emit(name, [], [], inputs, lanes, width, far)


def spread_kernel(lanes, cuts, flip, *refs):
    first, gots, outs, total = refs[0], refs[1:5], refs[5:-1], refs[-1]
    bits = {"x": high_of("x"), "z": high_of("z")}
    places = [0, 0]
    sizes = [sum(lane[1] for lane in lanes if lane[3] == group) for group in range(2)]
    for base, rows, order, group in lanes:
        at = places[group]
        places[group] += rows
        near, far = ("z", "x") if group == 0 else ("x", "z")
        got_near, got_far = gots[2 * group], gots[2 * group + 1]
        offset = at + (sizes[0] if group else 0)
        pieces = [
            (first[offset : offset + rows, :], ()),
            (got_near[at : at + rows, :], (near,)),
            (got_far[at : at + rows, :], (far,)),
            (got_far[sizes[group] + at : sizes[group] + at + rows, :], (near, far)),
        ]
        for value, flipped in pieces:
            index = [1 - bits[link] if link in flipped else bits[link] for link in order]
            start = base + (index[0] * 2 + index[1]) * rows
            total[pl.ds(aligned(start, rows), rows), :] = value.astype(F32)
    begin = 0
    for i, (out, size) in enumerate(zip(outs, cuts)):
        value = total[begin : begin + size, :]
        out[...] = value.T if i in flip else value
        begin += size


def spread(name, lanes, cuts, flip, first, gots):
    width = first.shape[1]
    return pl.pallas_call(
        functools.partial(spread_kernel, lanes, cuts, flip),
        out_shape=[shape((width, size) if i in flip else (size, width), F32) for i, size in enumerate(cuts)],
        in_specs=[vmem()] * 5,
        out_specs=[vmem()] * len(cuts),
        scratch_shapes=[pltpu.VMEM((sum(cuts), width), F32)],
        **params(name, 0, 8 * sum(cuts) * width),
    )(first, *gots)


def pass_kernel(passed_ref, got_ref, sums_ref, up_ref, send_ref, whole_ref):
    share = passed_ref.shape[0]
    send_ref[:share, :] = (passed_ref[...] + got_ref[share : 2 * share, :].astype(F32)).astype(BF16)
    whole = sums_ref[0:VECTORS, :].astype(BF16).astype(F32) + got_ref[2 * share :, :].astype(F32)[0:VECTORS]
    whole = whole.astype(BF16).astype(F32)
    zero = jnp.zeros((1, whole.shape[1]), F32)
    send_ref[share:, :] = jnp.concatenate([whole, up_ref[1, 0:1, :], zero], axis=0).astype(BF16)
    whole_ref[...] = jnp.concatenate([whole, up_ref[0, 0:1, :], zero], axis=0)


def pass_on(passed, got, sums, up_sums):
    share, width = passed.shape
    return pl.pallas_call(
        pass_kernel,
        out_shape=[shape((share + 8, width), BF16), shape((8, width), F32)],
        in_specs=[vmem()] * 4,
        out_specs=[vmem()] * 2,
        **params("pass_on", 0, 8 * share * width),
    )(*in_hbm(passed), got, sums, up_sums)


def finish_kernel(tok_ref, vec_ref, own_ref, got_ref, last_ref, mine_ref, out_ref, tok_buf, sem):
    share = out_ref.shape[0]
    start = pl.multiple_of(lax.axis_index("mp") * share, PIECE)
    copy = pltpu.make_async_copy(tok_ref.at[pl.ds(start, share), :], tok_buf, sem)
    copy.start()
    copy.wait()

    def back_rows(index, rows):
        normal, inverse = norm_stats(tok_buf[rows, :].astype(F32))
        grad = own_ref[rows, :] + got_ref[rows, :].astype(F32) + last_ref[rows, :].astype(F32)
        out_ref[rows, :] = mine_ref[rows, :] + norm_backward(grad, normal, inverse, vec_ref[row(GAIN_ATTN), :])

    over_pieces(share, back_rows)


def finish(rows2d, vecs, own, got, last, mine):
    share, width = own.shape
    return pl.pallas_call(
        finish_kernel,
        out_shape=shape((share, width), F32),
        in_specs=[anywhere()] + [vmem()] * 5,
        out_specs=vmem(),
        scratch_shapes=[pltpu.VMEM((share, width), BF16), pltpu.SemaphoreType.DMA],
        **params("finish", 0, 14 * share * width),
    )(*in_hbm(rows2d, vecs, own), got, last, *in_hbm(mine))


def add_low(left, right):
    return (left.astype(F32) + right.astype(F32)).astype(BF16)


def bit_of(axis, bit):
    return (lax.axis_index(axis) // bit) % 2


def take_half(value, high):
    half = value.shape[0] // 2
    return lax.dynamic_slice_in_dim(value, high * half, half, 0)


def put_half(mine, other, high):
    return jnp.concatenate([jnp.where(high > 0, other, mine), jnp.where(high > 0, mine, other)], axis=0)


def late_bits():
    bits = []
    bit = 4
    while bit < lax.axis_size("dp"):
        bits.append(bit)
        bit *= 2
    return bits


def finish_reduce(current, bit):
    high = bit_of("dp", bit)
    return add_low(take_half(current, high), swap(take_half(current, 1 - high), "dp", bit))


def finish_gather(current, bit):
    return put_half(current, swap(current, "dp", bit), bit_of("dp", bit))


def shards(
    tokens, lengths, gain_attn, bias_attn, query_w, query_b, key_w, value_w, value_b, out_w, out_b, gain_mlp, bias_mlp,
    up_w, up_b, down_w, down_b, deconv_w, scale_norm, shift_norm, cotangent
):
    items, seq, width = tokens.shape
    rows = items * seq
    me = lax.axis_index("mp")
    share = rows // lax.axis_size("mp")
    span = rows // 2
    hw = query_w.shape[1]
    rows2d = tokens.reshape(rows, width)
    side = bit_of("dp", 1)
    chip = bit_of("mp", 2)
    mixed = jnp.concatenate([query_b, value_b, scale_norm, shift_norm])
    mixed = jnp.pad(mixed, (0, width - mixed.shape[0]))
    vecs = jnp.concatenate([out_b, gain_mlp, bias_mlp, down_b, gain_attn, bias_attn, up_b, mixed])
    vecs = vecs.astype(F32).reshape(8, width)
    weights = [query_w.T, key_w.T, value_w.T]
    conv_w = deconv_w.T

    quarter = width // 4
    mine = lax.axis_index("dp") % 4

    def quarter_of(weight, index):
        count = weight.shape[0] // 4
        return lax.dynamic_slice_in_dim(weight, index * count, count, 0)

    def low_quarter(index):
        return jnp.concatenate([quarter_of(down_w, index), quarter_of(conv_w, index)], axis=0)

    bias_rows = jnp.broadcast_to(up_b[None, :], (PAD, width))
    out_far = swap(jnp.concatenate([out_w, bias_rows], axis=0), "mp", 2)
    up_part = swap(quarter_of(up_w, mine), "mp", 2)
    low_part = swap(low_quarter(mine), "mp", 2)

    normed, q, k, v, lse, near, other = attend(lengths, rows2d, vecs, *weights, items, seq)
    out_far, near, other, up_part, low_part = join(out_far, near, other, up_part, low_part)
    far = swap(other, "mp", 2)
    up_parts = [up_part, swap(up_part, "dp", 1), swap(up_part, "dp", 2)]
    cot_rows = cotangent.reshape(rows, -1)
    cot_sent = lax.dynamic_slice_in_dim(cot_rows, (1 - chip) * span, span, 0)
    low_sent = low_quarter(mine ^ 3)
    far, low_part, low_sent, cot_sent, *up_parts = join(far, low_part, low_sent, cot_sent, *up_parts)
    low_last = swap(low_sent, "mp", 2)
    last_half = quarter // 2
    up_parts.append(swap(up_parts[2][:last_half], "dp", 1))
    up_parts.append(swap(up_parts[1][last_half:], "dp", 2))

    part = project(near, far, out_w, out_far)
    part_got = swap(part, "mp", 1)
    part_got, low_part, cot_sent, *up_parts = join(part_got, low_part, cot_sent, *up_parts)
    down_parts = [low_part, swap(low_part, "dp", 1), swap(low_part, "dp", 2)]
    far_cot = swap(cot_sent, "mp", 2)
    mid, normed_two, act, slope = expand(rows2d, vecs, part, part_got, out_far, up_w, up_parts)
    act, low_last, *down_parts = join(act, low_last, *down_parts)
    down_parts.append(low_last)
    part = contract(act, down_w, down_parts)
    part, far_cot = join(part, far_cot)
    low, z, sums = convolve(
        lengths, vecs, mid, part, swap(part, "mp", 1), conv_w, down_parts, cot_rows, far_cot, items, seq
    )
    sums = sums + swap(sums, "mp", 1)
    vol_near, vol_far, dz, grad, norm_sums = norm_back(
        lengths, vecs, sums, swap(sums, "mp", 2), z, conv_w, down_parts, cot_rows, far_cot, items, seq, 2 * hw
    )
    grad_got = swap(grad, "mp", 1)
    conv_raw = products("conv_grad", [dz], low)
    grad_got, conv_raw = join(grad_got, conv_raw)
    block = conv_w.shape[0]
    half = block // 2
    third = width // 3
    lanes = [Lane(2, third, [(0, i * third, width)], link) for i, link in enumerate("yxz")]
    sends, kept, unused = emit("down_grad", [act], [add_low(grad, grad_got)], [], lanes, width)
    grad_got, sends["y"], sends["x"], sends["z"] = join(grad_got, sends["y"], sends["x"], sends["z"])
    came = send_all(sends)
    du, back, low_sums, up_sums = mlp_back(grad, grad_got, slope, up_w, down_w, up_parts, down_parts)
    back, came["y"], came["x"], came["z"] = join(back, came["y"], came["x"], came["z"])
    back_got = swap(back, "mp", 1)
    up_raw = products("up_grad", [normed_two], du)
    fresh = [(conv_raw, 0, block, 2, half), (conv_raw, half, block, 2, half)]
    sends, kept, unused = turn("turn_one", kept, came, "xzyxz", width, fresh)
    back_got, up_raw, sends["y"], sends["x"], sends["z"] = join(back_got, up_raw, sends["y"], sends["x"], sends["z"])
    came = send_all(sends)
    do_near, do_far, em, dmid, vec_sums = mid_back(vecs, mid, grad, grad_got, back, back_got, out_w, out_far)
    do_far, em, came["y"] = join(do_far, em, came["y"])
    do_got = swap(do_far, "mp", 2)
    out_raw = products("out_grad", [near, far], em)
    do_got, out_raw, came["y"], came["x"], came["z"] = join(do_got, out_raw, came["y"], came["x"], came["z"])
    cut = width * 5 // 12
    fresh = [(up_raw, 0, width, 2, cut), (up_raw, cut, width, 2, cut), (up_raw, 2 * cut, width, 2, width - 2 * cut)]
    fresh.append((out_raw, 0, hw, 2, hw))
    sends, kept, unused = turn("turn_two", kept, came, "zyxzxyxzz", width, fresh, True)
    do_got, sends["y"], sends["x"], sends["z"] = join(do_got, sends["y"], sends["x"], sends["z"])
    came = send_all(sends)

    *dqkv, qkv_grad, bias_sums = attend_back(lengths, normed, q, k, v, lse, do_near, do_got, items, seq, share)
    qkv_grad, vol_far, came["y"], came["x"], came["z"], *dqkv = join(
        qkv_grad, vol_far, came["y"], came["x"], came["z"], *dqkv
    )
    cut = qkv_grad.shape[0] * 4 // 9
    fresh = [(qkv_grad, 0, 0, 1, cut), (qkv_grad, cut, 0, 1, qkv_grad.shape[0] - cut)]
    sizes = [k.blocks * k.rows for k in kept[:3]]
    links = [None] * 3 + ["y", "y", "x", "z", "y", "y", "x", "z"]
    sends, kept, first = turn("turn_three", kept, came, links, width, fresh, True)
    for bit in late_bits():
        first = finish_reduce(first, bit)
    came = send_all(sends)
    sent, own, passed, own_sums = normed_back(
        lengths, rows2d, *dqkv, *weights, vec_sums, low_sums, items, seq, share
    )
    first, sent, came["y"], came["x"], came["z"] = join(first, sent, came["y"], came["x"], came["z"])
    for bit in reversed(late_bits()):
        first = finish_gather(first, bit)
    got = swap(sent, "mp", 1)
    conv_sizes = [k.blocks * k.rows for k in kept[:2]]
    came = {link: in_hbm(value)[0] for link, value in came.items()}
    sends, kept, early = turn("turn_four", kept, came, [None, None] + list("zyxxzx"), width)
    came = send_all(sends)
    first, got, vol_far, came["y"], came["x"], came["z"] = join(first, got, vol_far, came["y"], came["x"], came["z"])
    kept = [kept[i] for i in (0, 1, 4, 2, 3, 5)]
    unused, unused, last = turn("turn_five", kept, came, [None] * 6, width)
    last_sizes = [k.blocks * k.rows for k in kept] + conv_sizes
    last = jnp.concatenate([last, early], axis=0)
    for bit in late_bits():
        last = finish_reduce(last, bit)
    edge = sizes[0]
    sent_near = [first[:edge], first[edge:]]
    near_got = [swap(sent_near[0], "dp", 2), swap(sent_near[1], "dp", 1)]
    second, whole = pass_on(passed, got, own_sums, up_sums)
    second = swap(second, "mp", 2)
    far_got = [
        swap(jnp.concatenate([sent_near[0], near_got[0]], axis=0), "dp", 1),
        swap(jnp.concatenate([sent_near[1], near_got[1]], axis=0), "dp", 2),
    ]
    last, second, vol_far, *far_got = join(last, second, vol_far, *far_got)
    vol_got = swap(vol_far, "mp", 2)
    tokens_grad = finish(rows2d, vecs, own, got, second, dmid)
    for bit in reversed(late_bits()):
        last = finish_gather(last, bit)
    whole = (whole + second[share : share + 8].astype(F32))[: VECTORS + 1]
    lines = jnp.concatenate([whole, bias_sums[0:1], bias_sums[2:3], norm_sums[0:1]], axis=0)
    lines = lines + swap(lines, "dp", 1)
    (down_total,) = spread(
        "spread_one",
        [(0, sizes[0], "xz", 0), (third, sizes[1], "xz", 1), (2 * third, sizes[2], "zx", 1)],
        [width],
        [],
        first,
        [near_got[0], far_got[0], near_got[1], far_got[1]],
    )
    last, lines, down_total, tokens_grad = join(last, lines, down_total, tokens_grad)
    edge = sum(last_sizes[:3])
    sent_last = [last[:edge], last[edge:]]
    last_got = [swap(sent_last[0], "dp", 2), swap(sent_last[1], "dp", 1)]
    lines = lines + swap(lines, "dp", 2)
    for bit in late_bits():
        lines = lines + swap(lines, "dp", bit)
    last_far = [
        swap(jnp.concatenate([sent_last[0], last_got[0]], axis=0), "dp", 1),
        swap(jnp.concatenate([sent_last[1], last_got[1]], axis=0), "dp", 2),
    ]
    base = width + hw
    up_cut = width * 5 // 12
    up_total, out_total, query_total, key_total, value_total, conv_total = spread(
        "spread_two",
        [
            (0, last_sizes[0], "xz", 0),
            (up_cut, last_sizes[1], "xz", 0),
            (base, last_sizes[2], "xz", 0),
            (2 * up_cut, last_sizes[3], "zx", 1),
            (width, last_sizes[4], "zx", 1),
            (base + cut, last_sizes[5], "zx", 1),
            (base + 3 * hw, last_sizes[6], "xz", 1),
            (base + 3 * hw + half, last_sizes[7], "zx", 1),
        ],
        [width, hw, hw, hw, hw, block],
        [5],
        last,
        [last_got[0], last_far[0], last_got[1], last_far[1]],
    )
    volume = put_half(vol_near, vol_got, chip).astype(F32)
    return (
        volume.reshape(items, seq, -1),
        tokens_grad,
        lines[0],
        lines[1],
        query_total.T,
        lines[VECTORS + 1, :hw],
        key_total.T,
        value_total.T,
        lines[VECTORS + 2, :hw],
        out_total,
        lines[4],
        lines[2],
        lines[3],
        up_total,
        lines[VECTORS],
        down_total,
        lines[5],
        conv_total,
        lines[VECTORS + 3, :CH],
        lines[VECTORS + 3, CH : 2 * CH],
    )


def solution(mesh):
    in_specs = (
        P("dp", None, None),
        P("dp"),
        P(),
        P(),
        P(None, "mp"),
        P("mp"),
        P(None, "mp"),
        P(None, "mp"),
        P("mp"),
        P("mp", None),
        P(),
        P(),
        P(),
        P(None, "mp"),
        P("mp"),
        P("mp", None),
        P(),
        P(None, "mp"),
        P(),
        P(),
        P("dp", None, "mp"),
    )
    out_specs = (
        P("dp", None, "mp"),
        P(("dp", "mp"), None),
        P(),
        P(),
        P(None, "mp"),
        P("mp"),
        P(None, "mp"),
        P(None, "mp"),
        P("mp"),
        P("mp", None),
        P(),
        P(),
        P(),
        P(None, "mp"),
        P("mp"),
        P("mp", None),
        P(),
        P(None, "mp"),
        P(),
        P(),
    )
    return jax.shard_map(shards, mesh=mesh, in_specs=in_specs, out_specs=out_specs, check_vma=False)
```

```python
import functools

import jax
import jax.numpy as jnp
from jax import lax
from jax.experimental import pallas as pl
from jax.experimental.pallas import tpu as pltpu
from jax.sharding import PartitionSpec as P

HEAD_DIM = 64
CH = 128
EPSILON = 1e-05
SCALE = HEAD_DIM ** (-0.5)
F32 = jnp.float32
BF16 = jnp.bfloat16
TILE = 256
PIECE = 128
PAD = 16
VECTORS = 6
OUT_B, GAIN_MLP, BIAS_MLP, DOWN_B, GAIN_ATTN, BIAS_ATTN, UP_B, MIXED = range(8)
COST = 1
MIB = 1024 * 1024


def dot(left, right):
    return jnp.dot(left, right, preferred_element_type=F32)


def dot_rows(left, right):
    return lax.dot_general(left, right, (((0,), (0,)), ((), ())), preferred_element_type=F32)


def dot_cols(left, right):
    return lax.dot_general(left, right, (((1,), (1,)), ((), ())), preferred_element_type=F32)


def swap(value, axis, bit):
    size = lax.axis_size(axis)
    return lax.ppermute(value, axis, [(i, i ^ bit) for i in range(size)])


def norm_stats(values):
    center = values - jnp.mean(values, axis=-1, keepdims=True)
    inverse = lax.rsqrt(jnp.mean(center * center, axis=-1, keepdims=True) + EPSILON)
    return center * inverse, inverse


def norm_backward(upstream, normal, inverse, gain_vec):
    scaled = upstream * gain_vec
    mean_part = jnp.mean(scaled, axis=-1, keepdims=True)
    mean_cross = jnp.mean(scaled * normal, axis=-1, keepdims=True)
    return inverse * (scaled - mean_part - normal * mean_cross)


def vmem():
    return pl.BlockSpec(memory_space=pltpu.VMEM)


def anywhere():
    return pl.BlockSpec(memory_space=pl.ANY)


def row(index):
    return slice(index, index + 1)


def smem():
    return pl.BlockSpec(memory_space=pltpu.SMEM)


def shape(dims, dtype):
    return jax.ShapeDtypeStruct(dims, dtype)


def join(*values):
    return lax.optimization_barrier(values)


def in_hbm(*values):
    return [pltpu.with_memory_space_constraint(value, pltpu.HBM) for value in values]


def params(name, flops, moved, mebibytes=24):
    return dict(
        compiler_params=pltpu.CompilerParams(vmem_limit_bytes=mebibytes * MIB),
        cost_estimate=pl.CostEstimate(flops=flops // COST, transcendentals=0, bytes_accessed=moved // COST),
        name=name,
    )


def over_pieces(count, step):
    def body(index, carry):
        step(index, pl.ds(pl.multiple_of(index * PIECE, PIECE), PIECE))
        return carry

    lax.fori_loop(0, count // PIECE, body, 0)


def head_cols(head):
    return slice(head * HEAD_DIM, (head + 1) * HEAD_DIM)


def tiles(width):
    return [slice(start, start + TILE) for start in range(0, width, TILE)]


def chip_half():
    return lax.axis_index("mp") // 2


def x_side():
    return lax.axis_index("dp") % 2


def attend_kernel(
    items, heads, span_rows, info_ref, tok_ref, vec_ref, qw_ref, kw_ref, vw_ref,
    normed_ref, q_ref, k_ref, v_ref, lse_ref, near_ref, other_ref, o_ref
):
    seq = tok_ref.shape[0]
    item = pl.program_id(0)
    length = info_ref[item]
    for start in range(0, seq, PIECE):
        rows = slice(start, start + PIECE)
        normal, unused = norm_stats(tok_ref[rows, :].astype(F32))
        normed_ref[rows, :] = (normal * vec_ref[row(GAIN_ATTN), :] + vec_ref[row(BIAS_ATTN), :]).astype(BF16)
    normed = normed_ref[...]
    hw = q_ref.shape[1]
    q_ref[...] = (dot_cols(normed, qw_ref[...]) + vec_ref[row(MIXED), :hw]).astype(BF16) * jnp.asarray(SCALE, BF16)
    k_ref[...] = dot_cols(normed, kw_ref[...]).astype(BF16)
    v_ref[...] = (dot_cols(normed, vw_ref[...]) + vec_ref[row(MIXED), hw : 2 * hw]).astype(BF16)

    def run(span):
        valid = lax.broadcasted_iota(jnp.int32, (span, span), 0) < length
        for head in range(heads):
            cols = head_cols(head)
            scores = jnp.where(valid, dot_cols(k_ref[:span, cols], q_ref[:span, cols]), -1e9)
            top = jnp.max(scores, axis=0, keepdims=True)
            raised = jnp.exp(scores - top)
            total = jnp.sum(raised, axis=0, keepdims=True)
            mixed = dot_rows(v_ref[:span, cols], raised.astype(BF16)) / total
            o_ref[pl.ds(pl.multiple_of(item * seq, seq), span), cols] = mixed.T.astype(BF16)
            lse_ref[0, head : head + 1, :span] = top + jnp.log(total)
        if span < seq:
            o_ref[pl.ds(pl.multiple_of(item * seq + span, span), seq - span), :] = jnp.zeros(
                (seq - span, heads * HEAD_DIM), BF16
            )

    half = seq // 2

    @pl.when(length <= half)
    def _():
        run(half)

    @pl.when(length > half)
    def _():
        run(seq)

    @pl.when(item == items - 1)
    def _():
        start = chip_half() * span_rows
        near_ref[...] = o_ref[pl.ds(pl.multiple_of(start, PIECE), span_rows), :]
        other_ref[...] = o_ref[pl.ds(pl.multiple_of(span_rows - start, PIECE), span_rows), :]


def attend(info, rows2d, vecs, query_w, key_w, value_w, items, seq):
    rows, width = rows2d.shape
    hw = query_w.shape[0]
    heads = hw // HEAD_DIM
    row_block = lambda cols: pl.BlockSpec((seq, cols), lambda i, n: (i, 0))
    whole = lambda dims: pl.BlockSpec(dims, lambda i, n: (0,) * len(dims))
    return pl.pallas_call(
        functools.partial(attend_kernel, items, heads, rows // 2),
        out_shape=[pltpu.HBM((rows, width), BF16)]
        + [pltpu.HBM((rows, hw), BF16)] * 3
        + [pltpu.HBM((items, 8, seq), F32)]
        + [shape((rows // 2, hw), BF16)] * 2,
        grid_spec=pltpu.PrefetchScalarGridSpec(
            num_scalar_prefetch=1,
            grid=(items,),
            in_specs=[row_block(width), whole(vecs.shape)] + [whole((hw, width))] * 3,
            out_specs=[row_block(width)]
            + [row_block(hw)] * 3
            + [pl.BlockSpec((1, 8, seq), lambda i, n: (i, 0, 0))]
            + [whole((rows // 2, hw))] * 2,
            scratch_shapes=[pltpu.VMEM((rows, hw), BF16)],
        ),
        **params("attend", 6 * rows * width * hw + 4 * rows * seq * hw, 4 * rows * width),
    )(info, *in_hbm(rows2d, vecs, query_w, key_w, value_w))


def attend_back_kernel(
    items, heads, share, len_ref, normed_ref, q_ref, k_ref, v_ref, lse_ref, near_ref, other_ref,
    dq_ref, dk_ref, dv_ref, grad_ref, sums_ref, do_ref, grad_acc
):
    seq = normed_ref.shape[0]
    hw = heads * HEAD_DIM
    item = pl.program_id(0)
    length = len_ref[item]

    @pl.when(item == 0)
    def _():
        begin = chip_half() * 2 * share
        do_ref[pl.ds(pl.multiple_of(begin, PIECE), 2 * share), :] = near_ref[...]
        do_ref[pl.ds(pl.multiple_of(2 * share - begin, PIECE), 2 * share), :] = other_ref[...]
        sums_ref[...] = jnp.zeros_like(sums_ref)
        grad_acc[...] = jnp.zeros_like(grad_acc)

    def run(span):
        valid = lax.broadcasted_iota(jnp.int32, (span, span), 0) < length
        for head in range(heads):
            cols = head_cols(head)
            query, keys, vals = q_ref[:span, cols], k_ref[:span, cols], v_ref[:span, cols]
            upstream = do_ref[pl.ds(pl.multiple_of(item * seq, seq), span), cols]
            scores = jnp.where(valid, dot_cols(keys, query), -1e9)
            prob = jnp.exp(scores - lse_ref[0, head : head + 1, :span])
            dv_ref[:span, cols] = dot(prob.astype(BF16), upstream).astype(BF16)
            prob_grad = dot_cols(vals, upstream)
            product = prob * prob_grad
            row_term = jnp.sum(product, axis=0, keepdims=True)
            score_grad = (product - prob * row_term).astype(BF16)
            dk_ref[:span, cols] = dot(score_grad, query).astype(BF16)
            dq_ref[:span, cols] = (dot_rows(keys, score_grad) * SCALE).T.astype(BF16)
        for index, ref in enumerate((dq_ref, dk_ref, dv_ref)):
            grad_acc[index * hw : (index + 1) * hw, :] += dot_rows(ref[:span, :], normed_ref[:span, :])
            if index != 1:
                sums_ref[row(index), :hw] += jnp.sum(ref[:span, :].astype(F32), axis=0, keepdims=True)
            if span < seq:
                ref[span:, :] = jnp.zeros((seq - span, hw), BF16)

    half = seq // 2

    @pl.when(length <= half)
    def _():
        run(half)

    @pl.when(length > half)
    def _():
        run(seq)

    @pl.when(item == items - 1)
    def _():
        grad_ref[...] = grad_acc[...].astype(BF16)


def attend_back(lengths, normed, q, k, v, lse, near, other, items, seq, share):
    rows, width = normed.shape
    hw = q.shape[1]
    heads = hw // HEAD_DIM
    row_block = lambda cols: pl.BlockSpec((seq, cols), lambda i, n: (i, 0))
    whole = lambda dims: pl.BlockSpec(dims, lambda i, n: (0,) * len(dims))
    return pl.pallas_call(
        functools.partial(attend_back_kernel, items, heads, share),
        out_shape=[pltpu.HBM((rows, hw), BF16)] * 3 + [shape((3 * hw, width), BF16), shape((8, width), F32)],
        grid_spec=pltpu.PrefetchScalarGridSpec(
            num_scalar_prefetch=1,
            grid=(items,),
            in_specs=[row_block(width)]
            + [row_block(hw)] * 3
            + [pl.BlockSpec((1, 8, seq), lambda i, n: (i, 0, 0))]
            + [whole((2 * share, hw))] * 2,
            out_specs=[row_block(hw)] * 3 + [whole((3 * hw, width)), whole((8, width))],
            scratch_shapes=[pltpu.VMEM((rows, hw), BF16), pltpu.VMEM((3 * hw, width), F32)],
        ),
        **params("attend_back", 6 * rows * width * hw + 10 * rows * seq * hw, 8 * rows * width),
    )(lengths, *in_hbm(normed, q, k, v, lse, near, other))


def normed_back_kernel(
    items, share, len_ref, tok_ref, dq_ref, dk_ref, dv_ref, qw_ref, kw_ref, vw_ref, vec_in, low_in,
    send_ref, keep_ref, pass_ref, sums_ref, part_ref
):
    seq = tok_ref.shape[0]
    item = pl.program_id(0)
    length = len_ref[item]
    me = lax.axis_index("mp")

    @pl.when(item == 0)
    def _():
        sums_ref[...] = jnp.zeros_like(sums_ref)

    def run(span):
        start = pl.multiple_of(item * seq, seq)

        def back_rows(index, rows):
            piece = dot(dq_ref[rows, :], qw_ref[...]) + dot(dk_ref[rows, :], kw_ref[...]) + dot(dv_ref[rows, :], vw_ref[...])
            part_ref[pl.ds(pl.multiple_of(start + index * PIECE, PIECE), PIECE), :] = piece
            normal, unused = norm_stats(tok_ref[rows, :].astype(F32))
            sums_ref[row(0), :] += jnp.sum(piece * normal, axis=0, keepdims=True)
            sums_ref[row(1), :] += jnp.sum(piece, axis=0, keepdims=True)

        over_pieces(span, back_rows)
        if span < seq:
            part_ref[pl.ds(pl.multiple_of(start + span, span), seq - span), :] = jnp.zeros(
                (seq - span, part_ref.shape[1]), F32
            )

    half = seq // 2

    @pl.when(length <= half)
    def _():
        run(half)

    @pl.when(length > half)
    def _():
        run(seq)

    @pl.when(item == items - 1)
    def _():
        def block(k):
            return part_ref[pl.ds(pl.multiple_of((me ^ k) * share, PIECE), share), :]

        keep_ref[...] = block(0)
        pass_ref[...] = block(2)
        send_ref[:share, :] = block(1).astype(BF16)
        send_ref[share : 2 * share, :] = block(3).astype(BF16)
        sums_ref[2:5, :] = 0.5 * vec_in[0:3, :]
        sums_ref[5:6, :] = 0.5 * low_in[0:1, :]
        vectors = sums_ref[0:VECTORS, :]
        send_ref[2 * share :, :] = jnp.concatenate(
            [vectors, jnp.zeros((PAD - VECTORS, vectors.shape[1]), F32)], axis=0
        ).astype(BF16)


def normed_back(lengths, rows2d, dq, dk, dv, query_w, key_w, value_w, vec_in, low_in, items, seq, share):
    rows, width = rows2d.shape
    hw = query_w.shape[0]
    row_block = lambda cols: pl.BlockSpec((seq, cols), lambda i, n: (i, 0))
    whole = lambda dims: pl.BlockSpec(dims, lambda i, n: (0,) * len(dims))
    return pl.pallas_call(
        functools.partial(normed_back_kernel, items, share),
        out_shape=[
            shape((2 * share + PAD, width), BF16),
            pltpu.HBM((share, width), F32),
            pltpu.HBM((share, width), F32),
            shape((8, width), F32),
        ],
        grid_spec=pltpu.PrefetchScalarGridSpec(
            num_scalar_prefetch=1,
            grid=(items,),
            in_specs=[row_block(width)]
            + [row_block(hw)] * 3
            + [whole((hw, width))] * 3
            + [whole(vec_in.shape), whole(low_in.shape)],
            out_specs=[
                whole((2 * share + PAD, width)),
                whole((share, width)),
                whole((share, width)),
                whole((8, width)),
            ],
            scratch_shapes=[pltpu.VMEM((rows, width), F32)],
        ),
        **params("normed_back", 6 * rows * width * hw, 8 * rows * width),
    )(lengths, *in_hbm(rows2d, dq, dk, dv, query_w, key_w, value_w, vec_in, low_in))


def load_all(pairs, sems):
    copies = [pltpu.make_async_copy(source, target, sems.at[i]) for i, (source, target) in enumerate(pairs)]
    for copy in copies:
        copy.start()
    return copies


def halves(count):
    return [slice(start, start + count // 2) for start in range(0, count, count // 2)]


def project_kernel(near_ref, far_ref, own_ref, pack_ref, out_ref):
    hw = own_ref.shape[0]
    for cols in tiles(out_ref.shape[1]):
        out_ref[:, cols] = (dot(near_ref[...], own_ref[:, cols]) + dot(far_ref[...], pack_ref[:hw, cols])).astype(BF16)


def project(near, far, own, pack):
    span, hw = near.shape
    width = own.shape[1]
    return pl.pallas_call(
        project_kernel,
        out_shape=shape((span, width), BF16),
        in_specs=[vmem()] * 4,
        out_specs=vmem(),
        **params("project", 4 * span * width * hw, 4 * span * width),
    )(near, far, *in_hbm(own), pack)


def quad_pairs(own_ref, parts, buf, begin=0):
    rows = own_ref.shape[0] // 4
    mine = lax.axis_index("dp") % 4
    pairs = [(own_ref, buf.at[0])]
    for index, part in enumerate(parts):
        count = rows // 2 if len(parts) == 5 and index > 2 else rows
        start = (mine ^ min(index, 3)) * rows + (count if index == 4 else 0)
        pairs.append((part.at[pl.ds(begin, count), :], buf.at[1, pl.ds(pl.multiple_of(start, 32), count), :]))
    return pairs


def conv_pairs(conv_ref, parts, wc):
    return quad_pairs(conv_ref, parts, wc, parts[0].shape[0] - conv_ref.shape[0] // 4)


def cot_pairs(cot_ref, far_cot, cots):
    span = cots.shape[1]
    start = pl.multiple_of(chip_half() * span, PIECE)
    return [(cot_ref.at[pl.ds(start, span), :], cots.at[0]), (far_cot, cots.at[1])]


def expand_kernel(tok_ref, vec_ref, part_ref, other_ref, out_far, up_ref, *rest):
    up_parts = rest[:5]
    mid_ref, normed_ref, act_ref, slope_ref, wu, tok_buf, sems = rest[5:]
    span, width = mid_ref.shape
    start = pl.multiple_of(chip_half() * span, PIECE)
    copies = load_all([(tok_ref.at[pl.ds(start, span), :], tok_buf)] + quad_pairs(up_ref, up_parts, wu), sems)
    copies[0].wait()

    def add_rows(index, rows):
        mid = tok_buf[rows, :].astype(F32) + vec_ref[row(OUT_B), :] + part_ref[rows, :].astype(F32) + other_ref[rows, :].astype(F32)
        mid_ref[rows, :] = mid
        normal, unused = norm_stats(mid)
        normed_ref[rows, :] = (normal * vec_ref[row(GAIN_MLP), :] + vec_ref[row(BIAS_MLP), :]).astype(BF16)

    over_pieces(span, add_rows)
    for copy in copies[1:]:
        copy.wait()
    hw = out_far.shape[0] - PAD

    def body(step, carry):
        block = step % 2
        rows = pl.ds(pl.multiple_of(step // 2 * (span // 2), PIECE), span // 2)
        for cols in tiles(width):
            own_bias, other_bias = vec_ref[row(UP_B), cols], out_far[hw:, cols].astype(F32)[0:1]
            preact = dot(normed_ref[rows, :], wu[block, :, cols]) + jnp.where(block == 0, own_bias, other_bias)
            normal_cdf = 0.5 * lax.erf(preact * (0.5**0.5)) + 0.5
            density = jnp.exp(preact * preact * -0.5) * 0.3989422804014327
            act_ref[block, rows, cols] = (preact * normal_cdf).astype(BF16)
            slope_ref[block, rows, cols] = (normal_cdf + preact * density).astype(BF16)
        return carry

    lax.fori_loop(0, 4, body, 0)


def expand(rows2d, vecs, part, other, out_far, up_w, up_parts):
    span, width = part.shape
    return pl.pallas_call(
        expand_kernel,
        out_shape=[
            shape((span, width), F32),
            shape((span, width), BF16),
            shape((2, span, width), BF16),
            shape((2, span, width), BF16),
        ],
        in_specs=[anywhere()] + [vmem()] * 4 + [anywhere()] * 6,
        out_specs=[vmem()] * 4,
        scratch_shapes=[
            pltpu.VMEM((2, width, width), BF16),
            pltpu.VMEM((span, width), BF16),
            pltpu.SemaphoreType.DMA((7,)),
        ],
        **params("expand", 4 * span * width * width, 14 * width * width),
    )(*in_hbm(rows2d, vecs), part, other, *in_hbm(out_far, up_w, *up_parts))


def contract_kernel(act_ref, down_ref, *rest):
    down_parts = rest[:4]
    out_ref, wd, sems = rest[4:]
    for copy in load_all(quad_pairs(down_ref, down_parts, wd), sems):
        copy.wait()
    for cols in tiles(out_ref.shape[1]):
        out_ref[:, cols] = (dot(act_ref[0], wd[0, :, cols]) + dot(act_ref[1], wd[1, :, cols])).astype(BF16)


def contract(act, down_w, down_parts):
    unused, span, width = act.shape
    return pl.pallas_call(
        contract_kernel,
        out_shape=shape((span, width), BF16),
        in_specs=[vmem()] + [anywhere()] * 5,
        out_specs=vmem(),
        scratch_shapes=[pltpu.VMEM((2, width, width), BF16), pltpu.SemaphoreType.DMA((5,))],
        **params("contract", 4 * span * width * width, 8 * width * width),
    )(act, *in_hbm(down_w, *down_parts))


def piece_place(info_ref, items, seq, span, index):
    piece = chip_half() * (span // PIECE) + index
    per_item = seq // PIECE
    item = piece // per_item
    length = info_ref[item]
    slot = lax.broadcasted_iota(jnp.int32, (PIECE, 1), 0) + (piece % per_item) * PIECE
    return item, length, (slot < length).astype(F32)


def convolve_kernel(items, seq, info_ref, vec_ref, mid_ref, part_ref, other_ref, conv_ref, *rest):
    parts, (cot_ref, far_cot) = rest[:4], rest[4:6]
    low_ref, z_ref, sums_ref, wc, cots, sems = rest[6:]
    span, width = mid_ref.shape
    block = wc.shape[1]
    copies = load_all(conv_pairs(conv_ref, parts, wc) + cot_pairs(cot_ref, far_cot, cots), sems)
    low_ref[...] = (
        mid_ref[...] + vec_ref[row(DOWN_B), :] + part_ref[...].astype(F32) + other_ref[...].astype(F32)
    ).astype(BF16)
    for copy in copies:
        copy.wait()
    sums_ref[...] = jnp.zeros_like(sums_ref)
    for k in range(2):
        z_ref[k] = dot_cols(low_ref[...], wc[k])

        def add_sums(index, rows):
            item, unused, mask = piece_place(info_ref, items, seq, span, index)
            z = z_ref[k, rows, :]
            masked = z * mask
            upstream = cots[k, rows, :].astype(F32) * mask
            lines = [
                jnp.sum(part, axis=0, keepdims=True) for part in (masked, masked * z, upstream, upstream * z)
            ]
            total = jnp.concatenate(lines, axis=0)
            for base in range(0, block, CH):
                sums_ref[item] += total[:, base : base + CH]

        over_pieces(span, add_sums)


def convolve(info, vecs, mid, part, other, conv_w, parts, cot_rows, far_cot, items, seq):
    span, width = mid.shape
    block = cot_rows.shape[1]
    return pl.pallas_call(
        functools.partial(convolve_kernel, items, seq),
        out_shape=[shape((span, width), BF16), shape((2, span, block), F32), shape((items, 4, CH), F32)],
        in_specs=[smem()] + [vmem()] * 4 + [anywhere()] * 7,
        out_specs=[vmem()] * 3,
        scratch_shapes=[
            pltpu.VMEM((2, block, width), BF16),
            pltpu.VMEM((2, span, block), BF16),
            pltpu.SemaphoreType.DMA((7,)),
        ],
        **params("convolve", 4 * span * width * block, 14 * width * width),
    )(info, *in_hbm(vecs), mid, part, other, *in_hbm(conv_w, *parts, cot_rows, far_cot))


def norm_back_kernel(items, seq, norm_at, info_ref, norm_ref, tot_ref, got_ref, z_ref, conv_ref, *rest):
    parts, (cot_ref, far_cot) = rest[:4], rest[4:6]
    near_ref, far_ref, dz_ref, out_ref, sums_ref, wc, cots, sems = rest[6:]
    span, width = out_ref.shape
    block = z_ref.shape[2]
    copies = load_all(conv_pairs(conv_ref, parts, wc) + cot_pairs(cot_ref, far_cot, cots), sems)
    scale = norm_ref[row(MIXED), norm_at : norm_at + CH]
    shift = norm_ref[row(MIXED), norm_at + CH : norm_at + 2 * CH]

    def item_terms(item, length):
        count = (8 * length).astype(F32)
        total = tot_ref[item] + got_ref[item]
        center = total[0:1] / count
        spread = lax.rsqrt(total[1:2] / count - center * center + EPSILON)
        plain = total[2:3]
        cross = spread * (total[3:4] - center * plain)
        return count, center, spread, plain, cross

    sums_ref[...] = jnp.zeros_like(sums_ref)
    for item in range(items):
        unused, unused, unused, plain, cross = item_terms(item, info_ref[item])
        sums_ref[0:1, :CH] += cross
        sums_ref[0:1, CH : 2 * CH] += plain
    for copy in copies:
        copy.wait()

    def back_rows(index, rows):
        item, length, mask = piece_place(info_ref, items, seq, span, index)
        count, center, spread, plain, cross = item_terms(item, length)
        terms = [center, spread, plain / count, cross / count, scale, shift, spread * scale]
        wide = [jnp.concatenate([t] * (block // CH), axis=1) for t in terms]
        center, spread, plain, cross, scale_w, shift_w, factor = wide
        for k, vol_ref in enumerate((near_ref, far_ref)):
            normal = (z_ref[k, rows, :] - center) * spread
            vol_ref[rows, :] = (mask * (scale_w * normal + shift_w)).astype(BF16)
            upstream = cots[k, rows, :].astype(F32)
            dz_ref[k, rows, :] = (mask * factor * (upstream - plain - normal * cross)).astype(BF16)

    over_pieces(span, back_rows)
    for cols in tiles(width):
        out_ref[:, cols] = (dot(dz_ref[0], wc[0, :, cols]) + dot(dz_ref[1], wc[1, :, cols])).astype(BF16)


def norm_back(info, vecs, total, got, z, conv_w, parts, cot_rows, far_cot, items, seq, norm_at):
    unused, span, block = z.shape
    width = conv_w.shape[1]
    return pl.pallas_call(
        functools.partial(norm_back_kernel, items, seq, norm_at),
        out_shape=[
            shape((span, block), BF16),
            shape((span, block), BF16),
            shape((2, span, block), BF16),
            shape((span, width), BF16),
            shape((8, width), F32),
        ],
        in_specs=[smem()] + [vmem()] * 4 + [anywhere()] * 7,
        out_specs=[vmem()] * 5,
        scratch_shapes=[
            pltpu.VMEM((2, block, width), BF16),
            pltpu.VMEM((2, span, block), BF16),
            pltpu.SemaphoreType.DMA((7,)),
        ],
        **params("norm_back", 4 * span * width * block, 6 * width * width),
    )(info, *in_hbm(vecs), total, got, z, *in_hbm(conv_w, *parts, cot_rows, far_cot))


def mlp_back_kernel(part_ref, other_ref, slope_ref, up_ref, down_ref, *rest):
    up_parts, down_parts = rest[:5], rest[5:9]
    du_ref, out_ref, sums_ref, up_sums, low_ref, wu, wd, sems = rest[9:]
    span, width = out_ref.shape
    copies = load_all(quad_pairs(down_ref, down_parts, wd) + quad_pairs(up_ref, up_parts, wu), sems)
    sums_ref[...] = jnp.zeros_like(sums_ref)
    up_sums[...] = jnp.zeros_like(up_sums)
    for rows in halves(span):
        grad = part_ref[rows, :].astype(F32) + other_ref[rows, :].astype(F32)
        low_ref[rows, :] = grad.astype(BF16)
        sums_ref[0:1, :] += jnp.sum(grad, axis=0, keepdims=True)
    for copy in copies[:5]:
        copy.wait()

    def body(step, carry):
        block = step % 2
        rows = pl.ds(pl.multiple_of(step // 2 * (span // 2), PIECE), span // 2)
        for cols in tiles(width):
            grad = dot_cols(low_ref[rows, :], wd[block, cols, :]) * slope_ref[block, rows, cols].astype(F32)
            low = grad.astype(BF16)
            du_ref[block, rows, cols] = low
            up_sums[block, 0:1, cols] += jnp.sum(low.astype(F32), axis=0, keepdims=True)
        return carry

    lax.fori_loop(0, 4, body, 0)
    for copy in copies[5:]:
        copy.wait()
    for cols in tiles(width):
        out_ref[:, cols] = (dot_cols(du_ref[0], wu[0, cols, :]) + dot_cols(du_ref[1], wu[1, cols, :])).astype(BF16)


def mlp_back(part, other, slope, up_w, down_w, up_parts, down_parts):
    span, width = part.shape
    return pl.pallas_call(
        mlp_back_kernel,
        out_shape=[
            shape((2, span, width), BF16),
            shape((span, width), BF16),
            shape((8, width), F32),
            shape((2, 8, width), F32),
        ],
        in_specs=[vmem()] * 3 + [anywhere()] * 11,
        out_specs=[vmem()] * 4,
        scratch_shapes=[
            pltpu.VMEM((span, width), BF16),
            pltpu.VMEM((2, width, width), BF16),
            pltpu.VMEM((2, width, width), BF16),
            pltpu.SemaphoreType.DMA((11,)),
        ],
        **params("mlp_back", 8 * span * width * width, 20 * width * width),
    )(part, other, slope, *in_hbm(up_w, down_w, *up_parts, *down_parts))


def mid_back_kernel(share, vec_ref, mid_ref, part_ref, other_ref, grad_ref, got_ref, out_w, pack_ref, *rest):
    near_ref, far_ref, em_ref, mine_ref, sums_ref, dmid_ref = rest
    span, width = mid_ref.shape
    sums_ref[...] = jnp.zeros_like(sums_ref)

    def back_rows(index, rows):
        normal, inverse = norm_stats(mid_ref[rows, :])
        grad = grad_ref[rows, :].astype(F32) + got_ref[rows, :].astype(F32)
        dmid = part_ref[rows, :].astype(F32) + other_ref[rows, :].astype(F32)
        dmid += norm_backward(grad, normal, inverse, vec_ref[row(GAIN_MLP), :])
        dmid_ref[rows, :] = dmid
        em_ref[rows, :] = dmid.astype(BF16)
        sums_ref[0:1, :] += jnp.sum(grad * normal, axis=0, keepdims=True)
        sums_ref[1:2, :] += jnp.sum(grad, axis=0, keepdims=True)
        sums_ref[2:3, :] += jnp.sum(dmid, axis=0, keepdims=True)

    over_pieces(span, back_rows)
    far_ref[...] = dot_cols(em_ref[...], pack_ref[: out_w.shape[0], :]).astype(BF16)
    near_ref[...] = dot_cols(em_ref[...], out_w[...]).astype(BF16)
    mine_ref[...] = dmid_ref[pl.ds(pl.multiple_of(lax.axis_index("mp") % 2 * share, PIECE), share), :]


def mid_back(vecs, mid, part, other, grad, got, out_w, pack):
    span, width = mid.shape
    hw = out_w.shape[0]
    return pl.pallas_call(
        functools.partial(mid_back_kernel, span // 2),
        out_shape=[
            shape((span, hw), BF16),
            shape((span, hw), BF16),
            shape((span, width), BF16),
            shape((span // 2, width), F32),
            shape((8, width), F32),
        ],
        in_specs=[vmem()] * 8,
        out_specs=[vmem()] * 5,
        scratch_shapes=[pltpu.VMEM((span, width), F32)],
        **params("mid_back", 4 * span * width * hw, 12 * width * width),
    )(*in_hbm(vecs), mid, part, other, grad, got, *in_hbm(out_w, pack))


LINKS = {"y": ("mp", 2), "x": ("dp", 1), "z": ("dp", 2)}


class Lane:
    def __init__(self, blocks, rows, parts, link):
        self.blocks, self.rows, self.parts, self.link = blocks, rows, parts, link


class Kept:
    def __init__(self, blocks, rows, array, link, place):
        self.blocks, self.rows, self.array, self.link, self.place = blocks, rows, array, link, place


def high_of(link):
    axis, bit = LINKS[link]
    return (lax.axis_index(axis) // bit) % 2


def aligned(value, rows):
    return value if isinstance(value, int) else pl.multiple_of(value, rows & -rows)


def product_rows(left, right, block, out_ref, at):
    size = left.shape[-1]
    for base in range(0, size, TILE):
        cols = slice(base, min(base + TILE, size))
        lhs = left[block, :, cols] if len(left.shape) == 3 else left[:, cols]
        rhs = right[block] if len(right.shape) == 3 else right[...]
        out_ref[at + base : at + cols.stop, :] = dot_rows(lhs, rhs).astype(BF16)


def products_kernel(lefts, *refs):
    right, out_ref = refs[-2:]
    size = out_ref.shape[0] // 2
    for block in range(2):
        product_rows(refs[block] if lefts == 2 else refs[0], right, block, out_ref, block * size)


def products(name, lefts, right):
    span, width = right.shape[-2:]
    size = lefts[0].shape[-1]
    return pl.pallas_call(
        functools.partial(products_kernel, len(lefts)),
        out_shape=shape((2 * size, width), BF16),
        in_specs=[vmem()] * (len(lefts) + 1),
        out_specs=vmem(),
        **params(name, 4 * span * size * width, 8 * size * width),
    )(*lefts, right)


def emit_kernel(count, inputs, lanes, links, *refs):
    lefts, rights = refs[:count], refs[count : 2 * count]
    sources = list(refs[2 * count : 2 * count + inputs])
    outs = refs[2 * count + inputs :]
    if count:
        product, outs = outs[-1], outs[:-1]
        sources = [product] + sources
        total = product.shape[0] // 2
        begin = 0
        for left, right in zip(lefts, rights):
            for block in range(2):
                product_rows(left, right, block, product, block * total + begin)
            begin += left.shape[-1]
    sends = dict(zip(links, outs))
    kept = iter(outs[len(links) :])
    last = outs[-1]
    places = dict.fromkeys(list(links) + [None], 0)

    for lane in lanes:

        def total_of(block, start, size):
            values = [
                sources[index][pl.ds(aligned(base + block * stride + start, size), size), :]
                for index, base, stride in lane.parts
            ]
            if len(values) == 1:
                return values[0]
            return (values[0].astype(F32) + values[1].astype(F32)).astype(BF16)

        place = places[lane.link]
        if lane.link is None:
            last[place : place + lane.rows, :] = total_of(0, 0, lane.rows)
            places[None] += lane.rows
            continue
        send, keep = sends[lane.link], next(kept)
        if lane.link == "y":
            send[place : place + lane.rows, :] = total_of(1, 0, lane.rows)
            keep[...] = total_of(0, 0, lane.rows)
            places["y"] += lane.rows
            continue
        half = lane.rows // 2
        high = high_of(lane.link)
        for block in range(lane.blocks):
            rows = slice(block * half, (block + 1) * half)
            keep[rows, :] = total_of(block, high * half, half)
            send[place + rows.start : place + rows.stop, :] = total_of(block, (1 - high) * half, half)
        places[lane.link] += lane.blocks * half


def emit(name, lefts, rights, inputs, lanes, width, far=False):
    places = dict.fromkeys(list(LINKS) + [None], 0)
    kept = []
    for lane in lanes:
        sent = lane.blocks * lane.rows // 2 if lane.link else lane.rows
        if lane.link:
            blocks, rows = (1, lane.rows) if lane.link == "y" else (lane.blocks, lane.rows // 2)
            kept.append(Kept(blocks, rows, None, lane.link, places[lane.link]))
        places[lane.link] += sent
    links = [link for link in LINKS if places[link]]
    out_rows = [places[link] for link in links] + [k.blocks * k.rows for k in kept]
    if places[None]:
        out_rows.append(places[None])
    size = sum(left.shape[-1] for left in lefts)
    span = rights[0].shape[-2] if rights else 0
    results = pl.pallas_call(
        functools.partial(emit_kernel, len(lefts), len(inputs), lanes, links),
        out_shape=[
            pltpu.HBM((rows, width), BF16) if far and len(links) <= i < len(links) + len(kept) else shape((rows, width), BF16)
            for i, rows in enumerate(out_rows)
        ],
        in_specs=[vmem()] * (2 * len(lefts) + len(inputs)),
        out_specs=[vmem()] * len(out_rows),
        scratch_shapes=[pltpu.VMEM((2 * size, width), BF16)] if lefts else [],
        **params(name, 4 * span * size * width, 8 * size * width),
    )(*lefts, *rights, *inputs)
    for keep, array in zip(kept, results[len(links) :]):
        keep.array = array
        keep.far = far
    return dict(zip(links, results)), kept, results[-1] if places[None] else None


def send_all(sends):
    return {link: swap(value, *LINKS[link]) for link, value in sends.items()}


def turn(name, kept, got, links, width, fresh=(), far=False):
    inputs = [k.array for k in kept] + list(got.values()) + [lane[0] for lane in fresh]
    inputs = [in_hbm(v)[0] if k.far else v for k, v in zip(kept, inputs)] + inputs[len(kept) :]
    came = {link: len(kept) + i for i, link in enumerate(got)}
    lanes = []
    for i, (k, link) in enumerate(zip(kept, links)):
        lanes.append(Lane(k.blocks, k.rows, [(i, 0, k.rows), (came[k.link], k.place, k.rows)], link))
    for i, (lane, link) in enumerate(zip(fresh, links[len(kept) :])):
        lanes.append(Lane(lane[3], lane[4], [(len(kept) + len(got) + i, lane[1], lane[2])], link))
    return emit(name, [], [], inputs, lanes, width, far)


def spread_kernel(lanes, cuts, flip, *refs):
    first, gots, outs, total = refs[0], refs[1:5], refs[5:-1], refs[-1]
    bits = {"x": high_of("x"), "z": high_of("z")}
    places = [0, 0]
    sizes = [sum(lane[1] for lane in lanes if lane[3] == group) for group in range(2)]
    for base, rows, order, group in lanes:
        at = places[group]
        places[group] += rows
        near, far = ("z", "x") if group == 0 else ("x", "z")
        got_near, got_far = gots[2 * group], gots[2 * group + 1]
        offset = at + (sizes[0] if group else 0)
        pieces = [
            (first[offset : offset + rows, :], ()),
            (got_near[at : at + rows, :], (near,)),
            (got_far[at : at + rows, :], (far,)),
            (got_far[sizes[group] + at : sizes[group] + at + rows, :], (near, far)),
        ]
        for value, flipped in pieces:
            index = [1 - bits[link] if link in flipped else bits[link] for link in order]
            start = base + (index[0] * 2 + index[1]) * rows
            total[pl.ds(aligned(start, rows), rows), :] = value.astype(F32)
    begin = 0
    for i, (out, size) in enumerate(zip(outs, cuts)):
        value = total[begin : begin + size, :]
        out[...] = value.T if i in flip else value
        begin += size


def spread(name, lanes, cuts, flip, first, gots):
    width = first.shape[1]
    return pl.pallas_call(
        functools.partial(spread_kernel, lanes, cuts, flip),
        out_shape=[shape((width, size) if i in flip else (size, width), F32) for i, size in enumerate(cuts)],
        in_specs=[vmem()] * 5,
        out_specs=[vmem()] * len(cuts),
        scratch_shapes=[pltpu.VMEM((sum(cuts), width), F32)],
        **params(name, 0, 8 * sum(cuts) * width),
    )(first, *gots)


def pass_kernel(passed_ref, got_ref, sums_ref, up_ref, send_ref, whole_ref):
    share = passed_ref.shape[0]
    send_ref[:share, :] = (passed_ref[...] + got_ref[share : 2 * share, :].astype(F32)).astype(BF16)
    whole = sums_ref[0:VECTORS, :].astype(BF16).astype(F32) + got_ref[2 * share :, :].astype(F32)[0:VECTORS]
    whole = whole.astype(BF16).astype(F32)
    zero = jnp.zeros((1, whole.shape[1]), F32)
    send_ref[share:, :] = jnp.concatenate([whole, up_ref[1, 0:1, :], zero], axis=0).astype(BF16)
    whole_ref[...] = jnp.concatenate([whole, up_ref[0, 0:1, :], zero], axis=0)


def pass_on(passed, got, sums, up_sums):
    share, width = passed.shape
    return pl.pallas_call(
        pass_kernel,
        out_shape=[shape((share + 8, width), BF16), shape((8, width), F32)],
        in_specs=[vmem()] * 4,
        out_specs=[vmem()] * 2,
        **params("pass_on", 0, 8 * share * width),
    )(*in_hbm(passed), got, sums, up_sums)


def finish_kernel(tok_ref, vec_ref, own_ref, got_ref, last_ref, mine_ref, out_ref, tok_buf, sem):
    share = out_ref.shape[0]
    start = pl.multiple_of(lax.axis_index("mp") * share, PIECE)
    copy = pltpu.make_async_copy(tok_ref.at[pl.ds(start, share), :], tok_buf, sem)
    copy.start()
    copy.wait()

    def back_rows(index, rows):
        normal, inverse = norm_stats(tok_buf[rows, :].astype(F32))
        grad = own_ref[rows, :] + got_ref[rows, :].astype(F32) + last_ref[rows, :].astype(F32)
        out_ref[rows, :] = mine_ref[rows, :] + norm_backward(grad, normal, inverse, vec_ref[row(GAIN_ATTN), :])

    over_pieces(share, back_rows)


def finish(rows2d, vecs, own, got, last, mine):
    share, width = own.shape
    return pl.pallas_call(
        finish_kernel,
        out_shape=shape((share, width), F32),
        in_specs=[anywhere()] + [vmem()] * 5,
        out_specs=vmem(),
        scratch_shapes=[pltpu.VMEM((share, width), BF16), pltpu.SemaphoreType.DMA],
        **params("finish", 0, 14 * share * width),
    )(*in_hbm(rows2d, vecs, own), got, last, *in_hbm(mine))


def add_low(left, right):
    return (left.astype(F32) + right.astype(F32)).astype(BF16)


def bit_of(axis, bit):
    return (lax.axis_index(axis) // bit) % 2


def take_half(value, high):
    half = value.shape[0] // 2
    return lax.dynamic_slice_in_dim(value, high * half, half, 0)


def put_half(mine, other, high):
    return jnp.concatenate([jnp.where(high > 0, other, mine), jnp.where(high > 0, mine, other)], axis=0)


def late_bits():
    bits = []
    bit = 4
    while bit < lax.axis_size("dp"):
        bits.append(bit)
        bit *= 2
    return bits


def finish_reduce(current, bit):
    high = bit_of("dp", bit)
    return add_low(take_half(current, high), swap(take_half(current, 1 - high), "dp", bit))


def finish_gather(current, bit):
    return put_half(current, swap(current, "dp", bit), bit_of("dp", bit))


def shards(
    tokens, lengths, gain_attn, bias_attn, query_w, query_b, key_w, value_w, value_b, out_w, out_b, gain_mlp, bias_mlp,
    up_w, up_b, down_w, down_b, deconv_w, scale_norm, shift_norm, cotangent
):
    items, seq, width = tokens.shape
    rows = items * seq
    me = lax.axis_index("mp")
    share = rows // lax.axis_size("mp")
    span = rows // 2
    hw = query_w.shape[1]
    rows2d = tokens.reshape(rows, width)
    side = bit_of("dp", 1)
    chip = bit_of("mp", 2)
    mixed = jnp.concatenate([query_b, value_b, scale_norm, shift_norm])
    mixed = jnp.pad(mixed, (0, width - mixed.shape[0]))
    vecs = jnp.concatenate([out_b, gain_mlp, bias_mlp, down_b, gain_attn, bias_attn, up_b, mixed])
    vecs = vecs.astype(F32).reshape(8, width)
    weights = [query_w.T, key_w.T, value_w.T]
    conv_w = deconv_w.T

    quarter = width // 4
    mine = lax.axis_index("dp") % 4

    def quarter_of(weight, index):
        count = weight.shape[0] // 4
        return lax.dynamic_slice_in_dim(weight, index * count, count, 0)

    def low_quarter(index):
        return jnp.concatenate([quarter_of(down_w, index), quarter_of(conv_w, index)], axis=0)

    bias_rows = jnp.broadcast_to(up_b[None, :], (PAD, width))
    out_far = swap(jnp.concatenate([out_w, bias_rows], axis=0), "mp", 2)
    up_part = swap(quarter_of(up_w, mine), "mp", 2)
    low_part = swap(low_quarter(mine), "mp", 2)

    normed, q, k, v, lse, near, other = attend(lengths, rows2d, vecs, *weights, items, seq)
    out_far, near, other, up_part, low_part = join(out_far, near, other, up_part, low_part)
    far = swap(other, "mp", 2)
    up_parts = [up_part, swap(up_part, "dp", 1), swap(up_part, "dp", 2)]
    cot_rows = cotangent.reshape(rows, -1)
    cot_sent = lax.dynamic_slice_in_dim(cot_rows, (1 - chip) * span, span, 0)
    low_sent = low_quarter(mine ^ 3)
    far, low_part, low_sent, cot_sent, *up_parts = join(far, low_part, low_sent, cot_sent, *up_parts)
    low_last = swap(low_sent, "mp", 2)
    last_half = quarter // 2
    up_parts.append(swap(up_parts[2][:last_half], "dp", 1))
    up_parts.append(swap(up_parts[1][last_half:], "dp", 2))

    part = project(near, far, out_w, out_far)
    part_got = swap(part, "mp", 1)
    part_got, low_part, cot_sent, *up_parts = join(part_got, low_part, cot_sent, *up_parts)
    down_parts = [low_part, swap(low_part, "dp", 1), swap(low_part, "dp", 2)]
    far_cot = swap(cot_sent, "mp", 2)
    mid, normed_two, act, slope = expand(rows2d, vecs, part, part_got, out_far, up_w, up_parts)
    act, low_last, *down_parts = join(act, low_last, *down_parts)
    down_parts.append(low_last)
    part = contract(act, down_w, down_parts)
    part, far_cot = join(part, far_cot)
    low, z, sums = convolve(
        lengths, vecs, mid, part, swap(part, "mp", 1), conv_w, down_parts, cot_rows, far_cot, items, seq
    )
    sums = sums + swap(sums, "mp", 1)
    vol_near, vol_far, dz, grad, norm_sums = norm_back(
        lengths, vecs, sums, swap(sums, "mp", 2), z, conv_w, down_parts, cot_rows, far_cot, items, seq, 2 * hw
    )
    grad_got = swap(grad, "mp", 1)
    conv_raw = products("conv_grad", [dz], low)
    grad_got, conv_raw = join(grad_got, conv_raw)
    block = conv_w.shape[0]
    half = block // 2
    third = width // 3
    lanes = [Lane(2, third, [(0, i * third, width)], link) for i, link in enumerate("yxz")]
    sends, kept, unused = emit("down_grad", [act], [add_low(grad, grad_got)], [], lanes, width)
    grad_got, sends["y"], sends["x"], sends["z"] = join(grad_got, sends["y"], sends["x"], sends["z"])
    came = send_all(sends)
    du, back, low_sums, up_sums = mlp_back(grad, grad_got, slope, up_w, down_w, up_parts, down_parts)
    back, came["y"], came["x"], came["z"] = join(back, came["y"], came["x"], came["z"])
    back_got = swap(back, "mp", 1)
    up_raw = products("up_grad", [normed_two], du)
    fresh = [(conv_raw, 0, block, 2, half), (conv_raw, half, block, 2, half)]
    sends, kept, unused = turn("turn_one", kept, came, "xzyxz", width, fresh)
    back_got, up_raw, sends["y"], sends["x"], sends["z"] = join(back_got, up_raw, sends["y"], sends["x"], sends["z"])
    came = send_all(sends)
    do_near, do_far, em, dmid, vec_sums = mid_back(vecs, mid, grad, grad_got, back, back_got, out_w, out_far)
    do_far, em, came["y"] = join(do_far, em, came["y"])
    do_got = swap(do_far, "mp", 2)
    out_raw = products("out_grad", [near, far], em)
    out_raw, came["y"], came["x"], came["z"] = join(out_raw, came["y"], came["x"], came["z"])
    cut = width * 5 // 12
    fresh = [(up_raw, 0, width, 2, cut), (up_raw, cut, width, 2, cut), (up_raw, 2 * cut, width, 2, width - 2 * cut)]
    fresh.append((out_raw, 0, hw, 2, hw))
    sends, kept, unused = turn("turn_two", kept, came, "zyxzxyxzz", width, fresh, True)
    do_got, sends["y"], sends["x"], sends["z"] = join(do_got, sends["y"], sends["x"], sends["z"])
    came = send_all(sends)

    *dqkv, qkv_grad, bias_sums = attend_back(lengths, normed, q, k, v, lse, do_near, do_got, items, seq, share)
    qkv_grad, vol_far, came["y"], came["x"], came["z"], *dqkv = join(
        qkv_grad, vol_far, came["y"], came["x"], came["z"], *dqkv
    )
    cut = qkv_grad.shape[0] * 4 // 9
    fresh = [(qkv_grad, 0, 0, 1, cut), (qkv_grad, cut, 0, 1, qkv_grad.shape[0] - cut)]
    sizes = [k.blocks * k.rows for k in kept[:3]]
    links = [None] * 3 + ["y", "y", "x", "z", "y", "y", "x", "z"]
    sends, kept, first = turn("turn_three", kept, came, links, width, fresh, True)
    for bit in late_bits():
        first = finish_reduce(first, bit)
    came = send_all(sends)
    sent, own, passed, own_sums = normed_back(
        lengths, rows2d, *dqkv, *weights, vec_sums, low_sums, items, seq, share
    )
    first, sent, came["y"], came["x"], came["z"] = join(first, sent, came["y"], came["x"], came["z"])
    for bit in reversed(late_bits()):
        first = finish_gather(first, bit)
    got = swap(sent, "mp", 1)
    conv_sizes = [k.blocks * k.rows for k in kept[:2]]
    came = {link: in_hbm(value)[0] for link, value in came.items()}
    sends, kept, early = turn("turn_four", kept, came, [None, None] + list("zyxxzx"), width)
    came = send_all(sends)
    first, got, vol_far, came["y"], came["x"], came["z"] = join(first, got, vol_far, came["y"], came["x"], came["z"])
    kept = [kept[i] for i in (0, 1, 4, 2, 3, 5)]
    unused, unused, last = turn("turn_five", kept, came, [None] * 6, width)
    last_sizes = [k.blocks * k.rows for k in kept] + conv_sizes
    last = jnp.concatenate([last, early], axis=0)
    for bit in late_bits():
        last = finish_reduce(last, bit)
    edge = sizes[0] + sizes[1]
    sent_near = [first[:edge], first[edge:]]
    near_got = [swap(sent_near[0], "dp", 2), swap(sent_near[1], "dp", 1)]
    second, whole = pass_on(passed, got, own_sums, up_sums)
    second = swap(second, "mp", 2)
    far_got = [
        swap(jnp.concatenate([sent_near[0], near_got[0]], axis=0), "dp", 1),
        swap(jnp.concatenate([sent_near[1], near_got[1]], axis=0), "dp", 2),
    ]
    last, second, vol_far, *far_got = join(last, second, vol_far, *far_got)
    vol_got = swap(vol_far, "mp", 2)
    tokens_grad = finish(rows2d, vecs, own, got, second, dmid)
    for bit in reversed(late_bits()):
        last = finish_gather(last, bit)
    whole = (whole + second[share : share + 8].astype(F32))[: VECTORS + 1]
    lines = jnp.concatenate([whole, bias_sums[0:1], bias_sums[2:3], norm_sums[0:1]], axis=0)
    for bit in [1, 2] + late_bits():
        lines = lines + swap(lines, "dp", bit)
    (down_total,) = spread(
        "spread_one",
        [(0, sizes[0], "xz", 0), (third, sizes[1], "xz", 0), (2 * third, sizes[2], "zx", 1)],
        [width],
        [],
        first,
        [near_got[0], far_got[0], near_got[1], far_got[1]],
    )
    last, lines, down_total, tokens_grad = join(last, lines, down_total, tokens_grad)
    edge = sum(last_sizes[:3])
    sent_last = [last[:edge], last[edge:]]
    last_got = [swap(sent_last[0], "dp", 2), swap(sent_last[1], "dp", 1)]
    volume = put_half(vol_near, vol_got, chip).astype(F32)
    volume, *last_got = join(volume, *last_got)
    last_far = [
        swap(jnp.concatenate([sent_last[0], last_got[0]], axis=0), "dp", 1),
        swap(jnp.concatenate([sent_last[1], last_got[1]], axis=0), "dp", 2),
    ]
    base = width + hw
    up_cut = width * 5 // 12
    up_total, out_total, query_total, key_total, value_total, conv_total = spread(
        "spread_two",
        [
            (0, last_sizes[0], "xz", 0),
            (up_cut, last_sizes[1], "xz", 0),
            (base, last_sizes[2], "xz", 0),
            (2 * up_cut, last_sizes[3], "zx", 1),
            (width, last_sizes[4], "zx", 1),
            (base + cut, last_sizes[5], "zx", 1),
            (base + 3 * hw, last_sizes[6], "xz", 1),
            (base + 3 * hw + half, last_sizes[7], "zx", 1),
        ],
        [width, hw, hw, hw, hw, block],
        [5],
        last,
        [last_got[0], last_far[0], last_got[1], last_far[1]],
    )
    return (
        volume.reshape(items, seq, -1),
        tokens_grad,
        lines[0],
        lines[1],
        query_total.T,
        lines[VECTORS + 1, :hw],
        key_total.T,
        value_total.T,
        lines[VECTORS + 2, :hw],
        out_total,
        lines[4],
        lines[2],
        lines[3],
        up_total,
        lines[VECTORS],
        down_total,
        lines[5],
        conv_total,
        lines[VECTORS + 3, :CH],
        lines[VECTORS + 3, CH : 2 * CH],
    )


def solution(mesh):
    in_specs = (
        P("dp", None, None),
        P("dp"),
        P(),
        P(),
        P(None, "mp"),
        P("mp"),
        P(None, "mp"),
        P(None, "mp"),
        P("mp"),
        P("mp", None),
        P(),
        P(),
        P(),
        P(None, "mp"),
        P("mp"),
        P("mp", None),
        P(),
        P(None, "mp"),
        P(),
        P(),
        P("dp", None, "mp"),
    )
    out_specs = (
        P("dp", None, "mp"),
        P(("dp", "mp"), None),
        P(),
        P(),
        P(None, "mp"),
        P("mp"),
        P(None, "mp"),
        P(None, "mp"),
        P("mp"),
        P("mp", None),
        P(),
        P(),
        P(),
        P(None, "mp"),
        P("mp"),
        P("mp", None),
        P(),
        P(None, "mp"),
        P(),
        P(),
    )
    return jax.shard_map(shards, mesh=mesh, in_specs=in_specs, out_specs=out_specs, check_vma=False)
```

```python
import functools

import jax
import jax.numpy as jnp
from jax import lax
from jax.experimental import pallas as pl
from jax.experimental.pallas import tpu as pltpu
from jax.sharding import PartitionSpec as P

HEAD_DIM = 64
CH = 128
EPSILON = 1e-05
SCALE = HEAD_DIM ** (-0.5)
F32 = jnp.float32
BF16 = jnp.bfloat16
TILE = 256
PIECE = 128
PAD = 16
VECTORS = 6
OUT_B, GAIN_MLP, BIAS_MLP, DOWN_B, GAIN_ATTN, BIAS_ATTN, UP_B, MIXED = range(8)
COST = 1
MIB = 1024 * 1024


def dot(left, right):
    return jnp.dot(left, right, preferred_element_type=F32)


def dot_rows(left, right):
    return lax.dot_general(left, right, (((0,), (0,)), ((), ())), preferred_element_type=F32)


def dot_cols(left, right):
    return lax.dot_general(left, right, (((1,), (1,)), ((), ())), preferred_element_type=F32)


def swap(value, axis, bit):
    size = lax.axis_size(axis)
    return lax.ppermute(value, axis, [(i, i ^ bit) for i in range(size)])


def norm_stats(values):
    center = values - jnp.mean(values, axis=-1, keepdims=True)
    inverse = lax.rsqrt(jnp.mean(center * center, axis=-1, keepdims=True) + EPSILON)
    return center * inverse, inverse


def norm_backward(upstream, normal, inverse, gain_vec):
    scaled = upstream * gain_vec
    mean_part = jnp.mean(scaled, axis=-1, keepdims=True)
    mean_cross = jnp.mean(scaled * normal, axis=-1, keepdims=True)
    return inverse * (scaled - mean_part - normal * mean_cross)


def vmem():
    return pl.BlockSpec(memory_space=pltpu.VMEM)


def anywhere():
    return pl.BlockSpec(memory_space=pl.ANY)


def row(index):
    return slice(index, index + 1)


def smem():
    return pl.BlockSpec(memory_space=pltpu.SMEM)


def shape(dims, dtype):
    return jax.ShapeDtypeStruct(dims, dtype)


def join(*values):
    return lax.optimization_barrier(values)


def in_hbm(*values):
    return [pltpu.with_memory_space_constraint(value, pltpu.HBM) for value in values]


def params(name, flops, moved, mebibytes=24):
    return dict(
        compiler_params=pltpu.CompilerParams(vmem_limit_bytes=mebibytes * MIB),
        cost_estimate=pl.CostEstimate(flops=flops // COST, transcendentals=0, bytes_accessed=moved // COST),
        name=name,
    )


def over_pieces(count, step):
    def body(index, carry):
        step(index, pl.ds(pl.multiple_of(index * PIECE, PIECE), PIECE))
        return carry

    lax.fori_loop(0, count // PIECE, body, 0)


def head_cols(head):
    return slice(head * HEAD_DIM, (head + 1) * HEAD_DIM)


def tiles(width):
    return [slice(start, start + TILE) for start in range(0, width, TILE)]


def chip_half():
    return lax.axis_index("mp") // 2


def x_side():
    return lax.axis_index("dp") % 2


def attend_kernel(
    items, heads, span_rows, info_ref, tok_ref, vec_ref, qw_ref, kw_ref, vw_ref,
    normed_ref, q_ref, k_ref, v_ref, lse_ref, near_ref, other_ref, o_ref
):
    seq = tok_ref.shape[0]
    item = pl.program_id(0)
    length = info_ref[item]
    for start in range(0, seq, PIECE):
        rows = slice(start, start + PIECE)
        normal, unused = norm_stats(tok_ref[rows, :].astype(F32))
        normed_ref[rows, :] = (normal * vec_ref[row(GAIN_ATTN), :] + vec_ref[row(BIAS_ATTN), :]).astype(BF16)
    normed = normed_ref[...]
    hw = q_ref.shape[1]
    q_ref[...] = (dot_cols(normed, qw_ref[...]) + vec_ref[row(MIXED), :hw]).astype(BF16) * jnp.asarray(SCALE, BF16)
    k_ref[...] = dot_cols(normed, kw_ref[...]).astype(BF16)
    v_ref[...] = (dot_cols(normed, vw_ref[...]) + vec_ref[row(MIXED), hw : 2 * hw]).astype(BF16)

    def run(span):
        valid = lax.broadcasted_iota(jnp.int32, (span, span), 0) < length
        for head in range(heads):
            cols = head_cols(head)
            scores = jnp.where(valid, dot_cols(k_ref[:span, cols], q_ref[:span, cols]), -1e9)
            top = jnp.max(scores, axis=0, keepdims=True)
            raised = jnp.exp(scores - top)
            total = jnp.sum(raised, axis=0, keepdims=True)
            mixed = dot_rows(v_ref[:span, cols], raised.astype(BF16)) / total
            o_ref[pl.ds(pl.multiple_of(item * seq, seq), span), cols] = mixed.T.astype(BF16)
            lse_ref[0, head : head + 1, :span] = top + jnp.log(total)
        if span < seq:
            o_ref[pl.ds(pl.multiple_of(item * seq + span, span), seq - span), :] = jnp.zeros(
                (seq - span, heads * HEAD_DIM), BF16
            )

    half = seq // 2

    @pl.when(length <= half)
    def _():
        run(half)

    @pl.when(length > half)
    def _():
        run(seq)

    @pl.when(item == items - 1)
    def _():
        start = chip_half() * span_rows
        near_ref[...] = o_ref[pl.ds(pl.multiple_of(start, PIECE), span_rows), :]
        other_ref[...] = o_ref[pl.ds(pl.multiple_of(span_rows - start, PIECE), span_rows), :]


def attend(info, rows2d, vecs, query_w, key_w, value_w, items, seq):
    rows, width = rows2d.shape
    hw = query_w.shape[0]
    heads = hw // HEAD_DIM
    row_block = lambda cols: pl.BlockSpec((seq, cols), lambda i, n: (i, 0))
    whole = lambda dims: pl.BlockSpec(dims, lambda i, n: (0,) * len(dims))
    return pl.pallas_call(
        functools.partial(attend_kernel, items, heads, rows // 2),
        out_shape=[pltpu.HBM((rows, width), BF16)]
        + [pltpu.HBM((rows, hw), BF16)] * 3
        + [pltpu.HBM((items, 8, seq), F32)]
        + [shape((rows // 2, hw), BF16)] * 2,
        grid_spec=pltpu.PrefetchScalarGridSpec(
            num_scalar_prefetch=1,
            grid=(items,),
            in_specs=[row_block(width), whole(vecs.shape)] + [whole((hw, width))] * 3,
            out_specs=[row_block(width)]
            + [row_block(hw)] * 3
            + [pl.BlockSpec((1, 8, seq), lambda i, n: (i, 0, 0))]
            + [whole((rows // 2, hw))] * 2,
            scratch_shapes=[pltpu.VMEM((rows, hw), BF16)],
        ),
        **params("attend", 6 * rows * width * hw + 4 * rows * seq * hw, 4 * rows * width),
    )(info, *in_hbm(rows2d, vecs, query_w, key_w, value_w))


def attend_back_kernel(
    items, heads, share, len_ref, normed_ref, q_ref, k_ref, v_ref, lse_ref, near_ref, other_ref,
    dq_ref, dk_ref, dv_ref, grad_ref, sums_ref, do_ref, grad_acc
):
    seq = normed_ref.shape[0]
    hw = heads * HEAD_DIM
    item = pl.program_id(0)
    length = len_ref[item]

    @pl.when(item == 0)
    def _():
        begin = chip_half() * 2 * share
        do_ref[pl.ds(pl.multiple_of(begin, PIECE), 2 * share), :] = near_ref[...]
        do_ref[pl.ds(pl.multiple_of(2 * share - begin, PIECE), 2 * share), :] = other_ref[...]
        sums_ref[...] = jnp.zeros_like(sums_ref)
        grad_acc[...] = jnp.zeros_like(grad_acc)

    def run(span):
        valid = lax.broadcasted_iota(jnp.int32, (span, span), 0) < length
        for head in range(heads):
            cols = head_cols(head)
            query, keys, vals = q_ref[:span, cols], k_ref[:span, cols], v_ref[:span, cols]
            upstream = do_ref[pl.ds(pl.multiple_of(item * seq, seq), span), cols]
            scores = jnp.where(valid, dot_cols(keys, query), -1e9)
            prob = jnp.exp(scores - lse_ref[0, head : head + 1, :span])
            dv_ref[:span, cols] = dot(prob.astype(BF16), upstream).astype(BF16)
            prob_grad = dot_cols(vals, upstream)
            product = prob * prob_grad
            row_term = jnp.sum(product, axis=0, keepdims=True)
            score_grad = (product - prob * row_term).astype(BF16)
            dk_ref[:span, cols] = dot(score_grad, query).astype(BF16)
            dq_ref[:span, cols] = (dot_rows(keys, score_grad) * SCALE).T.astype(BF16)
        for index, ref in enumerate((dq_ref, dk_ref, dv_ref)):
            grad_acc[index * hw : (index + 1) * hw, :] += dot_rows(ref[:span, :], normed_ref[:span, :])
            if index != 1:
                sums_ref[row(index), :hw] += jnp.sum(ref[:span, :].astype(F32), axis=0, keepdims=True)
            if span < seq:
                ref[span:, :] = jnp.zeros((seq - span, hw), BF16)

    half = seq // 2

    @pl.when(length <= half)
    def _():
        run(half)

    @pl.when(length > half)
    def _():
        run(seq)

    @pl.when(item == items - 1)
    def _():
        grad_ref[...] = grad_acc[...].astype(BF16)


def attend_back(lengths, normed, q, k, v, lse, near, other, items, seq, share):
    rows, width = normed.shape
    hw = q.shape[1]
    heads = hw // HEAD_DIM
    row_block = lambda cols: pl.BlockSpec((seq, cols), lambda i, n: (i, 0))
    whole = lambda dims: pl.BlockSpec(dims, lambda i, n: (0,) * len(dims))
    return pl.pallas_call(
        functools.partial(attend_back_kernel, items, heads, share),
        out_shape=[pltpu.HBM((rows, hw), BF16)] * 3 + [shape((3 * hw, width), BF16), shape((8, width), F32)],
        grid_spec=pltpu.PrefetchScalarGridSpec(
            num_scalar_prefetch=1,
            grid=(items,),
            in_specs=[row_block(width)]
            + [row_block(hw)] * 3
            + [pl.BlockSpec((1, 8, seq), lambda i, n: (i, 0, 0))]
            + [whole((2 * share, hw))] * 2,
            out_specs=[row_block(hw)] * 3 + [whole((3 * hw, width)), whole((8, width))],
            scratch_shapes=[pltpu.VMEM((rows, hw), BF16), pltpu.VMEM((3 * hw, width), F32)],
        ),
        **params("attend_back", 6 * rows * width * hw + 10 * rows * seq * hw, 8 * rows * width),
    )(lengths, *in_hbm(normed, q, k, v, lse, near, other))


def normed_back_kernel(
    items, share, len_ref, tok_ref, dq_ref, dk_ref, dv_ref, qw_ref, kw_ref, vw_ref, vec_in, low_in,
    send_ref, keep_ref, pass_ref, sums_ref, part_ref
):
    seq = tok_ref.shape[0]
    item = pl.program_id(0)
    length = len_ref[item]
    me = lax.axis_index("mp")

    @pl.when(item == 0)
    def _():
        sums_ref[...] = jnp.zeros_like(sums_ref)

    def run(span):
        start = pl.multiple_of(item * seq, seq)

        def back_rows(index, rows):
            piece = dot(dq_ref[rows, :], qw_ref[...]) + dot(dk_ref[rows, :], kw_ref[...]) + dot(dv_ref[rows, :], vw_ref[...])
            part_ref[pl.ds(pl.multiple_of(start + index * PIECE, PIECE), PIECE), :] = piece
            normal, unused = norm_stats(tok_ref[rows, :].astype(F32))
            sums_ref[row(0), :] += jnp.sum(piece * normal, axis=0, keepdims=True)
            sums_ref[row(1), :] += jnp.sum(piece, axis=0, keepdims=True)

        over_pieces(span, back_rows)
        if span < seq:
            part_ref[pl.ds(pl.multiple_of(start + span, span), seq - span), :] = jnp.zeros(
                (seq - span, part_ref.shape[1]), F32
            )

    half = seq // 2

    @pl.when(length <= half)
    def _():
        run(half)

    @pl.when(length > half)
    def _():
        run(seq)

    @pl.when(item == items - 1)
    def _():
        def block(k):
            return part_ref[pl.ds(pl.multiple_of((me ^ k) * share, PIECE), share), :]

        keep_ref[...] = block(0)
        pass_ref[...] = block(2)
        send_ref[:share, :] = block(1).astype(BF16)
        send_ref[share : 2 * share, :] = block(3).astype(BF16)
        sums_ref[2:5, :] = 0.5 * vec_in[0:3, :]
        sums_ref[5:6, :] = 0.5 * low_in[0:1, :]
        vectors = sums_ref[0:VECTORS, :]
        send_ref[2 * share :, :] = jnp.concatenate(
            [vectors, jnp.zeros((PAD - VECTORS, vectors.shape[1]), F32)], axis=0
        ).astype(BF16)


def normed_back(lengths, rows2d, dq, dk, dv, query_w, key_w, value_w, vec_in, low_in, items, seq, share):
    rows, width = rows2d.shape
    hw = query_w.shape[0]
    row_block = lambda cols: pl.BlockSpec((seq, cols), lambda i, n: (i, 0))
    whole = lambda dims: pl.BlockSpec(dims, lambda i, n: (0,) * len(dims))
    return pl.pallas_call(
        functools.partial(normed_back_kernel, items, share),
        out_shape=[
            shape((2 * share + PAD, width), BF16),
            pltpu.HBM((share, width), F32),
            pltpu.HBM((share, width), F32),
            shape((8, width), F32),
        ],
        grid_spec=pltpu.PrefetchScalarGridSpec(
            num_scalar_prefetch=1,
            grid=(items,),
            in_specs=[row_block(width)]
            + [row_block(hw)] * 3
            + [whole((hw, width))] * 3
            + [whole(vec_in.shape), whole(low_in.shape)],
            out_specs=[
                whole((2 * share + PAD, width)),
                whole((share, width)),
                whole((share, width)),
                whole((8, width)),
            ],
            scratch_shapes=[pltpu.VMEM((rows, width), F32)],
        ),
        **params("normed_back", 6 * rows * width * hw, 8 * rows * width),
    )(lengths, *in_hbm(rows2d, dq, dk, dv, query_w, key_w, value_w, vec_in, low_in))


def load_all(pairs, sems):
    copies = [pltpu.make_async_copy(source, target, sems.at[i]) for i, (source, target) in enumerate(pairs)]
    for copy in copies:
        copy.start()
    return copies


def halves(count):
    return [slice(start, start + count // 2) for start in range(0, count, count // 2)]


def project_kernel(near_ref, far_ref, own_ref, pack_ref, out_ref):
    hw = own_ref.shape[0]
    for cols in tiles(out_ref.shape[1]):
        out_ref[:, cols] = (dot(near_ref[...], own_ref[:, cols]) + dot(far_ref[...], pack_ref[:hw, cols])).astype(BF16)


def project(near, far, own, pack):
    span, hw = near.shape
    width = own.shape[1]
    return pl.pallas_call(
        project_kernel,
        out_shape=shape((span, width), BF16),
        in_specs=[vmem()] * 4,
        out_specs=vmem(),
        **params("project", 4 * span * width * hw, 4 * span * width),
    )(near, far, *in_hbm(own), pack)


def quad_pairs(own_ref, parts, buf, begin=0):
    rows = own_ref.shape[0] // 4
    mine = lax.axis_index("dp") % 4
    pairs = [(own_ref, buf.at[0])]
    for index, part in enumerate(parts):
        count = rows // 2 if len(parts) == 5 and index > 2 else rows
        start = (mine ^ min(index, 3)) * rows + (count if index == 4 else 0)
        pairs.append((part.at[pl.ds(begin, count), :], buf.at[1, pl.ds(pl.multiple_of(start, 32), count), :]))
    return pairs


def conv_pairs(conv_ref, parts, wc):
    return quad_pairs(conv_ref, parts, wc, parts[0].shape[0] - conv_ref.shape[0] // 4)


def cot_pairs(cot_ref, far_cot, cots):
    span = cots.shape[1]
    start = pl.multiple_of(chip_half() * span, PIECE)
    return [(cot_ref.at[pl.ds(start, span), :], cots.at[0]), (far_cot, cots.at[1])]


def expand_kernel(tok_ref, vec_ref, part_ref, other_ref, out_far, up_ref, *rest):
    up_parts = rest[:5]
    mid_ref, normed_ref, act_ref, slope_ref, wu, tok_buf, sems = rest[5:]
    span, width = mid_ref.shape
    start = pl.multiple_of(chip_half() * span, PIECE)
    copies = load_all([(tok_ref.at[pl.ds(start, span), :], tok_buf)] + quad_pairs(up_ref, up_parts, wu), sems)
    copies[0].wait()

    def add_rows(index, rows):
        mid = tok_buf[rows, :].astype(F32) + vec_ref[row(OUT_B), :] + part_ref[rows, :].astype(F32) + other_ref[rows, :].astype(F32)
        mid_ref[rows, :] = mid
        normal, unused = norm_stats(mid)
        normed_ref[rows, :] = (normal * vec_ref[row(GAIN_MLP), :] + vec_ref[row(BIAS_MLP), :]).astype(BF16)

    over_pieces(span, add_rows)
    for copy in copies[1:]:
        copy.wait()
    hw = out_far.shape[0] - PAD

    def body(step, carry):
        block = step % 2
        rows = pl.ds(pl.multiple_of(step // 2 * (span // 2), PIECE), span // 2)
        for cols in tiles(width):
            own_bias, other_bias = vec_ref[row(UP_B), cols], out_far[hw:, cols].astype(F32)[0:1]
            preact = dot(normed_ref[rows, :], wu[block, :, cols]) + jnp.where(block == 0, own_bias, other_bias)
            normal_cdf = 0.5 * lax.erf(preact * (0.5**0.5)) + 0.5
            density = jnp.exp(preact * preact * -0.5) * 0.3989422804014327
            act_ref[block, rows, cols] = (preact * normal_cdf).astype(BF16)
            slope_ref[block, rows, cols] = (normal_cdf + preact * density).astype(BF16)
        return carry

    lax.fori_loop(0, 4, body, 0)


def expand(rows2d, vecs, part, other, out_far, up_w, up_parts):
    span, width = part.shape
    return pl.pallas_call(
        expand_kernel,
        out_shape=[
            shape((span, width), F32),
            shape((span, width), BF16),
            shape((2, span, width), BF16),
            shape((2, span, width), BF16),
        ],
        in_specs=[anywhere()] + [vmem()] * 4 + [anywhere()] * 6,
        out_specs=[vmem()] * 4,
        scratch_shapes=[
            pltpu.VMEM((2, width, width), BF16),
            pltpu.VMEM((span, width), BF16),
            pltpu.SemaphoreType.DMA((7,)),
        ],
        **params("expand", 4 * span * width * width, 14 * width * width),
    )(*in_hbm(rows2d, vecs), part, other, *in_hbm(out_far, up_w, *up_parts))


def contract_kernel(act_ref, down_ref, *rest):
    down_parts = rest[:4]
    out_ref, wd, sems = rest[4:]
    for copy in load_all(quad_pairs(down_ref, down_parts, wd), sems):
        copy.wait()
    for cols in tiles(out_ref.shape[1]):
        out_ref[:, cols] = (dot(act_ref[0], wd[0, :, cols]) + dot(act_ref[1], wd[1, :, cols])).astype(BF16)


def contract(act, down_w, down_parts):
    unused, span, width = act.shape
    return pl.pallas_call(
        contract_kernel,
        out_shape=shape((span, width), BF16),
        in_specs=[vmem()] + [anywhere()] * 5,
        out_specs=vmem(),
        scratch_shapes=[pltpu.VMEM((2, width, width), BF16), pltpu.SemaphoreType.DMA((5,))],
        **params("contract", 4 * span * width * width, 8 * width * width),
    )(act, *in_hbm(down_w, *down_parts))


def piece_place(info_ref, items, seq, span, index):
    piece = chip_half() * (span // PIECE) + index
    per_item = seq // PIECE
    item = piece // per_item
    length = info_ref[item]
    slot = lax.broadcasted_iota(jnp.int32, (PIECE, 1), 0) + (piece % per_item) * PIECE
    return item, length, (slot < length).astype(F32)


def convolve_kernel(items, seq, info_ref, vec_ref, mid_ref, part_ref, other_ref, conv_ref, *rest):
    parts, (cot_ref, far_cot) = rest[:4], rest[4:6]
    low_ref, z_ref, sums_ref, wc, cots, sems = rest[6:]
    span, width = mid_ref.shape
    block = wc.shape[1]
    copies = load_all(conv_pairs(conv_ref, parts, wc) + cot_pairs(cot_ref, far_cot, cots), sems)
    low_ref[...] = (
        mid_ref[...] + vec_ref[row(DOWN_B), :] + part_ref[...].astype(F32) + other_ref[...].astype(F32)
    ).astype(BF16)
    for copy in copies:
        copy.wait()
    sums_ref[...] = jnp.zeros_like(sums_ref)
    for k in range(2):
        z_ref[k] = dot_cols(low_ref[...], wc[k])

        def add_sums(index, rows):
            item, unused, mask = piece_place(info_ref, items, seq, span, index)
            z = z_ref[k, rows, :]
            masked = z * mask
            upstream = cots[k, rows, :].astype(F32) * mask
            lines = [
                jnp.sum(part, axis=0, keepdims=True) for part in (masked, masked * z, upstream, upstream * z)
            ]
            total = jnp.concatenate(lines, axis=0)
            for base in range(0, block, CH):
                sums_ref[item] += total[:, base : base + CH]

        over_pieces(span, add_sums)


def convolve(info, vecs, mid, part, other, conv_w, parts, cot_rows, far_cot, items, seq):
    span, width = mid.shape
    block = cot_rows.shape[1]
    return pl.pallas_call(
        functools.partial(convolve_kernel, items, seq),
        out_shape=[shape((span, width), BF16), shape((2, span, block), F32), shape((items, 4, CH), F32)],
        in_specs=[smem()] + [vmem()] * 4 + [anywhere()] * 7,
        out_specs=[vmem()] * 3,
        scratch_shapes=[
            pltpu.VMEM((2, block, width), BF16),
            pltpu.VMEM((2, span, block), BF16),
            pltpu.SemaphoreType.DMA((7,)),
        ],
        **params("convolve", 4 * span * width * block, 14 * width * width),
    )(info, *in_hbm(vecs), mid, part, other, *in_hbm(conv_w, *parts, cot_rows, far_cot))


def norm_back_kernel(items, seq, norm_at, info_ref, norm_ref, tot_ref, got_ref, z_ref, conv_ref, *rest):
    parts, (cot_ref, far_cot) = rest[:4], rest[4:6]
    near_ref, far_ref, dz_ref, out_ref, sums_ref, wc, cots, sems = rest[6:]
    span, width = out_ref.shape
    block = z_ref.shape[2]
    copies = load_all(conv_pairs(conv_ref, parts, wc) + cot_pairs(cot_ref, far_cot, cots), sems)
    scale = norm_ref[row(MIXED), norm_at : norm_at + CH]
    shift = norm_ref[row(MIXED), norm_at + CH : norm_at + 2 * CH]

    def item_terms(item, length):
        count = (8 * length).astype(F32)
        total = tot_ref[item] + got_ref[item]
        center = total[0:1] / count
        spread = lax.rsqrt(total[1:2] / count - center * center + EPSILON)
        plain = total[2:3]
        cross = spread * (total[3:4] - center * plain)
        return count, center, spread, plain, cross

    sums_ref[...] = jnp.zeros_like(sums_ref)
    for item in range(items):
        unused, unused, unused, plain, cross = item_terms(item, info_ref[item])
        sums_ref[0:1, :CH] += cross
        sums_ref[0:1, CH : 2 * CH] += plain
    for copy in copies:
        copy.wait()

    def back_rows(index, rows):
        item, length, mask = piece_place(info_ref, items, seq, span, index)
        count, center, spread, plain, cross = item_terms(item, length)
        terms = [center, spread, plain / count, cross / count, scale, shift, spread * scale]
        wide = [jnp.concatenate([t] * (block // CH), axis=1) for t in terms]
        center, spread, plain, cross, scale_w, shift_w, factor = wide
        for k, vol_ref in enumerate((near_ref, far_ref)):
            normal = (z_ref[k, rows, :] - center) * spread
            vol_ref[rows, :] = (mask * (scale_w * normal + shift_w)).astype(BF16)
            upstream = cots[k, rows, :].astype(F32)
            dz_ref[k, rows, :] = (mask * factor * (upstream - plain - normal * cross)).astype(BF16)

    over_pieces(span, back_rows)
    for cols in tiles(width):
        out_ref[:, cols] = (dot(dz_ref[0], wc[0, :, cols]) + dot(dz_ref[1], wc[1, :, cols])).astype(BF16)


def norm_back(info, vecs, total, got, z, conv_w, parts, cot_rows, far_cot, items, seq, norm_at):
    unused, span, block = z.shape
    width = conv_w.shape[1]
    return pl.pallas_call(
        functools.partial(norm_back_kernel, items, seq, norm_at),
        out_shape=[
            shape((span, block), BF16),
            shape((span, block), BF16),
            shape((2, span, block), BF16),
            shape((span, width), BF16),
            shape((8, width), F32),
        ],
        in_specs=[smem()] + [vmem()] * 4 + [anywhere()] * 7,
        out_specs=[vmem()] * 5,
        scratch_shapes=[
            pltpu.VMEM((2, block, width), BF16),
            pltpu.VMEM((2, span, block), BF16),
            pltpu.SemaphoreType.DMA((7,)),
        ],
        **params("norm_back", 4 * span * width * block, 6 * width * width),
    )(info, *in_hbm(vecs), total, got, z, *in_hbm(conv_w, *parts, cot_rows, far_cot))


def mlp_back_kernel(part_ref, other_ref, slope_ref, up_ref, down_ref, *rest):
    up_parts, down_parts = rest[:5], rest[5:9]
    du_ref, out_ref, sums_ref, up_sums, low_ref, wu, wd, sems = rest[9:]
    span, width = out_ref.shape
    copies = load_all(quad_pairs(down_ref, down_parts, wd) + quad_pairs(up_ref, up_parts, wu), sems)
    sums_ref[...] = jnp.zeros_like(sums_ref)
    up_sums[...] = jnp.zeros_like(up_sums)
    for rows in halves(span):
        grad = part_ref[rows, :].astype(F32) + other_ref[rows, :].astype(F32)
        low_ref[rows, :] = grad.astype(BF16)
        sums_ref[0:1, :] += jnp.sum(grad, axis=0, keepdims=True)
    for copy in copies[:5]:
        copy.wait()

    def body(step, carry):
        block = step % 2
        rows = pl.ds(pl.multiple_of(step // 2 * (span // 2), PIECE), span // 2)
        for cols in tiles(width):
            grad = dot_cols(low_ref[rows, :], wd[block, cols, :]) * slope_ref[block, rows, cols].astype(F32)
            low = grad.astype(BF16)
            du_ref[block, rows, cols] = low
            up_sums[block, 0:1, cols] += jnp.sum(low.astype(F32), axis=0, keepdims=True)
        return carry

    lax.fori_loop(0, 4, body, 0)
    for copy in copies[5:]:
        copy.wait()
    for cols in tiles(width):
        out_ref[:, cols] = (dot_cols(du_ref[0], wu[0, cols, :]) + dot_cols(du_ref[1], wu[1, cols, :])).astype(BF16)


def mlp_back(part, other, slope, up_w, down_w, up_parts, down_parts):
    span, width = part.shape
    return pl.pallas_call(
        mlp_back_kernel,
        out_shape=[
            shape((2, span, width), BF16),
            shape((span, width), BF16),
            shape((8, width), F32),
            shape((2, 8, width), F32),
        ],
        in_specs=[vmem()] * 3 + [anywhere()] * 11,
        out_specs=[vmem()] * 4,
        scratch_shapes=[
            pltpu.VMEM((span, width), BF16),
            pltpu.VMEM((2, width, width), BF16),
            pltpu.VMEM((2, width, width), BF16),
            pltpu.SemaphoreType.DMA((11,)),
        ],
        **params("mlp_back", 8 * span * width * width, 20 * width * width),
    )(part, other, slope, *in_hbm(up_w, down_w, *up_parts, *down_parts))


def mid_back_kernel(share, vec_ref, mid_ref, part_ref, other_ref, grad_ref, got_ref, out_w, pack_ref, *rest):
    near_ref, far_ref, em_ref, mine_ref, sums_ref, dmid_ref = rest
    span, width = mid_ref.shape
    sums_ref[...] = jnp.zeros_like(sums_ref)

    def back_rows(index, rows):
        normal, inverse = norm_stats(mid_ref[rows, :])
        grad = grad_ref[rows, :].astype(F32) + got_ref[rows, :].astype(F32)
        dmid = part_ref[rows, :].astype(F32) + other_ref[rows, :].astype(F32)
        dmid += norm_backward(grad, normal, inverse, vec_ref[row(GAIN_MLP), :])
        dmid_ref[rows, :] = dmid
        em_ref[rows, :] = dmid.astype(BF16)
        sums_ref[0:1, :] += jnp.sum(grad * normal, axis=0, keepdims=True)
        sums_ref[1:2, :] += jnp.sum(grad, axis=0, keepdims=True)
        sums_ref[2:3, :] += jnp.sum(dmid, axis=0, keepdims=True)

    over_pieces(span, back_rows)
    far_ref[...] = dot_cols(em_ref[...], pack_ref[: out_w.shape[0], :]).astype(BF16)
    near_ref[...] = dot_cols(em_ref[...], out_w[...]).astype(BF16)
    mine_ref[...] = dmid_ref[pl.ds(pl.multiple_of(lax.axis_index("mp") % 2 * share, PIECE), share), :]


def mid_back(vecs, mid, part, other, grad, got, out_w, pack):
    span, width = mid.shape
    hw = out_w.shape[0]
    return pl.pallas_call(
        functools.partial(mid_back_kernel, span // 2),
        out_shape=[
            shape((span, hw), BF16),
            shape((span, hw), BF16),
            shape((span, width), BF16),
            shape((span // 2, width), F32),
            shape((8, width), F32),
        ],
        in_specs=[vmem()] * 8,
        out_specs=[vmem()] * 5,
        scratch_shapes=[pltpu.VMEM((span, width), F32)],
        **params("mid_back", 4 * span * width * hw, 12 * width * width),
    )(vecs, mid, part, other, grad, got, out_w, pack)


LINKS = {"y": ("mp", 2), "x": ("dp", 1), "z": ("dp", 2)}


class Lane:
    def __init__(self, blocks, rows, parts, link):
        self.blocks, self.rows, self.parts, self.link = blocks, rows, parts, link


class Kept:
    def __init__(self, blocks, rows, array, link, place):
        self.blocks, self.rows, self.array, self.link, self.place = blocks, rows, array, link, place


def high_of(link):
    axis, bit = LINKS[link]
    return (lax.axis_index(axis) // bit) % 2


def aligned(value, rows):
    return value if isinstance(value, int) else pl.multiple_of(value, rows & -rows)


def product_rows(left, right, block, out_ref, at):
    size = left.shape[-1]
    for base in range(0, size, TILE):
        cols = slice(base, min(base + TILE, size))
        lhs = left[block, :, cols] if len(left.shape) == 3 else left[:, cols]
        rhs = right[block] if len(right.shape) == 3 else right[...]
        out_ref[at + base : at + cols.stop, :] = dot_rows(lhs, rhs).astype(BF16)


def products_kernel(lefts, *refs):
    right, out_ref = refs[-2:]
    size = out_ref.shape[0] // 2
    for block in range(2):
        product_rows(refs[block] if lefts == 2 else refs[0], right, block, out_ref, block * size)


def products(name, lefts, right):
    span, width = right.shape[-2:]
    size = lefts[0].shape[-1]
    return pl.pallas_call(
        functools.partial(products_kernel, len(lefts)),
        out_shape=shape((2 * size, width), BF16),
        in_specs=[vmem()] * (len(lefts) + 1),
        out_specs=vmem(),
        **params(name, 4 * span * size * width, 8 * size * width),
    )(*lefts, right)


def emit_kernel(count, inputs, lanes, links, *refs):
    lefts, rights = refs[:count], refs[count : 2 * count]
    sources = list(refs[2 * count : 2 * count + inputs])
    outs = refs[2 * count + inputs :]
    if count:
        product, outs = outs[-1], outs[:-1]
        sources = [product] + sources
        total = product.shape[0] // 2
        begin = 0
        for left, right in zip(lefts, rights):
            for block in range(2):
                product_rows(left, right, block, product, block * total + begin)
            begin += left.shape[-1]
    sends = dict(zip(links, outs))
    kept = iter(outs[len(links) :])
    last = outs[-1]
    places = dict.fromkeys(list(links) + [None], 0)

    for lane in lanes:

        def total_of(block, start, size):
            values = [
                sources[index][pl.ds(aligned(base + block * stride + start, size), size), :]
                for index, base, stride in lane.parts
            ]
            if len(values) == 1:
                return values[0]
            return (values[0].astype(F32) + values[1].astype(F32)).astype(BF16)

        place = places[lane.link]
        if lane.link is None:
            last[place : place + lane.rows, :] = total_of(0, 0, lane.rows)
            places[None] += lane.rows
            continue
        send, keep = sends[lane.link], next(kept)
        if lane.link == "y":
            send[place : place + lane.rows, :] = total_of(1, 0, lane.rows)
            keep[...] = total_of(0, 0, lane.rows)
            places["y"] += lane.rows
            continue
        half = lane.rows // 2
        high = high_of(lane.link)
        for block in range(lane.blocks):
            rows = slice(block * half, (block + 1) * half)
            keep[rows, :] = total_of(block, high * half, half)
            send[place + rows.start : place + rows.stop, :] = total_of(block, (1 - high) * half, half)
        places[lane.link] += lane.blocks * half


def emit(name, lefts, rights, inputs, lanes, width, far=False):
    places = dict.fromkeys(list(LINKS) + [None], 0)
    kept = []
    for lane in lanes:
        sent = lane.blocks * lane.rows // 2 if lane.link else lane.rows
        if lane.link:
            blocks, rows = (1, lane.rows) if lane.link == "y" else (lane.blocks, lane.rows // 2)
            kept.append(Kept(blocks, rows, None, lane.link, places[lane.link]))
        places[lane.link] += sent
    links = [link for link in LINKS if places[link]]
    out_rows = [places[link] for link in links] + [k.blocks * k.rows for k in kept]
    if places[None]:
        out_rows.append(places[None])
    size = sum(left.shape[-1] for left in lefts)
    span = rights[0].shape[-2] if rights else 0
    results = pl.pallas_call(
        functools.partial(emit_kernel, len(lefts), len(inputs), lanes, links),
        out_shape=[
            pltpu.HBM((rows, width), BF16) if far and len(links) <= i < len(links) + len(kept) else shape((rows, width), BF16)
            for i, rows in enumerate(out_rows)
        ],
        in_specs=[vmem()] * (2 * len(lefts) + len(inputs)),
        out_specs=[vmem()] * len(out_rows),
        scratch_shapes=[pltpu.VMEM((2 * size, width), BF16)] if lefts else [],
        **params(name, 4 * span * size * width, 8 * size * width),
    )(*lefts, *rights, *inputs)
    for keep, array in zip(kept, results[len(links) :]):
        keep.array = array
        keep.far = far
    return dict(zip(links, results)), kept, results[-1] if places[None] else None


def send_all(sends):
    return {link: swap(value, *LINKS[link]) for link, value in sends.items()}


def turn(name, kept, got, links, width, fresh=(), far=False):
    inputs = [k.array for k in kept] + list(got.values()) + [lane[0] for lane in fresh]
    inputs = [in_hbm(v)[0] if k.far else v for k, v in zip(kept, inputs)] + inputs[len(kept) :]
    came = {link: len(kept) + i for i, link in enumerate(got)}
    lanes = []
    for i, (k, link) in enumerate(zip(kept, links)):
        lanes.append(Lane(k.blocks, k.rows, [(i, 0, k.rows), (came[k.link], k.place, k.rows)], link))
    for i, (lane, link) in enumerate(zip(fresh, links[len(kept) :])):
        lanes.append(Lane(lane[3], lane[4], [(len(kept) + len(got) + i, lane[1], lane[2])], link))
    return emit(name, [], [], inputs, lanes, width, far)


def spread_kernel(lanes, cuts, flip, *refs):
    first, gots, outs, total = refs[0], refs[1:5], refs[5:-1], refs[-1]
    bits = {"x": high_of("x"), "z": high_of("z")}
    places = [0, 0]
    sizes = [sum(lane[1] for lane in lanes if lane[3] == group) for group in range(2)]
    for base, rows, order, group in lanes:
        at = places[group]
        places[group] += rows
        near, far = ("z", "x") if group == 0 else ("x", "z")
        got_near, got_far = gots[2 * group], gots[2 * group + 1]
        offset = at + (sizes[0] if group else 0)
        pieces = [
            (first[offset : offset + rows, :], ()),
            (got_near[at : at + rows, :], (near,)),
            (got_far[at : at + rows, :], (far,)),
            (got_far[sizes[group] + at : sizes[group] + at + rows, :], (near, far)),
        ]
        for value, flipped in pieces:
            index = [1 - bits[link] if link in flipped else bits[link] for link in order]
            start = base + (index[0] * 2 + index[1]) * rows
            total[pl.ds(aligned(start, rows), rows), :] = value.astype(F32)
    begin = 0
    for i, (out, size) in enumerate(zip(outs, cuts)):
        value = total[begin : begin + size, :]
        out[...] = value.T if i in flip else value
        begin += size


def spread(name, lanes, cuts, flip, first, gots):
    width = first.shape[1]
    return pl.pallas_call(
        functools.partial(spread_kernel, lanes, cuts, flip),
        out_shape=[shape((width, size) if i in flip else (size, width), F32) for i, size in enumerate(cuts)],
        in_specs=[vmem()] * 5,
        out_specs=[vmem()] * len(cuts),
        scratch_shapes=[pltpu.VMEM((sum(cuts), width), F32)],
        **params(name, 0, 8 * sum(cuts) * width),
    )(first, *gots)


def pass_kernel(passed_ref, got_ref, sums_ref, up_ref, send_ref, whole_ref):
    share = passed_ref.shape[0]
    send_ref[:share, :] = (passed_ref[...] + got_ref[share : 2 * share, :].astype(F32)).astype(BF16)
    whole = sums_ref[0:VECTORS, :].astype(BF16).astype(F32) + got_ref[2 * share :, :].astype(F32)[0:VECTORS]
    whole = whole.astype(BF16).astype(F32)
    zero = jnp.zeros((1, whole.shape[1]), F32)
    send_ref[share:, :] = jnp.concatenate([whole, up_ref[1, 0:1, :], zero], axis=0).astype(BF16)
    whole_ref[...] = jnp.concatenate([whole, up_ref[0, 0:1, :], zero], axis=0)


def pass_on(passed, got, sums, up_sums):
    share, width = passed.shape
    return pl.pallas_call(
        pass_kernel,
        out_shape=[shape((share + 8, width), BF16), shape((8, width), F32)],
        in_specs=[vmem()] * 4,
        out_specs=[vmem()] * 2,
        **params("pass_on", 0, 8 * share * width),
    )(*in_hbm(passed), got, sums, up_sums)


def finish_kernel(tok_ref, vec_ref, own_ref, got_ref, last_ref, mine_ref, out_ref, tok_buf, sem):
    share = out_ref.shape[0]
    start = pl.multiple_of(lax.axis_index("mp") * share, PIECE)
    copy = pltpu.make_async_copy(tok_ref.at[pl.ds(start, share), :], tok_buf, sem)
    copy.start()
    copy.wait()

    def back_rows(index, rows):
        normal, inverse = norm_stats(tok_buf[rows, :].astype(F32))
        grad = own_ref[rows, :] + got_ref[rows, :].astype(F32) + last_ref[rows, :].astype(F32)
        out_ref[rows, :] = mine_ref[rows, :] + norm_backward(grad, normal, inverse, vec_ref[row(GAIN_ATTN), :])

    over_pieces(share, back_rows)


def finish(rows2d, vecs, own, got, last, mine):
    share, width = own.shape
    return pl.pallas_call(
        finish_kernel,
        out_shape=shape((share, width), F32),
        in_specs=[anywhere()] + [vmem()] * 5,
        out_specs=vmem(),
        scratch_shapes=[pltpu.VMEM((share, width), BF16), pltpu.SemaphoreType.DMA],
        **params("finish", 0, 14 * share * width),
    )(*in_hbm(rows2d, vecs, own), got, last, *in_hbm(mine))


def add_low(left, right):
    return (left.astype(F32) + right.astype(F32)).astype(BF16)


def bit_of(axis, bit):
    return (lax.axis_index(axis) // bit) % 2


def take_half(value, high):
    half = value.shape[0] // 2
    return lax.dynamic_slice_in_dim(value, high * half, half, 0)


def put_half(mine, other, high):
    return jnp.concatenate([jnp.where(high > 0, other, mine), jnp.where(high > 0, mine, other)], axis=0)


def late_bits():
    bits = []
    bit = 4
    while bit < lax.axis_size("dp"):
        bits.append(bit)
        bit *= 2
    return bits


def finish_reduce(current, bit):
    high = bit_of("dp", bit)
    return add_low(take_half(current, high), swap(take_half(current, 1 - high), "dp", bit))


def finish_gather(current, bit):
    return put_half(current, swap(current, "dp", bit), bit_of("dp", bit))


def shards(
    tokens, lengths, gain_attn, bias_attn, query_w, query_b, key_w, value_w, value_b, out_w, out_b, gain_mlp, bias_mlp,
    up_w, up_b, down_w, down_b, deconv_w, scale_norm, shift_norm, cotangent
):
    items, seq, width = tokens.shape
    rows = items * seq
    me = lax.axis_index("mp")
    share = rows // lax.axis_size("mp")
    span = rows // 2
    hw = query_w.shape[1]
    rows2d = tokens.reshape(rows, width)
    side = bit_of("dp", 1)
    chip = bit_of("mp", 2)
    mixed = jnp.concatenate([query_b, value_b, scale_norm, shift_norm])
    mixed = jnp.pad(mixed, (0, width - mixed.shape[0]))
    vecs = jnp.concatenate([out_b, gain_mlp, bias_mlp, down_b, gain_attn, bias_attn, up_b, mixed])
    vecs = vecs.astype(F32).reshape(8, width)
    weights = [query_w.T, key_w.T, value_w.T]
    conv_w = deconv_w.T

    quarter = width // 4
    mine = lax.axis_index("dp") % 4

    def quarter_of(weight, index):
        count = weight.shape[0] // 4
        return lax.dynamic_slice_in_dim(weight, index * count, count, 0)

    def low_quarter(index):
        return jnp.concatenate([quarter_of(down_w, index), quarter_of(conv_w, index)], axis=0)

    bias_rows = jnp.broadcast_to(up_b[None, :], (PAD, width))
    out_far = swap(jnp.concatenate([out_w, bias_rows], axis=0), "mp", 2)
    up_part = swap(quarter_of(up_w, mine), "mp", 2)
    low_part = swap(low_quarter(mine), "mp", 2)

    normed, q, k, v, lse, near, other = attend(lengths, rows2d, vecs, *weights, items, seq)
    out_far, near, other, up_part, low_part = join(out_far, near, other, up_part, low_part)
    far = swap(other, "mp", 2)
    up_parts = [up_part, swap(up_part, "dp", 1), swap(up_part, "dp", 2)]
    cot_rows = cotangent.reshape(rows, -1)
    cot_sent = lax.dynamic_slice_in_dim(cot_rows, (1 - chip) * span, span, 0)
    low_sent = low_quarter(mine ^ 3)
    last_half = quarter // 2
    turned = [up_parts[2][:last_half], up_parts[1][last_half:]]
    far, low_part, low_sent, cot_sent, turned[0], turned[1], *up_parts = join(
        far, low_part, low_sent, cot_sent, *turned, *up_parts
    )
    low_last = swap(low_sent, "mp", 2)
    up_parts.append(swap(turned[0], "dp", 1))
    up_parts.append(swap(turned[1], "dp", 2))

    part = project(near, far, out_w, out_far)
    part_got = swap(part, "mp", 1)
    part_got, low_part, cot_sent, *up_parts = join(part_got, low_part, cot_sent, *up_parts)
    down_parts = [low_part, swap(low_part, "dp", 1), swap(low_part, "dp", 2)]
    far_cot = swap(cot_sent, "mp", 2)
    mid, normed_two, act, slope = expand(rows2d, vecs, part, part_got, out_far, up_w, up_parts)
    act, low_last, *down_parts = join(act, low_last, *down_parts)
    down_parts.append(low_last)
    part = contract(act, down_w, down_parts)
    part, far_cot = join(part, far_cot)
    low, z, sums = convolve(
        lengths, vecs, mid, part, swap(part, "mp", 1), conv_w, down_parts, cot_rows, far_cot, items, seq
    )
    sums = sums + swap(sums, "mp", 1)
    vol_near, vol_far, dz, grad, norm_sums = norm_back(
        lengths, vecs, sums, swap(sums, "mp", 2), z, conv_w, down_parts, cot_rows, far_cot, items, seq, 2 * hw
    )
    grad_got = swap(grad, "mp", 1)
    conv_raw = products("conv_grad", [dz], low)
    grad_got, conv_raw = join(grad_got, conv_raw)
    block = conv_w.shape[0]
    half = block // 2
    third = width // 3
    lanes = [Lane(2, third, [(0, i * third, width)], link) for i, link in enumerate("yxz")]
    sends, kept, unused = emit("down_grad", [act], [add_low(grad, grad_got)], [], lanes, width)
    grad_got, sends["y"], sends["x"], sends["z"] = join(grad_got, sends["y"], sends["x"], sends["z"])
    came = send_all(sends)
    du, back, low_sums, up_sums = mlp_back(grad, grad_got, slope, up_w, down_w, up_parts, down_parts)
    back, came["y"], came["x"], came["z"] = join(back, came["y"], came["x"], came["z"])
    back_got = swap(back, "mp", 1)
    up_raw = products("up_grad", [normed_two], du)
    fresh = [(conv_raw, 0, block, 2, half), (conv_raw, half, block, 2, half)]
    sends, kept, unused = turn("turn_one", kept, came, "xzyxz", width, fresh)
    back_got, up_raw, sends["y"], sends["x"], sends["z"] = join(back_got, up_raw, sends["y"], sends["x"], sends["z"])
    came = send_all(sends)
    do_near, do_far, em, dmid, vec_sums = mid_back(vecs, mid, grad, grad_got, back, back_got, out_w, out_far)
    do_far, em, came["y"] = join(do_far, em, came["y"])
    do_got = swap(do_far, "mp", 2)
    out_raw = products("out_grad", [near, far], em)
    out_raw, came["y"], came["x"], came["z"] = join(out_raw, came["y"], came["x"], came["z"])
    cut = width * 5 // 12
    fresh = [(up_raw, 0, width, 2, cut), (up_raw, cut, width, 2, cut), (up_raw, 2 * cut, width, 2, width - 2 * cut)]
    fresh.append((out_raw, 0, hw, 2, hw))
    sends, kept, unused = turn("turn_two", kept, came, "zyxzxyxzz", width, fresh, True)
    do_got, sends["y"], sends["x"], sends["z"] = join(do_got, sends["y"], sends["x"], sends["z"])
    came = send_all(sends)

    *dqkv, qkv_grad, bias_sums = attend_back(lengths, normed, q, k, v, lse, do_near, do_got, items, seq, share)
    qkv_grad, vol_far, came["y"], came["x"], came["z"], *dqkv = join(
        qkv_grad, vol_far, came["y"], came["x"], came["z"], *dqkv
    )
    cut = qkv_grad.shape[0] * 4 // 9
    fresh = [(qkv_grad, 0, 0, 1, cut), (qkv_grad, cut, 0, 1, qkv_grad.shape[0] - cut)]
    sizes = [k.blocks * k.rows for k in kept[:3]]
    links = [None] * 3 + ["y", "y", "x", "z", "y", "y", "x", "z"]
    sends, kept, first = turn("turn_three", kept, came, links, width, fresh, True)
    for bit in late_bits():
        first = finish_reduce(first, bit)
    came = send_all(sends)
    sent, own, passed, own_sums = normed_back(
        lengths, rows2d, *dqkv, *weights, vec_sums, low_sums, items, seq, share
    )
    first, sent, came["y"], came["x"], came["z"] = join(first, sent, came["y"], came["x"], came["z"])
    for bit in reversed(late_bits()):
        first = finish_gather(first, bit)
    got = swap(sent, "mp", 1)
    conv_sizes = [k.blocks * k.rows for k in kept[:2]]
    came = {link: in_hbm(value)[0] for link, value in came.items()}
    sends, kept, early = turn("turn_four", kept, came, [None, None] + list("zyxxzx"), width)
    came = send_all(sends)
    first, got, vol_far, came["y"], came["x"], came["z"] = join(first, got, vol_far, came["y"], came["x"], came["z"])
    kept = [kept[i] for i in (0, 1, 4, 2, 3, 5)]
    unused, unused, last = turn("turn_five", kept, came, [None] * 6, width)
    last_sizes = [k.blocks * k.rows for k in kept] + conv_sizes
    last = jnp.concatenate([last, early], axis=0)
    for bit in late_bits():
        last = finish_reduce(last, bit)
    edge = sizes[0] + sizes[1]
    sent_near = [first[:edge], first[edge:]]
    near_got = [swap(sent_near[0], "dp", 2), swap(sent_near[1], "dp", 1)]
    second, whole = pass_on(passed, got, own_sums, up_sums)
    second = swap(second, "mp", 2)
    far_got = [
        swap(jnp.concatenate([sent_near[0], near_got[0]], axis=0), "dp", 1),
        swap(jnp.concatenate([sent_near[1], near_got[1]], axis=0), "dp", 2),
    ]
    last, second, vol_far, *far_got = join(last, second, vol_far, *far_got)
    vol_got = swap(vol_far, "mp", 2)
    tokens_grad = finish(rows2d, vecs, own, got, second, dmid)
    for bit in reversed(late_bits()):
        last = finish_gather(last, bit)
    whole = (whole + second[share : share + 8].astype(F32))[: VECTORS + 1]
    lines = jnp.concatenate([whole, bias_sums[0:1], bias_sums[2:3], norm_sums[0:1]], axis=0)
    for bit in [1, 2] + late_bits():
        lines = lines + swap(lines, "dp", bit)
    (down_total,) = spread(
        "spread_one",
        [(0, sizes[0], "xz", 0), (third, sizes[1], "xz", 0), (2 * third, sizes[2], "zx", 1)],
        [width],
        [],
        first,
        [near_got[0], far_got[0], near_got[1], far_got[1]],
    )
    last, lines, down_total, tokens_grad = join(last, lines, down_total, tokens_grad)
    edge = sum(last_sizes[:3])
    sent_last = [last[:edge], last[edge:]]
    last_got = [swap(sent_last[0], "dp", 2), swap(sent_last[1], "dp", 1)]
    volume = put_half(vol_near, vol_got, chip).astype(F32)
    volume, *last_got = join(volume, *last_got)
    last_far = [
        swap(jnp.concatenate([sent_last[0], last_got[0]], axis=0), "dp", 1),
        swap(jnp.concatenate([sent_last[1], last_got[1]], axis=0), "dp", 2),
    ]
    base = width + hw
    up_cut = width * 5 // 12
    up_total, out_total, query_total, key_total, value_total, conv_total = spread(
        "spread_two",
        [
            (0, last_sizes[0], "xz", 0),
            (up_cut, last_sizes[1], "xz", 0),
            (base, last_sizes[2], "xz", 0),
            (2 * up_cut, last_sizes[3], "zx", 1),
            (width, last_sizes[4], "zx", 1),
            (base + cut, last_sizes[5], "zx", 1),
            (base + 3 * hw, last_sizes[6], "xz", 1),
            (base + 3 * hw + half, last_sizes[7], "zx", 1),
        ],
        [width, hw, hw, hw, hw, block],
        [5],
        last,
        [last_got[0], last_far[0], last_got[1], last_far[1]],
    )
    return (
        volume.reshape(items, seq, -1),
        tokens_grad,
        lines[0],
        lines[1],
        query_total.T,
        lines[VECTORS + 1, :hw],
        key_total.T,
        value_total.T,
        lines[VECTORS + 2, :hw],
        out_total,
        lines[4],
        lines[2],
        lines[3],
        up_total,
        lines[VECTORS],
        down_total,
        lines[5],
        conv_total,
        lines[VECTORS + 3, :CH],
        lines[VECTORS + 3, CH : 2 * CH],
    )


def solution(mesh):
    in_specs = (
        P("dp", None, None),
        P("dp"),
        P(),
        P(),
        P(None, "mp"),
        P("mp"),
        P(None, "mp"),
        P(None, "mp"),
        P("mp"),
        P("mp", None),
        P(),
        P(),
        P(),
        P(None, "mp"),
        P("mp"),
        P("mp", None),
        P(),
        P(None, "mp"),
        P(),
        P(),
        P("dp", None, "mp"),
    )
    out_specs = (
        P("dp", None, "mp"),
        P(("dp", "mp"), None),
        P(),
        P(),
        P(None, "mp"),
        P("mp"),
        P(None, "mp"),
        P(None, "mp"),
        P("mp"),
        P("mp", None),
        P(),
        P(),
        P(),
        P(None, "mp"),
        P("mp"),
        P("mp", None),
        P(),
        P(None, "mp"),
        P(),
        P(),
    )
    return jax.shard_map(shards, mesh=mesh, in_specs=in_specs, out_specs=out_specs, check_vma=False)
```

```python
import functools

import jax
import jax.numpy as jnp
from jax import lax
from jax.experimental import pallas as pl
from jax.experimental.pallas import tpu as pltpu
from jax.sharding import PartitionSpec as P

HEAD_DIM = 64
CH = 128
EPSILON = 1e-05
SCALE = HEAD_DIM ** (-0.5)
F32 = jnp.float32
BF16 = jnp.bfloat16
TILE = 256
PIECE = 128
PAD = 16
VECTORS = 6
OUT_B, GAIN_MLP, BIAS_MLP, DOWN_B, GAIN_ATTN, BIAS_ATTN, UP_B, MIXED = range(8)
COST = 1
MIB = 1024 * 1024


def dot(left, right):
    return jnp.dot(left, right, preferred_element_type=F32)


def dot_rows(left, right):
    return lax.dot_general(left, right, (((0,), (0,)), ((), ())), preferred_element_type=F32)


def dot_cols(left, right):
    return lax.dot_general(left, right, (((1,), (1,)), ((), ())), preferred_element_type=F32)


def swap(value, axis, bit):
    size = lax.axis_size(axis)
    return lax.ppermute(value, axis, [(i, i ^ bit) for i in range(size)])


def norm_stats(values):
    center = values - jnp.mean(values, axis=-1, keepdims=True)
    inverse = lax.rsqrt(jnp.mean(center * center, axis=-1, keepdims=True) + EPSILON)
    return center * inverse, inverse


def norm_backward(upstream, normal, inverse, gain_vec):
    scaled = upstream * gain_vec
    mean_part = jnp.mean(scaled, axis=-1, keepdims=True)
    mean_cross = jnp.mean(scaled * normal, axis=-1, keepdims=True)
    return inverse * (scaled - mean_part - normal * mean_cross)


def vmem():
    return pl.BlockSpec(memory_space=pltpu.VMEM)


def anywhere():
    return pl.BlockSpec(memory_space=pl.ANY)


def row(index):
    return slice(index, index + 1)


def smem():
    return pl.BlockSpec(memory_space=pltpu.SMEM)


def shape(dims, dtype):
    return jax.ShapeDtypeStruct(dims, dtype)


def join(*values):
    return lax.optimization_barrier(values)


def in_hbm(*values):
    return [pltpu.with_memory_space_constraint(value, pltpu.HBM) for value in values]


def params(name, flops, moved, mebibytes=24):
    return dict(
        compiler_params=pltpu.CompilerParams(vmem_limit_bytes=mebibytes * MIB),
        cost_estimate=pl.CostEstimate(flops=flops // COST, transcendentals=0, bytes_accessed=moved // COST),
        name=name,
    )


def over_pieces(count, step):
    def body(index, carry):
        step(index, pl.ds(pl.multiple_of(index * PIECE, PIECE), PIECE))
        return carry

    lax.fori_loop(0, count // PIECE, body, 0)


def head_cols(head):
    return slice(head * HEAD_DIM, (head + 1) * HEAD_DIM)


def tiles(width):
    return [slice(start, start + TILE) for start in range(0, width, TILE)]


def chip_half():
    return lax.axis_index("mp") // 2


def x_side():
    return lax.axis_index("dp") % 2


def attend_kernel(
    items, heads, span_rows, info_ref, tok_ref, vec_ref, qw_ref, kw_ref, vw_ref,
    normed_ref, q_ref, k_ref, v_ref, lse_ref, near_ref, other_ref, o_ref
):
    seq = tok_ref.shape[0]
    item = pl.program_id(0)
    length = info_ref[item]
    for start in range(0, seq, PIECE):
        rows = slice(start, start + PIECE)
        normal, unused = norm_stats(tok_ref[rows, :].astype(F32))
        normed_ref[rows, :] = (normal * vec_ref[row(GAIN_ATTN), :] + vec_ref[row(BIAS_ATTN), :]).astype(BF16)
    normed = normed_ref[...]
    hw = q_ref.shape[1]
    q_ref[...] = (dot_cols(normed, qw_ref[...]) + vec_ref[row(MIXED), :hw]).astype(BF16) * jnp.asarray(SCALE, BF16)
    k_ref[...] = dot_cols(normed, kw_ref[...]).astype(BF16)
    v_ref[...] = (dot_cols(normed, vw_ref[...]) + vec_ref[row(MIXED), hw : 2 * hw]).astype(BF16)

    def run(span):
        valid = lax.broadcasted_iota(jnp.int32, (span, span), 0) < length
        for head in range(heads):
            cols = head_cols(head)
            scores = jnp.where(valid, dot_cols(k_ref[:span, cols], q_ref[:span, cols]), -1e9)
            top = jnp.max(scores, axis=0, keepdims=True)
            raised = jnp.exp(scores - top)
            total = jnp.sum(raised, axis=0, keepdims=True)
            mixed = dot_rows(v_ref[:span, cols], raised.astype(BF16)) / total
            o_ref[pl.ds(pl.multiple_of(item * seq, seq), span), cols] = mixed.T.astype(BF16)
            lse_ref[0, head : head + 1, :span] = top + jnp.log(total)
        if span < seq:
            o_ref[pl.ds(pl.multiple_of(item * seq + span, span), seq - span), :] = jnp.zeros(
                (seq - span, heads * HEAD_DIM), BF16
            )

    half = seq // 2

    @pl.when(length <= half)
    def _():
        run(half)

    @pl.when(length > half)
    def _():
        run(seq)

    @pl.when(item == items - 1)
    def _():
        start = chip_half() * span_rows
        near_ref[...] = o_ref[pl.ds(pl.multiple_of(start, PIECE), span_rows), :]
        other_ref[...] = o_ref[pl.ds(pl.multiple_of(span_rows - start, PIECE), span_rows), :]


def attend(info, rows2d, vecs, query_w, key_w, value_w, items, seq):
    rows, width = rows2d.shape
    hw = query_w.shape[0]
    heads = hw // HEAD_DIM
    row_block = lambda cols: pl.BlockSpec((seq, cols), lambda i, n: (i, 0))
    whole = lambda dims: pl.BlockSpec(dims, lambda i, n: (0,) * len(dims))
    return pl.pallas_call(
        functools.partial(attend_kernel, items, heads, rows // 2),
        out_shape=[pltpu.HBM((rows, width), BF16)]
        + [pltpu.HBM((rows, hw), BF16)] * 3
        + [pltpu.HBM((items, 8, seq), F32)]
        + [shape((rows // 2, hw), BF16)] * 2,
        grid_spec=pltpu.PrefetchScalarGridSpec(
            num_scalar_prefetch=1,
            grid=(items,),
            in_specs=[row_block(width), whole(vecs.shape)] + [whole((hw, width))] * 3,
            out_specs=[row_block(width)]
            + [row_block(hw)] * 3
            + [pl.BlockSpec((1, 8, seq), lambda i, n: (i, 0, 0))]
            + [whole((rows // 2, hw))] * 2,
            scratch_shapes=[pltpu.VMEM((rows, hw), BF16)],
        ),
        **params("attend", 6 * rows * width * hw + 4 * rows * seq * hw, 4 * rows * width),
    )(info, *in_hbm(rows2d, vecs, query_w, key_w, value_w))


def attend_back_kernel(
    items, heads, share, len_ref, normed_ref, q_ref, k_ref, v_ref, lse_ref, near_ref, other_ref,
    dq_ref, dk_ref, dv_ref, grad_ref, sums_ref, do_ref, grad_acc
):
    seq = normed_ref.shape[0]
    hw = heads * HEAD_DIM
    item = pl.program_id(0)
    length = len_ref[item]

    @pl.when(item == 0)
    def _():
        begin = chip_half() * 2 * share
        do_ref[pl.ds(pl.multiple_of(begin, PIECE), 2 * share), :] = near_ref[...]
        do_ref[pl.ds(pl.multiple_of(2 * share - begin, PIECE), 2 * share), :] = other_ref[...]
        sums_ref[...] = jnp.zeros_like(sums_ref)
        grad_acc[...] = jnp.zeros_like(grad_acc)

    def run(span):
        valid = lax.broadcasted_iota(jnp.int32, (span, span), 0) < length
        for head in range(heads):
            cols = head_cols(head)
            query, keys, vals = q_ref[:span, cols], k_ref[:span, cols], v_ref[:span, cols]
            upstream = do_ref[pl.ds(pl.multiple_of(item * seq, seq), span), cols]
            scores = jnp.where(valid, dot_cols(keys, query), -1e9)
            prob = jnp.exp(scores - lse_ref[0, head : head + 1, :span])
            dv_ref[:span, cols] = dot(prob.astype(BF16), upstream).astype(BF16)
            prob_grad = dot_cols(vals, upstream)
            product = prob * prob_grad
            row_term = jnp.sum(product, axis=0, keepdims=True)
            score_grad = (product - prob * row_term).astype(BF16)
            dk_ref[:span, cols] = dot(score_grad, query).astype(BF16)
            dq_ref[:span, cols] = (dot_rows(keys, score_grad) * SCALE).T.astype(BF16)
        for index, ref in enumerate((dq_ref, dk_ref, dv_ref)):
            grad_acc[index * hw : (index + 1) * hw, :] += dot_rows(ref[:span, :], normed_ref[:span, :])
            if index != 1:
                sums_ref[row(index), :hw] += jnp.sum(ref[:span, :].astype(F32), axis=0, keepdims=True)
            if span < seq:
                ref[span:, :] = jnp.zeros((seq - span, hw), BF16)

    half = seq // 2

    @pl.when(length <= half)
    def _():
        run(half)

    @pl.when(length > half)
    def _():
        run(seq)

    @pl.when(item == items - 1)
    def _():
        grad_ref[...] = grad_acc[...].astype(BF16)


def attend_back(lengths, normed, q, k, v, lse, near, other, items, seq, share):
    rows, width = normed.shape
    hw = q.shape[1]
    heads = hw // HEAD_DIM
    row_block = lambda cols: pl.BlockSpec((seq, cols), lambda i, n: (i, 0))
    whole = lambda dims: pl.BlockSpec(dims, lambda i, n: (0,) * len(dims))
    return pl.pallas_call(
        functools.partial(attend_back_kernel, items, heads, share),
        out_shape=[pltpu.HBM((rows, hw), BF16)] * 3 + [shape((3 * hw, width), BF16), shape((8, width), F32)],
        grid_spec=pltpu.PrefetchScalarGridSpec(
            num_scalar_prefetch=1,
            grid=(items,),
            in_specs=[row_block(width)]
            + [row_block(hw)] * 3
            + [pl.BlockSpec((1, 8, seq), lambda i, n: (i, 0, 0))]
            + [whole((2 * share, hw))] * 2,
            out_specs=[row_block(hw)] * 3 + [whole((3 * hw, width)), whole((8, width))],
            scratch_shapes=[pltpu.VMEM((rows, hw), BF16), pltpu.VMEM((3 * hw, width), F32)],
        ),
        **params("attend_back", 6 * rows * width * hw + 10 * rows * seq * hw, 8 * rows * width),
    )(lengths, *in_hbm(normed, q, k, v, lse, near, other))


def normed_back_kernel(
    items, share, len_ref, tok_ref, dq_ref, dk_ref, dv_ref, qw_ref, kw_ref, vw_ref, vec_in, low_in,
    send_ref, keep_ref, pass_ref, sums_ref, part_ref
):
    seq = tok_ref.shape[0]
    item = pl.program_id(0)
    length = len_ref[item]
    me = lax.axis_index("mp")

    @pl.when(item == 0)
    def _():
        sums_ref[...] = jnp.zeros_like(sums_ref)

    def run(span):
        start = pl.multiple_of(item * seq, seq)

        def back_rows(index, rows):
            piece = dot(dq_ref[rows, :], qw_ref[...]) + dot(dk_ref[rows, :], kw_ref[...]) + dot(dv_ref[rows, :], vw_ref[...])
            part_ref[pl.ds(pl.multiple_of(start + index * PIECE, PIECE), PIECE), :] = piece
            normal, unused = norm_stats(tok_ref[rows, :].astype(F32))
            sums_ref[row(0), :] += jnp.sum(piece * normal, axis=0, keepdims=True)
            sums_ref[row(1), :] += jnp.sum(piece, axis=0, keepdims=True)

        over_pieces(span, back_rows)
        if span < seq:
            part_ref[pl.ds(pl.multiple_of(start + span, span), seq - span), :] = jnp.zeros(
                (seq - span, part_ref.shape[1]), F32
            )

    half = seq // 2

    @pl.when(length <= half)
    def _():
        run(half)

    @pl.when(length > half)
    def _():
        run(seq)

    @pl.when(item == items - 1)
    def _():
        def block(k):
            return part_ref[pl.ds(pl.multiple_of((me ^ k) * share, PIECE), share), :]

        keep_ref[...] = block(0)
        pass_ref[...] = block(2)
        send_ref[:share, :] = block(1).astype(BF16)
        send_ref[share : 2 * share, :] = block(3).astype(BF16)
        sums_ref[2:5, :] = 0.5 * vec_in[0:3, :]
        sums_ref[5:6, :] = 0.5 * low_in[0:1, :]
        vectors = sums_ref[0:VECTORS, :]
        send_ref[2 * share :, :] = jnp.concatenate(
            [vectors, jnp.zeros((PAD - VECTORS, vectors.shape[1]), F32)], axis=0
        ).astype(BF16)


def normed_back(lengths, rows2d, dq, dk, dv, query_w, key_w, value_w, vec_in, low_in, items, seq, share):
    rows, width = rows2d.shape
    hw = query_w.shape[0]
    row_block = lambda cols: pl.BlockSpec((seq, cols), lambda i, n: (i, 0))
    whole = lambda dims: pl.BlockSpec(dims, lambda i, n: (0,) * len(dims))
    return pl.pallas_call(
        functools.partial(normed_back_kernel, items, share),
        out_shape=[
            shape((2 * share + PAD, width), BF16),
            pltpu.HBM((share, width), F32),
            pltpu.HBM((share, width), F32),
            shape((8, width), F32),
        ],
        grid_spec=pltpu.PrefetchScalarGridSpec(
            num_scalar_prefetch=1,
            grid=(items,),
            in_specs=[row_block(width)]
            + [row_block(hw)] * 3
            + [whole((hw, width))] * 3
            + [whole(vec_in.shape), whole(low_in.shape)],
            out_specs=[
                whole((2 * share + PAD, width)),
                whole((share, width)),
                whole((share, width)),
                whole((8, width)),
            ],
            scratch_shapes=[pltpu.VMEM((rows, width), F32)],
        ),
        **params("normed_back", 6 * rows * width * hw, 8 * rows * width),
    )(lengths, *in_hbm(rows2d, dq, dk, dv, query_w, key_w, value_w, vec_in, low_in))


def load_all(pairs, sems):
    copies = [pltpu.make_async_copy(source, target, sems.at[i]) for i, (source, target) in enumerate(pairs)]
    for copy in copies:
        copy.start()
    return copies


def halves(count):
    return [slice(start, start + count // 2) for start in range(0, count, count // 2)]


def project_kernel(near_ref, far_ref, own_ref, pack_ref, out_ref):
    hw = own_ref.shape[0]
    for cols in tiles(out_ref.shape[1]):
        out_ref[:, cols] = (dot(near_ref[...], own_ref[:, cols]) + dot(far_ref[...], pack_ref[:hw, cols])).astype(BF16)


def project(near, far, own, pack):
    span, hw = near.shape
    width = own.shape[1]
    return pl.pallas_call(
        project_kernel,
        out_shape=shape((span, width), BF16),
        in_specs=[vmem()] * 4,
        out_specs=vmem(),
        **params("project", 4 * span * width * hw, 4 * span * width),
    )(near, far, *in_hbm(own), pack)


def quad_pairs(own_ref, parts, buf, begin=0):
    rows = own_ref.shape[0] // 4
    mine = lax.axis_index("dp") % 4
    pairs = [(own_ref, buf.at[0])]
    for index, part in enumerate(parts):
        count = rows // 2 if len(parts) == 5 and index > 2 else rows
        start = (mine ^ min(index, 3)) * rows + (count if index == 4 else 0)
        pairs.append((part.at[pl.ds(begin, count), :], buf.at[1, pl.ds(pl.multiple_of(start, 32), count), :]))
    return pairs


def conv_pairs(conv_ref, parts, wc):
    return quad_pairs(conv_ref, parts, wc, parts[0].shape[0] - conv_ref.shape[0] // 4)


def cot_pairs(cot_ref, far_cot, cots):
    span = cots.shape[1]
    start = pl.multiple_of(chip_half() * span, PIECE)
    return [(cot_ref.at[pl.ds(start, span), :], cots.at[0]), (far_cot, cots.at[1])]


def expand_kernel(tok_ref, vec_ref, part_ref, other_ref, out_far, up_ref, *rest):
    up_parts = rest[:5]
    mid_ref, normed_ref, act_ref, slope_ref, wu, tok_buf, sems = rest[5:]
    span, width = mid_ref.shape
    start = pl.multiple_of(chip_half() * span, PIECE)
    copies = load_all([(tok_ref.at[pl.ds(start, span), :], tok_buf)] + quad_pairs(up_ref, up_parts, wu), sems)
    copies[0].wait()

    def add_rows(index, rows):
        mid = tok_buf[rows, :].astype(F32) + vec_ref[row(OUT_B), :] + part_ref[rows, :].astype(F32) + other_ref[rows, :].astype(F32)
        mid_ref[rows, :] = mid
        normal, unused = norm_stats(mid)
        normed_ref[rows, :] = (normal * vec_ref[row(GAIN_MLP), :] + vec_ref[row(BIAS_MLP), :]).astype(BF16)

    over_pieces(span, add_rows)
    for copy in copies[1:]:
        copy.wait()
    hw = out_far.shape[0] - PAD

    def body(step, carry):
        block = step % 2
        rows = pl.ds(pl.multiple_of(step // 2 * (span // 2), PIECE), span // 2)
        for cols in tiles(width):
            own_bias, other_bias = vec_ref[row(UP_B), cols], out_far[hw:, cols].astype(F32)[0:1]
            preact = dot(normed_ref[rows, :], wu[block, :, cols]) + jnp.where(block == 0, own_bias, other_bias)
            normal_cdf = 0.5 * lax.erf(preact * (0.5**0.5)) + 0.5
            density = jnp.exp(preact * preact * -0.5) * 0.3989422804014327
            act_ref[block, rows, cols] = (preact * normal_cdf).astype(BF16)
            slope_ref[block, rows, cols] = (normal_cdf + preact * density).astype(BF16)
        return carry

    lax.fori_loop(0, 4, body, 0)


def expand(rows2d, vecs, part, other, out_far, up_w, up_parts):
    span, width = part.shape
    return pl.pallas_call(
        expand_kernel,
        out_shape=[
            shape((span, width), F32),
            shape((span, width), BF16),
            shape((2, span, width), BF16),
            shape((2, span, width), BF16),
        ],
        in_specs=[anywhere()] + [vmem()] * 4 + [anywhere()] * 6,
        out_specs=[vmem()] * 4,
        scratch_shapes=[
            pltpu.VMEM((2, width, width), BF16),
            pltpu.VMEM((span, width), BF16),
            pltpu.SemaphoreType.DMA((7,)),
        ],
        **params("expand", 4 * span * width * width, 14 * width * width),
    )(*in_hbm(rows2d, vecs), part, other, *in_hbm(out_far, up_w, *up_parts))


def contract_kernel(act_ref, down_ref, *rest):
    down_parts = rest[:4]
    out_ref, wd, sems = rest[4:]
    for copy in load_all(quad_pairs(down_ref, down_parts, wd), sems):
        copy.wait()
    for cols in tiles(out_ref.shape[1]):
        out_ref[:, cols] = (dot(act_ref[0], wd[0, :, cols]) + dot(act_ref[1], wd[1, :, cols])).astype(BF16)


def contract(act, down_w, down_parts):
    unused, span, width = act.shape
    return pl.pallas_call(
        contract_kernel,
        out_shape=shape((span, width), BF16),
        in_specs=[vmem()] + [anywhere()] * 5,
        out_specs=vmem(),
        scratch_shapes=[pltpu.VMEM((2, width, width), BF16), pltpu.SemaphoreType.DMA((5,))],
        **params("contract", 4 * span * width * width, 8 * width * width),
    )(act, *in_hbm(down_w, *down_parts))


def piece_place(info_ref, items, seq, span, index):
    piece = chip_half() * (span // PIECE) + index
    per_item = seq // PIECE
    item = piece // per_item
    length = info_ref[item]
    slot = lax.broadcasted_iota(jnp.int32, (PIECE, 1), 0) + (piece % per_item) * PIECE
    return item, length, (slot < length).astype(F32)


def convolve_kernel(items, seq, info_ref, vec_ref, mid_ref, part_ref, other_ref, conv_ref, *rest):
    parts, (cot_ref, far_cot) = rest[:4], rest[4:6]
    low_ref, z_ref, sums_ref, wc, cots, sems = rest[6:]
    span, width = mid_ref.shape
    block = wc.shape[1]
    copies = load_all(conv_pairs(conv_ref, parts, wc) + cot_pairs(cot_ref, far_cot, cots), sems)
    low_ref[...] = (
        mid_ref[...] + vec_ref[row(DOWN_B), :] + part_ref[...].astype(F32) + other_ref[...].astype(F32)
    ).astype(BF16)
    for copy in copies:
        copy.wait()
    sums_ref[...] = jnp.zeros_like(sums_ref)
    for k in range(2):
        z_ref[k] = dot_cols(low_ref[...], wc[k])

        def add_sums(index, rows):
            item, unused, mask = piece_place(info_ref, items, seq, span, index)
            z = z_ref[k, rows, :]
            masked = z * mask
            upstream = cots[k, rows, :].astype(F32) * mask
            lines = [
                jnp.sum(part, axis=0, keepdims=True) for part in (masked, masked * z, upstream, upstream * z)
            ]
            total = jnp.concatenate(lines, axis=0)
            for base in range(0, block, CH):
                sums_ref[item] += total[:, base : base + CH]

        over_pieces(span, add_sums)


def convolve(info, vecs, mid, part, other, conv_w, parts, cot_rows, far_cot, items, seq):
    span, width = mid.shape
    block = cot_rows.shape[1]
    return pl.pallas_call(
        functools.partial(convolve_kernel, items, seq),
        out_shape=[shape((span, width), BF16), shape((2, span, block), F32), shape((items, 4, CH), F32)],
        in_specs=[smem()] + [vmem()] * 4 + [anywhere()] * 7,
        out_specs=[vmem()] * 3,
        scratch_shapes=[
            pltpu.VMEM((2, block, width), BF16),
            pltpu.VMEM((2, span, block), BF16),
            pltpu.SemaphoreType.DMA((7,)),
        ],
        **params("convolve", 4 * span * width * block, 14 * width * width),
    )(info, *in_hbm(vecs), mid, part, other, *in_hbm(conv_w, *parts, cot_rows, far_cot))


def norm_back_kernel(items, seq, norm_at, info_ref, norm_ref, tot_ref, got_ref, z_ref, conv_ref, *rest):
    parts, (cot_ref, far_cot) = rest[:4], rest[4:6]
    near_ref, far_ref, dz_ref, out_ref, sums_ref, wc, cots, sems = rest[6:]
    span, width = out_ref.shape
    block = z_ref.shape[2]
    copies = load_all(conv_pairs(conv_ref, parts, wc) + cot_pairs(cot_ref, far_cot, cots), sems)
    scale = norm_ref[row(MIXED), norm_at : norm_at + CH]
    shift = norm_ref[row(MIXED), norm_at + CH : norm_at + 2 * CH]

    def item_terms(item, length):
        count = (8 * length).astype(F32)
        total = tot_ref[item] + got_ref[item]
        center = total[0:1] / count
        spread = lax.rsqrt(total[1:2] / count - center * center + EPSILON)
        plain = total[2:3]
        cross = spread * (total[3:4] - center * plain)
        return count, center, spread, plain, cross

    sums_ref[...] = jnp.zeros_like(sums_ref)
    for item in range(items):
        unused, unused, unused, plain, cross = item_terms(item, info_ref[item])
        sums_ref[0:1, :CH] += cross
        sums_ref[0:1, CH : 2 * CH] += plain
    for copy in copies:
        copy.wait()

    def back_rows(index, rows):
        item, length, mask = piece_place(info_ref, items, seq, span, index)
        count, center, spread, plain, cross = item_terms(item, length)
        terms = [center, spread, plain / count, cross / count, scale, shift, spread * scale]
        wide = [jnp.concatenate([t] * (block // CH), axis=1) for t in terms]
        center, spread, plain, cross, scale_w, shift_w, factor = wide
        for k, vol_ref in enumerate((near_ref, far_ref)):
            normal = (z_ref[k, rows, :] - center) * spread
            vol_ref[rows, :] = (mask * (scale_w * normal + shift_w)).astype(BF16)
            upstream = cots[k, rows, :].astype(F32)
            dz_ref[k, rows, :] = (mask * factor * (upstream - plain - normal * cross)).astype(BF16)

    over_pieces(span, back_rows)
    for cols in tiles(width):
        out_ref[:, cols] = (dot(dz_ref[0], wc[0, :, cols]) + dot(dz_ref[1], wc[1, :, cols])).astype(BF16)


def norm_back(info, vecs, total, got, z, conv_w, parts, cot_rows, far_cot, items, seq, norm_at):
    unused, span, block = z.shape
    width = conv_w.shape[1]
    return pl.pallas_call(
        functools.partial(norm_back_kernel, items, seq, norm_at),
        out_shape=[
            shape((span, block), BF16),
            shape((span, block), BF16),
            shape((2, span, block), BF16),
            shape((span, width), BF16),
            shape((8, width), F32),
        ],
        in_specs=[smem()] + [vmem()] * 4 + [anywhere()] * 7,
        out_specs=[vmem()] * 5,
        scratch_shapes=[
            pltpu.VMEM((2, block, width), BF16),
            pltpu.VMEM((2, span, block), BF16),
            pltpu.SemaphoreType.DMA((7,)),
        ],
        **params("norm_back", 4 * span * width * block, 6 * width * width),
    )(info, *in_hbm(vecs), total, got, z, *in_hbm(conv_w, *parts, cot_rows, far_cot))


def mlp_back_kernel(part_ref, other_ref, slope_ref, up_ref, down_ref, *rest):
    up_parts, down_parts = rest[:5], rest[5:9]
    du_ref, out_ref, sums_ref, up_sums, low_ref, wu, wd, sems = rest[9:]
    span, width = out_ref.shape
    copies = load_all(quad_pairs(down_ref, down_parts, wd) + quad_pairs(up_ref, up_parts, wu), sems)
    sums_ref[...] = jnp.zeros_like(sums_ref)
    up_sums[...] = jnp.zeros_like(up_sums)
    for rows in halves(span):
        grad = part_ref[rows, :].astype(F32) + other_ref[rows, :].astype(F32)
        low_ref[rows, :] = grad.astype(BF16)
        sums_ref[0:1, :] += jnp.sum(grad, axis=0, keepdims=True)
    for copy in copies[:5]:
        copy.wait()

    def body(step, carry):
        block = step % 2
        rows = pl.ds(pl.multiple_of(step // 2 * (span // 2), PIECE), span // 2)
        for cols in tiles(width):
            grad = dot_cols(low_ref[rows, :], wd[block, cols, :]) * slope_ref[block, rows, cols].astype(F32)
            low = grad.astype(BF16)
            du_ref[block, rows, cols] = low
            up_sums[block, 0:1, cols] += jnp.sum(low.astype(F32), axis=0, keepdims=True)
        return carry

    lax.fori_loop(0, 4, body, 0)
    for copy in copies[5:]:
        copy.wait()
    for cols in tiles(width):
        out_ref[:, cols] = (dot_cols(du_ref[0], wu[0, cols, :]) + dot_cols(du_ref[1], wu[1, cols, :])).astype(BF16)


def mlp_back(part, other, slope, up_w, down_w, up_parts, down_parts):
    span, width = part.shape
    return pl.pallas_call(
        mlp_back_kernel,
        out_shape=[
            shape((2, span, width), BF16),
            shape((span, width), BF16),
            shape((8, width), F32),
            shape((2, 8, width), F32),
        ],
        in_specs=[vmem()] * 3 + [anywhere()] * 11,
        out_specs=[vmem()] * 4,
        scratch_shapes=[
            pltpu.VMEM((span, width), BF16),
            pltpu.VMEM((2, width, width), BF16),
            pltpu.VMEM((2, width, width), BF16),
            pltpu.SemaphoreType.DMA((11,)),
        ],
        **params("mlp_back", 8 * span * width * width, 20 * width * width),
    )(part, other, slope, *in_hbm(up_w, down_w, *up_parts, *down_parts))


def mid_back_kernel(share, vec_ref, mid_ref, part_ref, other_ref, grad_ref, got_ref, out_w, pack_ref, *rest):
    near_ref, far_ref, em_ref, mine_ref, sums_ref, dmid_ref = rest
    span, width = mid_ref.shape
    sums_ref[...] = jnp.zeros_like(sums_ref)

    def back_rows(index, rows):
        normal, inverse = norm_stats(mid_ref[rows, :])
        grad = grad_ref[rows, :].astype(F32) + got_ref[rows, :].astype(F32)
        dmid = part_ref[rows, :].astype(F32) + other_ref[rows, :].astype(F32)
        dmid += norm_backward(grad, normal, inverse, vec_ref[row(GAIN_MLP), :])
        dmid_ref[rows, :] = dmid
        em_ref[rows, :] = dmid.astype(BF16)
        sums_ref[0:1, :] += jnp.sum(grad * normal, axis=0, keepdims=True)
        sums_ref[1:2, :] += jnp.sum(grad, axis=0, keepdims=True)
        sums_ref[2:3, :] += jnp.sum(dmid, axis=0, keepdims=True)

    over_pieces(span, back_rows)
    far_ref[...] = dot_cols(em_ref[...], pack_ref[: out_w.shape[0], :]).astype(BF16)
    near_ref[...] = dot_cols(em_ref[...], out_w[...]).astype(BF16)
    mine_ref[...] = dmid_ref[pl.ds(pl.multiple_of(lax.axis_index("mp") % 2 * share, PIECE), share), :]


def mid_back(vecs, mid, part, other, grad, got, out_w, pack):
    span, width = mid.shape
    hw = out_w.shape[0]
    return pl.pallas_call(
        functools.partial(mid_back_kernel, span // 2),
        out_shape=[
            shape((span, hw), BF16),
            shape((span, hw), BF16),
            shape((span, width), BF16),
            shape((span // 2, width), F32),
            shape((8, width), F32),
        ],
        in_specs=[vmem()] * 8,
        out_specs=[vmem()] * 5,
        scratch_shapes=[pltpu.VMEM((span, width), F32)],
        **params("mid_back", 4 * span * width * hw, 12 * width * width),
    )(vecs, mid, part, other, grad, got, out_w, pack)


LINKS = {"y": ("mp", 2), "x": ("dp", 1), "z": ("dp", 2)}


class Lane:
    def __init__(self, blocks, rows, parts, link):
        self.blocks, self.rows, self.parts, self.link = blocks, rows, parts, link


class Kept:
    def __init__(self, blocks, rows, array, link, place):
        self.blocks, self.rows, self.array, self.link, self.place = blocks, rows, array, link, place


def high_of(link):
    axis, bit = LINKS[link]
    return (lax.axis_index(axis) // bit) % 2


def aligned(value, rows):
    return value if isinstance(value, int) else pl.multiple_of(value, rows & -rows)


def product_rows(left, right, block, out_ref, at):
    size = left.shape[-1]
    for base in range(0, size, TILE):
        cols = slice(base, min(base + TILE, size))
        lhs = left[block, :, cols] if len(left.shape) == 3 else left[:, cols]
        rhs = right[block] if len(right.shape) == 3 else right[...]
        out_ref[at + base : at + cols.stop, :] = dot_rows(lhs, rhs).astype(BF16)


def products_kernel(lefts, *refs):
    right, out_ref = refs[-2:]
    size = out_ref.shape[0] // 2
    for block in range(2):
        product_rows(refs[block] if lefts == 2 else refs[0], right, block, out_ref, block * size)


def products(name, lefts, right):
    span, width = right.shape[-2:]
    size = lefts[0].shape[-1]
    return pl.pallas_call(
        functools.partial(products_kernel, len(lefts)),
        out_shape=shape((2 * size, width), BF16),
        in_specs=[vmem()] * (len(lefts) + 1),
        out_specs=vmem(),
        **params(name, 4 * span * size * width, 8 * size * width),
    )(*lefts, right)


def emit_kernel(count, inputs, lanes, links, *refs):
    lefts, rights = refs[:count], refs[count : 2 * count]
    sources = list(refs[2 * count : 2 * count + inputs])
    outs = refs[2 * count + inputs :]
    if count:
        product, outs = outs[-1], outs[:-1]
        sources = [product] + sources
        total = product.shape[0] // 2
        begin = 0
        for left, right in zip(lefts, rights):
            for block in range(2):
                product_rows(left, right, block, product, block * total + begin)
            begin += left.shape[-1]
    sends = dict(zip(links, outs))
    kept = iter(outs[len(links) :])
    last = outs[-1]
    places = dict.fromkeys(list(links) + [None], 0)

    for lane in lanes:

        def total_of(block, start, size):
            values = [
                sources[index][pl.ds(aligned(base + block * stride + start, size), size), :]
                for index, base, stride in lane.parts
            ]
            if len(values) == 1:
                return values[0]
            return (values[0].astype(F32) + values[1].astype(F32)).astype(BF16)

        place = places[lane.link]
        if lane.link is None:
            last[place : place + lane.rows, :] = total_of(0, 0, lane.rows)
            places[None] += lane.rows
            continue
        send, keep = sends[lane.link], next(kept)
        if lane.link == "y":
            send[place : place + lane.rows, :] = total_of(1, 0, lane.rows)
            keep[...] = total_of(0, 0, lane.rows)
            places["y"] += lane.rows
            continue
        half = lane.rows // 2
        high = high_of(lane.link)
        for block in range(lane.blocks):
            rows = slice(block * half, (block + 1) * half)
            keep[rows, :] = total_of(block, high * half, half)
            send[place + rows.start : place + rows.stop, :] = total_of(block, (1 - high) * half, half)
        places[lane.link] += lane.blocks * half


def emit(name, lefts, rights, inputs, lanes, width, far=False):
    places = dict.fromkeys(list(LINKS) + [None], 0)
    kept = []
    for lane in lanes:
        sent = lane.blocks * lane.rows // 2 if lane.link else lane.rows
        if lane.link:
            blocks, rows = (1, lane.rows) if lane.link == "y" else (lane.blocks, lane.rows // 2)
            kept.append(Kept(blocks, rows, None, lane.link, places[lane.link]))
        places[lane.link] += sent
    links = [link for link in LINKS if places[link]]
    out_rows = [places[link] for link in links] + [k.blocks * k.rows for k in kept]
    if places[None]:
        out_rows.append(places[None])
    size = sum(left.shape[-1] for left in lefts)
    span = rights[0].shape[-2] if rights else 0
    results = pl.pallas_call(
        functools.partial(emit_kernel, len(lefts), len(inputs), lanes, links),
        out_shape=[
            pltpu.HBM((rows, width), BF16) if far and len(links) <= i < len(links) + len(kept) else shape((rows, width), BF16)
            for i, rows in enumerate(out_rows)
        ],
        in_specs=[vmem()] * (2 * len(lefts) + len(inputs)),
        out_specs=[vmem()] * len(out_rows),
        scratch_shapes=[pltpu.VMEM((2 * size, width), BF16)] if lefts else [],
        **params(name, 4 * span * size * width, 8 * size * width),
    )(*lefts, *rights, *inputs)
    for keep, array in zip(kept, results[len(links) :]):
        keep.array = array
        keep.far = far
    return dict(zip(links, results)), kept, results[-1] if places[None] else None


def send_all(sends):
    return {link: swap(value, *LINKS[link]) for link, value in sends.items()}


def turn(name, kept, got, links, width, fresh=(), far=False):
    inputs = [k.array for k in kept] + list(got.values()) + [lane[0] for lane in fresh]
    inputs = [in_hbm(v)[0] if k.far else v for k, v in zip(kept, inputs)] + inputs[len(kept) :]
    came = {link: len(kept) + i for i, link in enumerate(got)}
    lanes = []
    for i, (k, link) in enumerate(zip(kept, links)):
        lanes.append(Lane(k.blocks, k.rows, [(i, 0, k.rows), (came[k.link], k.place, k.rows)], link))
    for i, (lane, link) in enumerate(zip(fresh, links[len(kept) :])):
        lanes.append(Lane(lane[3], lane[4], [(len(kept) + len(got) + i, lane[1], lane[2])], link))
    return emit(name, [], [], inputs, lanes, width, far)


def spread_kernel(lanes, cuts, flip, *refs):
    first, gots, outs, total = refs[0], refs[1:5], refs[5:-1], refs[-1]
    bits = {"x": high_of("x"), "z": high_of("z")}
    places = [0, 0]
    sizes = [sum(lane[1] for lane in lanes if lane[3] == group) for group in range(2)]
    for base, rows, order, group in lanes:
        at = places[group]
        places[group] += rows
        near, far = ("z", "x") if group == 0 else ("x", "z")
        got_near, got_far = gots[2 * group], gots[2 * group + 1]
        offset = at + (sizes[0] if group else 0)
        pieces = [
            (first[offset : offset + rows, :], ()),
            (got_near[at : at + rows, :], (near,)),
            (got_far[at : at + rows, :], (far,)),
            (got_far[sizes[group] + at : sizes[group] + at + rows, :], (near, far)),
        ]
        for value, flipped in pieces:
            index = [1 - bits[link] if link in flipped else bits[link] for link in order]
            start = base + (index[0] * 2 + index[1]) * rows
            total[pl.ds(aligned(start, rows), rows), :] = value.astype(F32)
    begin = 0
    for i, (out, size) in enumerate(zip(outs, cuts)):
        value = total[begin : begin + size, :]
        out[...] = value.T if i in flip else value
        begin += size


def spread(name, lanes, cuts, flip, first, gots):
    width = first.shape[1]
    return pl.pallas_call(
        functools.partial(spread_kernel, lanes, cuts, flip),
        out_shape=[shape((width, size) if i in flip else (size, width), F32) for i, size in enumerate(cuts)],
        in_specs=[vmem()] * 5,
        out_specs=[vmem()] * len(cuts),
        scratch_shapes=[pltpu.VMEM((sum(cuts), width), F32)],
        **params(name, 0, 8 * sum(cuts) * width),
    )(first, *gots)


def pass_kernel(passed_ref, got_ref, sums_ref, up_ref, send_ref, whole_ref):
    share = passed_ref.shape[0]
    send_ref[:share, :] = (passed_ref[...] + got_ref[share : 2 * share, :].astype(F32)).astype(BF16)
    whole = sums_ref[0:VECTORS, :].astype(BF16).astype(F32) + got_ref[2 * share :, :].astype(F32)[0:VECTORS]
    whole = whole.astype(BF16).astype(F32)
    zero = jnp.zeros((1, whole.shape[1]), F32)
    send_ref[share:, :] = jnp.concatenate([whole, up_ref[1, 0:1, :], zero], axis=0).astype(BF16)
    whole_ref[...] = jnp.concatenate([whole, up_ref[0, 0:1, :], zero], axis=0)


def pass_on(passed, got, sums, up_sums):
    share, width = passed.shape
    return pl.pallas_call(
        pass_kernel,
        out_shape=[shape((share + 8, width), BF16), shape((8, width), F32)],
        in_specs=[vmem()] * 4,
        out_specs=[vmem()] * 2,
        **params("pass_on", 0, 8 * share * width),
    )(*in_hbm(passed), got, sums, up_sums)


def finish_kernel(tok_ref, vec_ref, own_ref, got_ref, last_ref, mine_ref, out_ref, tok_buf, sem):
    share = out_ref.shape[0]
    start = pl.multiple_of(lax.axis_index("mp") * share, PIECE)
    copy = pltpu.make_async_copy(tok_ref.at[pl.ds(start, share), :], tok_buf, sem)
    copy.start()
    copy.wait()

    def back_rows(index, rows):
        normal, inverse = norm_stats(tok_buf[rows, :].astype(F32))
        grad = own_ref[rows, :] + got_ref[rows, :].astype(F32) + last_ref[rows, :].astype(F32)
        out_ref[rows, :] = mine_ref[rows, :] + norm_backward(grad, normal, inverse, vec_ref[row(GAIN_ATTN), :])

    over_pieces(share, back_rows)


def finish(rows2d, vecs, own, got, last, mine):
    share, width = own.shape
    return pl.pallas_call(
        finish_kernel,
        out_shape=shape((share, width), F32),
        in_specs=[anywhere()] + [vmem()] * 5,
        out_specs=vmem(),
        scratch_shapes=[pltpu.VMEM((share, width), BF16), pltpu.SemaphoreType.DMA],
        **params("finish", 0, 14 * share * width),
    )(*in_hbm(rows2d, vecs, own), got, last, *in_hbm(mine))


def add_low(left, right):
    return (left.astype(F32) + right.astype(F32)).astype(BF16)


def bit_of(axis, bit):
    return (lax.axis_index(axis) // bit) % 2


def take_half(value, high):
    half = value.shape[0] // 2
    return lax.dynamic_slice_in_dim(value, high * half, half, 0)


def put_half(mine, other, high):
    return jnp.concatenate([jnp.where(high > 0, other, mine), jnp.where(high > 0, mine, other)], axis=0)


def late_bits():
    bits = []
    bit = 4
    while bit < lax.axis_size("dp"):
        bits.append(bit)
        bit *= 2
    return bits


def finish_reduce(current, bit):
    high = bit_of("dp", bit)
    return add_low(take_half(current, high), swap(take_half(current, 1 - high), "dp", bit))


def finish_gather(current, bit):
    return put_half(current, swap(current, "dp", bit), bit_of("dp", bit))


def shards(
    tokens, lengths, gain_attn, bias_attn, query_w, query_b, key_w, value_w, value_b, out_w, out_b, gain_mlp, bias_mlp,
    up_w, up_b, down_w, down_b, deconv_w, scale_norm, shift_norm, cotangent
):
    items, seq, width = tokens.shape
    rows = items * seq
    me = lax.axis_index("mp")
    share = rows // lax.axis_size("mp")
    span = rows // 2
    hw = query_w.shape[1]
    rows2d = tokens.reshape(rows, width)
    side = bit_of("dp", 1)
    chip = bit_of("mp", 2)
    mixed = jnp.concatenate([query_b, value_b, scale_norm, shift_norm])
    mixed = jnp.pad(mixed, (0, width - mixed.shape[0]))
    vecs = jnp.concatenate([out_b, gain_mlp, bias_mlp, down_b, gain_attn, bias_attn, up_b, mixed])
    vecs = vecs.astype(F32).reshape(8, width)
    weights = [query_w.T, key_w.T, value_w.T]
    conv_w = deconv_w.T

    quarter = width // 4
    mine = lax.axis_index("dp") % 4

    def quarter_of(weight, index):
        count = weight.shape[0] // 4
        return lax.dynamic_slice_in_dim(weight, index * count, count, 0)

    def low_quarter(index):
        return jnp.concatenate([quarter_of(down_w, index), quarter_of(conv_w, index)], axis=0)

    bias_rows = jnp.broadcast_to(up_b[None, :], (PAD, width))
    out_far = swap(jnp.concatenate([out_w, bias_rows], axis=0), "mp", 2)
    up_part = swap(quarter_of(up_w, mine), "mp", 2)
    low_part = swap(low_quarter(mine), "mp", 2)

    normed, q, k, v, lse, near, other = attend(lengths, rows2d, vecs, *weights, items, seq)
    out_far, near, other, up_part = join(out_far, near, other, up_part)
    far = swap(other, "mp", 2)
    cot_rows = cotangent.reshape(rows, -1)
    cot_sent = lax.dynamic_slice_in_dim(cot_rows, (1 - chip) * span, span, 0)
    low_sent = low_quarter(mine ^ 3)
    up_part, low_sent = join(up_part, low_sent)
    up_parts = [up_part, swap(up_part, "dp", 1), swap(up_part, "dp", 2)]
    last_half = quarter // 2
    turned = [up_parts[2][:last_half], up_parts[1][last_half:]]
    far, low_sent, cot_sent, turned[0], turned[1], *up_parts = join(far, low_sent, cot_sent, *turned, *up_parts)
    low_last = swap(low_sent, "mp", 2)
    up_parts.append(swap(turned[0], "dp", 1))
    up_parts.append(swap(turned[1], "dp", 2))

    part = project(near, far, out_w, out_far)
    part_got = swap(part, "mp", 1)
    part_got, low_part, cot_sent, *up_parts = join(part_got, low_part, cot_sent, *up_parts)
    down_parts = [low_part, swap(low_part, "dp", 1), swap(low_part, "dp", 2)]
    far_cot = swap(cot_sent, "mp", 2)
    mid, normed_two, act, slope = expand(rows2d, vecs, part, part_got, out_far, up_w, up_parts)
    act, low_last, *down_parts = join(act, low_last, *down_parts)
    down_parts.append(low_last)
    part = contract(act, down_w, down_parts)
    part, far_cot = join(part, far_cot)
    low, z, sums = convolve(
        lengths, vecs, mid, part, swap(part, "mp", 1), conv_w, down_parts, cot_rows, far_cot, items, seq
    )
    sums = sums + swap(sums, "mp", 1)
    vol_near, vol_far, dz, grad, norm_sums = norm_back(
        lengths, vecs, sums, swap(sums, "mp", 2), z, conv_w, down_parts, cot_rows, far_cot, items, seq, 2 * hw
    )
    grad_got = swap(grad, "mp", 1)
    conv_raw = products("conv_grad", [dz], low)
    grad_got, conv_raw = join(grad_got, conv_raw)
    block = conv_w.shape[0]
    half = block // 2
    third = width // 3
    lanes = [Lane(2, third, [(0, i * third, width)], link) for i, link in enumerate("yxz")]
    sends, kept, unused = emit("down_grad", [act], [add_low(grad, grad_got)], [], lanes, width)
    grad_got, sends["y"], sends["x"], sends["z"] = join(grad_got, sends["y"], sends["x"], sends["z"])
    came = send_all(sends)
    du, back, low_sums, up_sums = mlp_back(grad, grad_got, slope, up_w, down_w, up_parts, down_parts)
    back, came["y"], came["x"], came["z"] = join(back, came["y"], came["x"], came["z"])
    back_got = swap(back, "mp", 1)
    up_raw = products("up_grad", [normed_two], du)
    fresh = [(conv_raw, 0, block, 2, half), (conv_raw, half, block, 2, half)]
    sends, kept, unused = turn("turn_one", kept, came, "xzyxz", width, fresh)
    back_got, up_raw, sends["y"], sends["x"], sends["z"] = join(back_got, up_raw, sends["y"], sends["x"], sends["z"])
    came = send_all(sends)
    do_near, do_far, em, dmid, vec_sums = mid_back(vecs, mid, grad, grad_got, back, back_got, out_w, out_far)
    do_far, em, came["y"] = join(do_far, em, came["y"])
    do_got = swap(do_far, "mp", 2)
    out_raw = products("out_grad", [near, far], em)
    out_raw, came["y"], came["x"], came["z"] = join(out_raw, came["y"], came["x"], came["z"])
    cut = width * 5 // 12
    fresh = [(up_raw, 0, width, 2, cut), (up_raw, cut, width, 2, cut), (up_raw, 2 * cut, width, 2, width - 2 * cut)]
    fresh.append((out_raw, 0, hw, 2, hw))
    sends, kept, unused = turn("turn_two", kept, came, "zyxzxyxzz", width, fresh, True)
    do_got, sends["y"], sends["x"], sends["z"] = join(do_got, sends["y"], sends["x"], sends["z"])
    came = send_all(sends)

    *dqkv, qkv_grad, bias_sums = attend_back(lengths, normed, q, k, v, lse, do_near, do_got, items, seq, share)
    qkv_grad, vol_far, came["y"], came["x"], came["z"], *dqkv = join(
        qkv_grad, vol_far, came["y"], came["x"], came["z"], *dqkv
    )
    cut = qkv_grad.shape[0] * 4 // 9
    fresh = [(qkv_grad, 0, 0, 1, cut), (qkv_grad, cut, 0, 1, qkv_grad.shape[0] - cut)]
    sizes = [k.blocks * k.rows for k in kept[:3]]
    links = [None] * 3 + ["y", "y", "x", "z", "y", "y", "x", "z"]
    sends, kept, first = turn("turn_three", kept, came, links, width, fresh, True)
    for bit in late_bits():
        first = finish_reduce(first, bit)
    came = send_all(sends)
    sent, own, passed, own_sums = normed_back(
        lengths, rows2d, *dqkv, *weights, vec_sums, low_sums, items, seq, share
    )
    first, sent, came["y"], came["x"], came["z"] = join(first, sent, came["y"], came["x"], came["z"])
    for bit in reversed(late_bits()):
        first = finish_gather(first, bit)
    got = swap(sent, "mp", 1)
    conv_sizes = [k.blocks * k.rows for k in kept[:2]]
    came = {link: in_hbm(value)[0] for link, value in came.items()}
    sends, kept, early = turn("turn_four", kept, came, [None, None] + list("zyxxzx"), width)
    came = send_all(sends)
    edge = sizes[0] + sizes[1]
    sent_near = [first[:edge], first[edge:]]
    sent_near[0], sent_near[1], first, got, vol_far, came["y"], came["x"], came["z"] = join(
        *sent_near, first, got, vol_far, came["y"], came["x"], came["z"]
    )
    kept = [kept[i] for i in (0, 1, 4, 2, 3, 5)]
    unused, unused, last = turn("turn_five", kept, came, [None] * 6, width)
    last_sizes = [k.blocks * k.rows for k in kept] + conv_sizes
    last = jnp.concatenate([last, early], axis=0)
    for bit in late_bits():
        last = finish_reduce(last, bit)
    near_got = [swap(sent_near[0], "dp", 2), swap(sent_near[1], "dp", 1)]
    second, whole = pass_on(passed, got, own_sums, up_sums)
    second = swap(second, "mp", 2)
    far_got = [
        swap(jnp.concatenate([sent_near[0], near_got[0]], axis=0), "dp", 1),
        swap(jnp.concatenate([sent_near[1], near_got[1]], axis=0), "dp", 2),
    ]
    last, second, vol_far, *far_got = join(last, second, vol_far, *far_got)
    vol_got = swap(vol_far, "mp", 2)
    tokens_grad = finish(rows2d, vecs, own, got, second, dmid)
    for bit in reversed(late_bits()):
        last = finish_gather(last, bit)
    whole = (whole + second[share : share + 8].astype(F32))[: VECTORS + 1]
    lines = jnp.concatenate([whole, bias_sums[0:1], bias_sums[2:3], norm_sums[0:1]], axis=0)
    for bit in [1, 2] + late_bits():
        lines = lines + swap(lines, "dp", bit)
    (down_total,) = spread(
        "spread_one",
        [(0, sizes[0], "xz", 0), (third, sizes[1], "xz", 0), (2 * third, sizes[2], "zx", 1)],
        [width],
        [],
        first,
        [near_got[0], far_got[0], near_got[1], far_got[1]],
    )
    last, lines, down_total, tokens_grad = join(last, lines, down_total, tokens_grad)
    edge = sum(last_sizes[:3])
    sent_last = [last[:edge], last[edge:]]
    last_got = [swap(sent_last[0], "dp", 2), swap(sent_last[1], "dp", 1)]
    volume = put_half(vol_near, vol_got, chip).astype(F32)
    volume, *last_got = join(volume, *last_got)
    last_far = [
        swap(jnp.concatenate([sent_last[0], last_got[0]], axis=0), "dp", 1),
        swap(jnp.concatenate([sent_last[1], last_got[1]], axis=0), "dp", 2),
    ]
    base = width + hw
    up_cut = width * 5 // 12
    up_total, out_total, query_total, key_total, value_total, conv_total = spread(
        "spread_two",
        [
            (0, last_sizes[0], "xz", 0),
            (up_cut, last_sizes[1], "xz", 0),
            (base, last_sizes[2], "xz", 0),
            (2 * up_cut, last_sizes[3], "zx", 1),
            (width, last_sizes[4], "zx", 1),
            (base + cut, last_sizes[5], "zx", 1),
            (base + 3 * hw, last_sizes[6], "xz", 1),
            (base + 3 * hw + half, last_sizes[7], "zx", 1),
        ],
        [width, hw, hw, hw, hw, block],
        [5],
        last,
        [last_got[0], last_far[0], last_got[1], last_far[1]],
    )
    return (
        volume.reshape(items, seq, -1),
        tokens_grad,
        lines[0],
        lines[1],
        query_total.T,
        lines[VECTORS + 1, :hw],
        key_total.T,
        value_total.T,
        lines[VECTORS + 2, :hw],
        out_total,
        lines[4],
        lines[2],
        lines[3],
        up_total,
        lines[VECTORS],
        down_total,
        lines[5],
        conv_total,
        lines[VECTORS + 3, :CH],
        lines[VECTORS + 3, CH : 2 * CH],
    )


def solution(mesh):
    in_specs = (
        P("dp", None, None),
        P("dp"),
        P(),
        P(),
        P(None, "mp"),
        P("mp"),
        P(None, "mp"),
        P(None, "mp"),
        P("mp"),
        P("mp", None),
        P(),
        P(),
        P(),
        P(None, "mp"),
        P("mp"),
        P("mp", None),
        P(),
        P(None, "mp"),
        P(),
        P(),
        P("dp", None, "mp"),
    )
    out_specs = (
        P("dp", None, "mp"),
        P(("dp", "mp"), None),
        P(),
        P(),
        P(None, "mp"),
        P("mp"),
        P(None, "mp"),
        P(None, "mp"),
        P("mp"),
        P("mp", None),
        P(),
        P(),
        P(),
        P(None, "mp"),
        P("mp"),
        P("mp", None),
        P(),
        P(None, "mp"),
        P(),
        P(),
    )
    return jax.shard_map(shards, mesh=mesh, in_specs=in_specs, out_specs=out_specs, check_vma=False)
```
